32 devices in a mesh: wide: 8 (over z, x), narrow: 4 (over y, core).
Axes of the slice: x: 2, y: 2, z: 4, core: 2. Of those that a mesh axis runs over, the one named last changes fastest.
Arguments:
- tokens: bfloat16 [2, 16, 256, 1152], P(None, 'wide'), may hold values from -6 to 6
- conditioning: bfloat16 [2, 1, 1152], replicated, may hold values from -6 to 6
- frame_segments: int32 [2, 1, 16], replicated, may hold values from 0 to 3, never falling along the last dimension, each value on 1 to 8 neighbouring positions
- cotangent: bfloat16 [2, 16, 256, 1152], P(None, 'wide'), may hold values from -6 to 6
- qkv_weight: bfloat16 [2, 1152, 3, 1152], P(None, 'wide', None, 'narrow'), may hold values from -0.1875 to 0.1875
- qkv_bias: bfloat16 [2, 2, 1152], P(None, None, 'narrow'), may hold values from -3 to 3
- proj_weight: bfloat16 [2, 1152, 1152], P(None, 'narrow', 'wide'), may hold values from -0.75 to 0.75
- proj_bias: bfloat16 [2, 1152], replicated, may hold values from -3 to 3
- up_weight: bfloat16 [2, 1152, 4608], P(None, 'wide', 'narrow'), may hold values from -0.1875 to 0.1875
- up_bias: bfloat16 [2, 4608], P(None, 'narrow'), may hold values from -3 to 3
- down_weight: bfloat16 [2, 4608, 1152], P(None, 'narrow', 'wide'), may hold values from -0.09375 to 0.09375
- down_bias: bfloat16 [2, 1152], replicated, may hold values from -3 to 3
- ada_weight: bfloat16 [2, 1152, 6, 1152], P(None, 'wide', None, 'narrow'), may hold values from -0.1875 to 0.1875
- ada_bias: bfloat16 [2, 6, 1152], P(None, None, 'narrow'), may hold values from -3 to 3
Outputs:
- layer_out: bfloat16 [2, 16, 256, 1152], P(None, 'wide')
- input_grad: float32 [2, 16, 256, 1152], P(None, 'wide')
- qkv_wgrad: float32 [2, 1152, 3, 1152], P(None, 'wide', None, 'narrow')
- qkv_bgrad: float32 [2, 2, 1152], P(None, None, 'narrow')
- proj_wgrad: float32 [2, 1152, 1152], P(None, 'narrow', 'wide')
- proj_bgrad: float32 [2, 1152], replicated
- up_wgrad: float32 [2, 1152, 4608], P(None, 'wide', 'narrow')
- up_bgrad: float32 [2, 4608], P(None, 'narrow')
- down_wgrad: float32 [2, 4608, 1152], P(None, 'narrow', 'wide')
- down_bgrad: float32 [2, 1152], replicated
- ada_wgrad: float32 [2, 1152, 6, 1152], P(None, 'wide', None, 'narrow')
- ada_bgrad: float32 [2, 6, 1152], P(None, None, 'narrow')
The draws below stay inside these ranges and needn't reach their ends.
Inputs may be any that keep to these rules, and one draw needn't show every extreme that they name: `frame_segments`: in each sequence the frames' clip numbers never fall, every number from 0 to 3 occurs, and each covers 1 to 8 frames.
All inputs are finite; a program needn't handle non-finite values.
Results may differ from the reference program's by a relative error of at most 0.035.
Values may be sent and summed in bfloat16 or wider, within the bound.
A program may use at most 320 MiB of HBM per device.

```python
import math
import jax
import jax.numpy as jnp
import numpy as np
from jax import lax

D = 1152
HEADS = 16
FF = 4608
HEAD_DIM = 72
P_SIZE = 256
FRAMES = 16
MB = 2
SEQ_MB = 1
GFRAMES = 16
N_NARROW = 4


def block_levels(rng, dims, shards, least, top_value):
    def one(dim, parts):
        heights = jax.random.uniform(jax.random.fold_in(jax.random.fold_in(rng, 6), dim), (parts,), jnp.float32, least / len(shards), top_value / len(shards))
        return jnp.repeat(jnp.exp(heights), dims[dim] // parts).reshape((-1,) + (1,) * (len(dims) - dim - 1))

    gain = one(*shards[0])
    for cut in shards[1:]:
        gain = gain * one(*cut)
    return gain


def profile(count, total, reach, lean):
    portions = [(1 << 20) // math.isqrt(standing ** lean) + 1 for standing in range(2, count + 1)]
    spare, given = total - reach - (count - 1), [1] * (count - 1)
    while spare > 0:
        free = [i for i in range(count - 1) if given[i] < reach]
        mass, budget = sum([portions[i] for i in free]), spare
        for i in free:
            extra = min(reach - given[i], max(1, budget * portions[i] // mass), spare)
            given[i] = given[i] + extra
            spare = spare - extra
    return np.array([reach] + given)


def uneven_parts(own_key, count, total, reach, skew):
    if count == 2:
        one = jax.random.randint(own_key, (), max(1, total - reach), min(reach, total - 1) + 1)
        return jnp.stack([one, total - one])
    tallies = jnp.asarray(profile(count, total, reach, skew), jnp.int32)
    couples = (count - 1) // 2
    donor, taker = tallies[1:1 + 2 * couples:2], tallies[2:2 + 2 * couples:2]
    margin = jnp.minimum(donor - 1, reach - taker)
    shifted = jax.random.randint(jax.random.fold_in(own_key, 1), (couples,), 0, 1 << 20) % (margin + 1)
    tallies = tallies.at[1:1 + 2 * couples:2].set(donor - shifted).at[2:2 + 2 * couples:2].set(taker + shifted)
    return tallies[jax.random.permutation(jax.random.fold_in(own_key, 2), count)]


def bell_draw(own_key, shape, deviation, bound, shards=(), held_as=jnp.bfloat16):
    drawn = deviation * jax.random.normal(own_key, shape, jnp.float32)
    if shards:
        drawn = drawn * block_levels(own_key, shape, shards, -0.22, 0.18)
    return jnp.clip(drawn, -bound, bound).astype(held_as)


def setup_inputs(seed: int = 0) -> dict:
    arg_keys = jax.random.split(jax.random.key(seed), 15)
    tokens = bell_draw(arg_keys[0], (MB, GFRAMES, P_SIZE, D), 1.0, 6.0, ((1, 8),))
    conditioning = bell_draw(arg_keys[1], (MB, SEQ_MB, D), 1.0, 6.0)
    frame_segments = jax.vmap(lambda own: jnp.searchsorted(jnp.cumsum(uneven_parts(own, FRAMES // 4, FRAMES, FRAMES // 2, 0)), jnp.arange(FRAMES), side="right"))(jax.random.split(arg_keys[2], MB * SEQ_MB)).reshape((MB, SEQ_MB, FRAMES)).astype(jnp.int32)
    cotangent = bell_draw(arg_keys[3], (MB, GFRAMES, P_SIZE, D), 1.0, 6.0, ((1, 8),))
    qkv_weight = bell_draw(arg_keys[4], (2, D, 3, D), D ** -0.5, 0.1875, ((1, 8), (3, 4)))
    qkv_bias = bell_draw(arg_keys[5], (2, 2, D), 0.5, 3.0, ((2, 4),))
    proj_weight = bell_draw(arg_keys[6], (2, D, D), (D // 16) ** -0.5, 0.75, ((1, 4), (2, 8)))
    proj_bias = bell_draw(arg_keys[7], (2, D), 0.5, 3.0)
    up_weight = bell_draw(arg_keys[8], (2, D, FF), D ** -0.5, 0.1875, ((1, 8), (2, 4)))
    up_bias = bell_draw(arg_keys[9], (2, FF), 0.5, 3.0, ((1, 4),))
    down_weight = bell_draw(arg_keys[10], (2, FF, D), FF ** -0.5, 0.09375, ((1, 4), (2, 8)))
    down_bias = bell_draw(arg_keys[11], (2, D), 0.5, 3.0)
    ada_weight = bell_draw(arg_keys[12], (2, D, 6, D), D ** -0.5, 0.1875, ((1, 8), (3, 4)))
    ada_bias = bell_draw(arg_keys[13], (2, 6, D), 0.5, 3.0, ((2, 4),))
    return dict(tokens=tokens, conditioning=conditioning, frame_segments=frame_segments, cotangent=cotangent, qkv_weight=qkv_weight, qkv_bias=qkv_bias, proj_weight=proj_weight, proj_bias=proj_bias, up_weight=up_weight, up_bias=up_bias, down_weight=down_weight, down_bias=down_bias, ada_weight=ada_weight, ada_bias=ada_bias)


@jax.custom_vjp
def low(v):
    return lax.optimization_barrier(v.astype(jnp.bfloat16)).astype(jnp.float32)

@jax.custom_vjp
def low_back(v):
    return v

def low_keep(v):
    return (low(v), None)

def low_pass(kept, grad):
    return (grad,)

def back_keep(v):
    return (v, None)

def back_low(kept, grad):
    return (low(grad),)
low.defvjp(low_keep, low_pass)
low_back.defvjp(back_keep, back_low)
HIGHEST = lax.Precision.HIGHEST
norm_eps = 1e-06
masked_score = -1e+30

def norm_rows(rows_in):
    centred = rows_in - lax.optimization_barrier(jnp.mean(rows_in, axis=-1, keepdims=True))
    spread = lax.optimization_barrier(jnp.mean(centred * centred, axis=-1, keepdims=True))
    return centred * lax.rsqrt(spread + norm_eps)

def modulate(rows_in, shift_row, scale_row):
    return norm_rows(rows_in) * (1.0 + scale_row) + shift_row

def attend(queries, key_rows, value_rows, visible, form_set):
    score_form, value_form = form_set
    raw_scores = jnp.einsum(score_form, queries, key_rows, precision=HIGHEST)
    scores = low_back(raw_scores) * HEAD_DIM ** (-0.5)
    if visible is not None:
        scores = jnp.where(visible, scores, masked_score)
    weights = jax.nn.softmax(scores, axis=-1)
    return jnp.einsum(value_form, low(weights), value_rows, precision=HIGHEST)

def block(hidden_in, cond_row, frame_ids, weights, temporal):
    qkv_w, qkv_b, proj_w, proj_b, up_w, up_b, down_w, down_b, ada_w, ada_b = weights
    group_width = D // N_NARROW
    group_hidden = FF // N_NARROW
    silu_row = low(jax.nn.silu(cond_row))
    modulation = jnp.dot(silu_row, ada_w.reshape(D, 6 * D), precision=HIGHEST).reshape(6, D) + ada_b
    normed = low(modulate(hidden_in, modulation[0], modulation[1]))
    pieces = []
    for group_index in range(N_NARROW):
        columns = slice(group_index * group_width, (group_index + 1) * group_width)
        pieces.append(jnp.einsum('fpd,dce->fpce', low_back(normed), qkv_w[:, :, columns], precision=HIGHEST))
    projected = jnp.concatenate(pieces, axis=-1)
    head_shape = (FRAMES, P_SIZE, HEADS, HEAD_DIM)
    queries = low(low_back(projected[:, :, 0] + qkv_b[0])).reshape(head_shape)
    key_rows = low(low_back(projected[:, :, 1])).reshape(head_shape)
    value_rows = low(low_back(projected[:, :, 2] + qkv_b[1])).reshape(head_shape)
    if temporal:
        visible = (frame_ids[:, None] == frame_ids[None, :])[None, None]
        attended = attend(queries, key_rows, value_rows, visible, ('qphe,kphe->phqk', 'phqk,kphe->qphe'))
    else:
        attended = attend(queries, key_rows, value_rows, None, ('fqhe,fkhe->fhqk', 'fhqk,fkhe->fqhe'))
    attended = low(low_back(attended.reshape(FRAMES, P_SIZE, D)))
    branch = jnp.zeros((FRAMES, P_SIZE, D), jnp.float32)
    for group_index in range(N_NARROW):
        columns = slice(group_index * group_width, (group_index + 1) * group_width)
        branch = branch + low(jnp.einsum('fpc,cd->fpd', attended[:, :, columns], proj_w[columns], precision=HIGHEST))
    branch = low_back(branch)
    mixed = hidden_in + modulation[2] * (branch + proj_b)
    normed_two = low(modulate(mixed, modulation[3], modulation[4]))
    feed_out = jnp.zeros((FRAMES, P_SIZE, D), jnp.float32)
    for group_index in range(N_NARROW):
        columns = slice(group_index * group_hidden, (group_index + 1) * group_hidden)
        before = low_back(jnp.einsum('fpd,dc->fpc', low_back(normed_two), up_w[:, columns], precision=HIGHEST) + up_b[columns])
        active = low(jax.nn.gelu(before, approximate=True))
        feed_out = feed_out + low(jnp.einsum('fpc,cd->fpd', active, down_w[columns], precision=HIGHEST))
    feed_out = low_back(feed_out)
    return mixed + modulation[5] * (feed_out + down_b)

def layer(hidden_in, cond_row, frame_ids, weights):
    for block_index in range(2):
        block_weights = tuple((member[block_index] for member in weights))
        hidden_in = block(hidden_in, cond_row, frame_ids, block_weights, block_index == 1)
    return hidden_in

def reference(tokens, conditioning, frame_segments, cotangent, qkv_weight, qkv_bias, proj_weight, proj_bias, up_weight, up_bias, down_weight, down_bias, ada_weight, ada_bias):
    seq_count = MB * SEQ_MB
    flat_tokens = tokens.astype(jnp.float32).reshape(seq_count, FRAMES, P_SIZE, D)
    flat_cond = conditioning.astype(jnp.float32).reshape(seq_count, D)
    flat_segments = frame_segments.reshape(seq_count, FRAMES).astype(jnp.int32)
    params = tuple((member.astype(jnp.float32) for member in (qkv_weight, qkv_bias, proj_weight, proj_bias, up_weight, up_bias, down_weight, down_bias, ada_weight, ada_bias)))

    def forward(inputs, weights):

        def one_sequence(item):
            return layer(item[0], item[1], item[2], weights)
        return lax.map(jax.checkpoint(one_sequence), (inputs, flat_cond, flat_segments))
    result, pullback = jax.vjp(forward, flat_tokens, params)
    grad_tokens, grad_params = pullback(cotangent.astype(jnp.float32).reshape(seq_count, FRAMES, P_SIZE, D))
    layer_out = result.reshape(tokens.shape).astype(jnp.bfloat16)
    input_grad = grad_tokens.reshape(tokens.shape)
    return (layer_out, input_grad, grad_params[0], grad_params[1], grad_params[2], grad_params[3], grad_params[4], grad_params[5], grad_params[6], grad_params[7], grad_params[8], grad_params[9])
```

```python
import functools
import types

import jax
import jax.numpy as jnp
from jax import lax
from jax.experimental import pallas as pl
from jax.experimental.pallas import tpu as pltpu
from jax.sharding import PartitionSpec as P

HEAD_DIM = 72
NORM_EPS = 1e-06
MASKED = -1e30
BF16 = jnp.bfloat16
F32 = jnp.float32


NN, NT, TN = ((1,), (0,)), ((1,), (1,)), ((0,), (0,))
CHUNKS = 4
GELU_C = 0.7978845608028654
GELU_A = 0.044715


def kdot(a, b, dims):
    return lax.dot_general(a, b, (dims, ((), ())), preferred_element_type=F32)


def call(name, body, ins, outs, scratch, cid=None, hbm=()):
    names = list(ins) + list(outs) + list(scratch)

    def spec(key):
        return pl.BlockSpec(memory_space=pl.ANY if key in hbm else pltpu.VMEM)

    def kernel(*refs):
        body(types.SimpleNamespace(**dict(zip(names, refs))))

    results = pl.pallas_call(
        kernel,
        in_specs=[spec(key) for key in ins],
        out_specs=[spec(key) for key in outs],
        out_shape=list(outs.values()),
        scratch_shapes=list(scratch.values()),
        compiler_params=pltpu.CompilerParams(
            vmem_limit_bytes=60 << 20,
            collective_id=cid,
            has_side_effects=cid is not None,
        ),
        name=name,
    )(*ins.values())
    return dict(zip(outs, results))


def pipeline(count, stages):
    for step in range(count + max(lag for lag, _ in stages)):
        for lag, stage in stages:
            if 0 <= step - lag < count:
                stage(step - lag)


class Narrow:
    def __init__(self, refs):
        n = lax.axis_index("narrow")
        self.n, self.core, self.across, self.far = (
            n,
            n + 1 - 2 * lax.rem(n, 2),
            lax.rem(n + 2, 4),
            3 - n,
        )
        self.r = refs

    def barrier(self):
        sem = pltpu.get_barrier_semaphore()
        for other in (self.core, self.across):
            pl.semaphore_signal(sem, inc=1, device_id={"narrow": other})
        pl.semaphore_wait(sem, 2)

    def remote(self, src, dst, sems, index, other):
        return pltpu.make_async_remote_copy(
            src_ref=src,
            dst_ref=dst,
            send_sem=sems.at[(0,) + index],
            recv_sem=sems.at[(1,) + index],
            device_id={"narrow": other},
        )

    def sum_scratch(rows, d):
        return dict(
            part=pltpu.VMEM((CHUNKS // 2, 4, 2, rows, d), BF16),
            near=pltpu.VMEM((CHUNKS, 2, rows, d), BF16),
            pair=pltpu.VMEM((CHUNKS, rows, d), BF16),
            cross=pltpu.VMEM((CHUNKS, rows, d), BF16),
            near_sem=pltpu.SemaphoreType.DMA((2, CHUNKS, 2)),
            cross_sem=pltpu.SemaphoreType.DMA((2, CHUNKS)),
        )

    def near_copy(self, i, which):
        owner = self.core if which == 0 else self.far
        return self.remote(
            self.r.part.at[i // 2, owner, i % 2],
            self.r.near.at[i, which],
            self.r.near_sem,
            (i, which),
            self.core,
        )

    def cross_copy(self, i):
        return self.remote(
            self.r.pair.at[i], self.r.cross.at[i], self.r.cross_sem, (i,), self.across
        )

    def sum_start(self, i):
        self.near_copy(i, 1).start()
        self.near_copy(i, 0).start()

    def sum_cross(self, i):
        self.near_copy(i, 1).wait_recv()
        mine = self.r.part[i // 2, self.across, i % 2].astype(F32)
        self.r.pair[i] = (mine + self.r.near[i, 1].astype(F32)).astype(BF16)
        self.cross_copy(i).start()

    def sum_end(self, i):
        self.near_copy(i, 0).wait_recv()
        total = self.r.part[i // 2, self.n, i % 2].astype(F32) + self.r.near[i, 0].astype(F32)
        self.cross_copy(i).wait_recv()
        return total + self.r.cross[i].astype(F32)

    def sum_drain(self):
        for i in range(CHUNKS):
            self.near_copy(i, 0).wait_send()
            self.near_copy(i, 1).wait_send()
            self.cross_copy(i).wait_send()

    def gather_scratch(rows, d):
        return dict(
            own=pltpu.VMEM((CHUNKS, rows, d), BF16),
            own_sem=pltpu.SemaphoreType.DMA((CHUNKS,)),
            out_sem=pltpu.SemaphoreType.DMA((2, CHUNKS, 3)),
        )

    def place(self, i, n):
        return self.r.full.at[i // 2, n, i % 2]

    def out_copy(self, i, which):
        if which == 2:
            rows = self.place(i, self.across)
            return self.remote(rows, rows, self.r.out_sem, (i, 2), self.core)
        other = self.across if which == 0 else self.core
        return self.remote(
            self.r.own.at[i], self.place(i, self.n), self.r.out_sem, (i, which), other
        )

    def own_copy(self, i):
        return pltpu.make_async_copy(
            self.r.own.at[i], self.place(i, self.n), self.r.own_sem.at[i]
        )

    def gather_start(self, i, value):
        self.r.own[i] = value
        self.out_copy(i, 0).start()
        self.out_copy(i, 1).start()
        self.own_copy(i).start()

    def gather_forward(self, i):
        self.out_copy(i, 0).wait_recv()
        self.out_copy(i, 2).start()

    def gather_drain(self):
        for i in range(CHUNKS):
            self.own_copy(i).wait()
            for which in range(3):
                self.out_copy(i, which).wait_send()
                if which:
                    self.out_copy(i, which).wait_recv()


def norm_rows(v):
    centred = v - jnp.mean(v, axis=-1, keepdims=True)
    r = lax.rsqrt(jnp.mean(centred * centred, axis=-1, keepdims=True) + NORM_EPS)
    return centred * r, r


def norm_back(grad, n, r, scale):
    dn = grad * (1.0 + scale)
    return r * (
        dn
        - jnp.mean(dn, axis=-1, keepdims=True)
        - n * jnp.mean(dn * n, axis=-1, keepdims=True)
    )


def column_sum(v):
    return jnp.sum(v, axis=0, keepdims=True)


def sds(shape, dtype=BF16):
    return jax.ShapeDtypeStruct(shape, dtype)


def softmax_rows(q, k, mask):
    s = kdot(q, k, NT) * HEAD_DIM ** (-0.5)
    if mask is not None:
        s = s + mask
    p = jnp.exp(s - jnp.max(s, axis=-1, keepdims=True))
    return p * (1.0 / jnp.sum(p, axis=-1, keepdims=True))


def attend(qkv, mask, heads):
    rows = qkv.shape[0]
    size = rows if mask is None else mask.shape[0]
    width = heads * HEAD_DIM
    tiles = []
    for t in range(rows // size):
        here = qkv[t * size : (t + 1) * size]
        outs = []
        for h in range(heads):
            q, k, v = (
                here[:, j * width + h * HEAD_DIM : j * width + (h + 1) * HEAD_DIM] for j in range(3)
            )
            outs.append(kdot(softmax_rows(q, k, mask).astype(BF16), v, NN).astype(BF16))
        tiles.append(jnp.concatenate(outs, axis=1))
    return tiles[0] if len(tiles) == 1 else jnp.concatenate(tiles, axis=0)


def attend_back(qkv, grad, mask, heads):
    rows = qkv.shape[0]
    size = rows if mask is None else mask.shape[0]
    width = heads * HEAD_DIM
    tiles = []
    for t in range(rows // size):
        here, grad_here = qkv[t * size : (t + 1) * size], grad[t * size : (t + 1) * size]
        dq, dk, dv = [], [], []
        for h in range(heads):
            q, k, v = (
                here[:, j * width + h * HEAD_DIM : j * width + (h + 1) * HEAD_DIM] for j in range(3)
            )
            g = grad_here[:, h * HEAD_DIM : (h + 1) * HEAD_DIM]
            p = softmax_rows(q, k, mask)
            dv.append(kdot(p.astype(BF16), g, TN).astype(BF16))
            dp = kdot(g, v, NT)
            ds = p * (dp - jnp.sum(p * dp, axis=-1, keepdims=True)) * HEAD_DIM ** (-0.5)
            ds = ds.astype(BF16)
            dq.append(kdot(ds, k, NN).astype(BF16))
            dk.append(kdot(ds, q, TN).astype(BF16))
        tiles.append(jnp.concatenate(dq + dk + dv, axis=1))
    return tiles[0] if len(tiles) == 1 else jnp.concatenate(tiles, axis=0)


def gelu_tanh(v):
    return jnp.tanh(GELU_C * (v + GELU_A * v * v * v))


def tile_at(ref, i, temporal):
    if temporal:
        return ref.at[i // 2, pl.ds(i % 2 * 2, 2)]
    return ref.at[i // 2, :, i % 2]


def flat(v):
    return v.reshape(-1, v.shape[-1])


def after_tiles(temporal, i):
    if not temporal:
        return (i,)
    return (i - 1, i) if i % 2 else ()


def attention_up(x_or_h, x_own, mod, weights, biases, mask, cid):
    temporal = mask is not None
    qkv_w, proj_t = weights
    d, hc = proj_t.shape
    c = qkv_w.shape[1]
    heads = hc // HEAD_DIM
    _, rows, _ = x_own.shape
    tokens = 4 * rows
    ins = dict(src=x_or_h, x_own=x_own, mod=mod, qkv_w=qkv_w, proj_t=proj_t)
    ins.update(qkv_b=biases[0], proj_b=biases[1])
    if temporal:
        ins.update(mask=mask)
    outs = dict(
        qkv=sds((4, tokens, c)),
        att=sds((4, tokens, hc)),
        branch=sds(x_own.shape),
        mixed=sds(x_own.shape, F32),
        full=sds((2, 4, 2, rows, d)),
    )
    if not temporal:
        outs.update(h1=sds((4, tokens, d)))

    def body(r):
        net = Narrow(r)
        net.barrier()

        def tile(i):
            if temporal:
                h = r.src[i]
            else:
                v, _ = norm_rows(r.src[i].astype(F32))
                h = (v * (1.0 + r.mod[i // 2, 1:2]) + r.mod[i // 2, 0:1]).astype(BF16)
                r.h1[i] = h
            qkv = (kdot(h, r.qkv_w[...], NN) + r.qkv_b[...]).astype(BF16)
            r.qkv[i] = qkv
            att = attend(qkv, r.mask[i // 2] if temporal else None, heads)
            r.att[i] = att
            part = kdot(att, r.proj_t[...], NT).astype(BF16)
            target = tile_at(r.part, i, temporal)
            target[...] = part.reshape(target.shape)
            for j in after_tiles(temporal, i):
                net.sum_start(j)

        def middle(i):
            m = i // 2
            branch = net.sum_end(i)
            r.branch[i] = branch.astype(BF16)
            mixed = r.x_own[i].astype(F32) + r.mod[m, 2:3] * (branch + r.proj_b[...])
            r.mixed[i] = mixed
            v, _ = norm_rows(mixed)
            net.gather_start(i, (v * (1.0 + r.mod[m, 4:5]) + r.mod[m, 3:4]).astype(BF16))

        late = 1 if temporal else 0
        pipeline(
            4,
            [(0, tile), (1 + late, net.sum_cross), (2 + late, middle), (3 + late, net.gather_forward)],
        )
        net.sum_drain()
        net.gather_drain()

    scratch = dict(Narrow.sum_scratch(rows, d), **Narrow.gather_scratch(rows, d))
    return call("attention_up", body, ins, outs, scratch, cid, hbm=("full",))


def feed_forward(h2, mixed, mod, weights, biases, cid):
    up_w, down_t = weights
    d, c = up_w.shape
    _, rows, _ = mixed.shape
    ins = dict(h2=h2, mixed=mixed, mod=mod, up_w=up_w, down_t=down_t)
    ins.update(up_b=biases[0], down_b=biases[1])
    outs = dict(before=sds((4, 4 * rows, c)), feed=sds(mixed.shape), y=sds(mixed.shape))

    def body(r):
        net = Narrow(r)
        net.barrier()

        def tile(i):
            v = kdot(flat(r.h2[i // 2, :, i % 2]), r.up_w[...], NN) + r.up_b[...]
            r.before[i] = v.astype(BF16)
            active = (0.5 * v * (1.0 + gelu_tanh(v))).astype(BF16)
            part = kdot(active, r.down_t[...], NT).astype(BF16)
            r.part[i // 2, :, i % 2] = part.reshape(4, rows, d)
            net.sum_start(i)

        def middle(i):
            feed = net.sum_end(i)
            r.feed[i] = feed.astype(BF16)
            r.y[i] = (r.mixed[i] + r.mod[i // 2, 5:6] * (feed + r.down_b[...])).astype(BF16)

        pipeline(4, [(0, tile), (1, net.sum_cross), (2, middle)])
        net.sum_drain()

    return call("feed_forward", body, ins, outs, Narrow.sum_scratch(rows, d), cid)


def gather_own(name, value_of, ins, more_outs, rows, d, cid):
    def body(r):
        net = Narrow(r)
        net.barrier()
        pipeline(
            4,
            [(0, lambda i: net.gather_start(i, value_of(r, i))), (2, net.gather_forward)],
        )
        net.gather_drain()

    outs = dict(full=sds((2, 4, 2, rows, d)), **more_outs)
    return call(name, body, ins, outs, Narrow.gather_scratch(rows, d), cid, hbm=("full",))


def gather_normed(x_own, mod, cid):
    def value(r, i):
        v, _ = norm_rows(r.x[i].astype(F32))
        return (v * (1.0 + r.mod[i // 2, 1:2]) + r.mod[i // 2, 0:1]).astype(BF16)

    _, rows, d = x_own.shape
    return gather_own("gather_normed", value, dict(x=x_own, mod=mod), {}, rows, d, cid)["full"]


def add_rows(ref, index, v, first):
    if first:
        ref[index] = v
    else:
        ref[index] += v


def gather_gated(dy, feed, mod, down_b, cid):
    def value(r, i):
        m = i // 2
        v = r.dy[i].astype(F32)
        gated = r.mod[m, 5:6] * v
        dgate = column_sum(v * (r.feed[i].astype(F32) + r.down_b[...]))
        add_rows(r.dgate, pl.ds(m, 1), dgate, i % 2 == 0)
        add_rows(r.dbias, pl.ds(0, 1), column_sum(gated), i == 0)
        return gated.astype(BF16)

    _, rows, d = dy.shape
    out = gather_own(
        "gather_gated",
        value,
        dict(dy=dy, feed=feed, mod=mod, down_b=down_b),
        dict(dgate=sds((2, d), F32), dbias=sds((1, d), F32)),
        rows,
        d,
        cid,
    )
    return out["full"], out["dgate"], out["dbias"]


def gather_plain(own, cid):
    _, rows, d = own.shape
    return gather_own("gather_plain", lambda r, i: r.x[i], dict(x=own), {}, rows, d, cid)["full"]


def feed_back(dfeed, before, h2, mixed, dy, branch, mod, weights, proj_b, cid):
    up_w, down_t = weights
    d, c = up_w.shape
    _, rows, _ = mixed.shape
    tokens = 4 * rows
    ins = dict(dfeed=dfeed, before=before, h2=h2, mixed=mixed, dy=dy, branch=branch, mod=mod)
    ins.update(up_w=up_w, down_t=down_t, proj_b=proj_b)
    outs = dict(
        full=sds((2, 4, 2, rows, d)),
        dmixed=sds(mixed.shape, F32),
        dup=sds(up_w.shape),
        ddown=sds(down_t.shape),
        dup_b=sds((1, c), F32),
        dshift=sds((2, d), F32),
        dscale=sds((2, d), F32),
        dgate=sds((2, d), F32),
        dproj_b=sds((1, d), F32),
    )
    strip = c // 3

    def body(r):
        net = Narrow(r)
        net.barrier()

        def tile(i):
            da = kdot(flat(r.dfeed[i // 2, :, i % 2]), r.down_t[...], NN)
            v = r.before[i].astype(F32)
            t = gelu_tanh(v)
            r.active[i // 2, :, i % 2] = (0.5 * v * (1.0 + t)).astype(BF16).reshape(4, rows, c)
            slope = 0.5 * (1.0 + t) + 0.5 * v * (1.0 - t * t) * (
                GELU_C * (1.0 + 3.0 * GELU_A * v * v)
            )
            db = (da * slope).astype(BF16)
            r.dbefore[i // 2, :, i % 2] = db.reshape(4, rows, c)
            add_rows(r.dup_b, pl.ds(0, 1), column_sum(db.astype(F32)), i == 0)
            part = kdot(db, r.up_w[...], NT).astype(BF16)
            r.part[i // 2, :, i % 2] = part.reshape(4, rows, d)
            net.sum_start(i)

        def middle(i):
            m = i // 2
            dh = net.sum_end(i)
            v, rs = norm_rows(r.mixed[i])
            add_rows(r.dshift, pl.ds(m, 1), column_sum(dh), i % 2 == 0)
            add_rows(r.dscale, pl.ds(m, 1), column_sum(dh * v), i % 2 == 0)
            dmixed = r.dy[i].astype(F32) + norm_back(dh, v, rs, r.mod[m, 4:5])
            r.dmixed[i] = dmixed
            gated = r.mod[m, 2:3] * dmixed
            dgate = column_sum(dmixed * (r.branch[i].astype(F32) + r.proj_b[...]))
            add_rows(r.dgate, pl.ds(m, 1), dgate, i % 2 == 0)
            add_rows(r.dproj_b, pl.ds(0, 1), column_sum(gated), i == 0)
            net.gather_start(i, gated.astype(BF16))

        def weight_strip(j):
            cols = pl.ds(j % 3 * strip, strip)
            if j < 3:
                r.dup[:, cols] = kdot(
                    flat(r.h2[...]), r.dbefore[:, :, :, :, cols].reshape(4 * tokens, strip), TN
                ).astype(BF16)
            else:
                r.ddown[:, cols] = kdot(
                    flat(r.dfeed[...]), r.active[:, :, :, :, cols].reshape(4 * tokens, strip), TN
                ).astype(BF16)

        pipeline(4, [(0, tile), (1, net.sum_cross), (2, middle), (4, net.gather_forward), (4, weight_strip)])
        weight_strip(4)
        weight_strip(5)
        net.sum_drain()
        net.gather_drain()

    scratch = dict(Narrow.sum_scratch(rows, d), **Narrow.gather_scratch(rows, d))
    scratch.update(
        dbefore=pltpu.VMEM((2, 4, 2, rows, c), BF16), active=pltpu.VMEM((2, 4, 2, rows, c), BF16)
    )
    return call("feed_back", body, ins, outs, scratch, cid, hbm=("full",))


def attention_back(dbranch, qkv, att, h1, x_own, dmixed, mod, weights, mask, cid):
    temporal = mask is not None
    qkv_w, proj_t = weights
    d, hc = proj_t.shape
    c = qkv_w.shape[1]
    heads = hc // HEAD_DIM
    _, rows, _ = x_own.shape
    tokens = 4 * rows
    ins = dict(dbranch=dbranch, qkv=qkv, att=att, h1=h1, x_own=x_own, dmixed=dmixed, mod=mod)
    ins.update(qkv_w=qkv_w, proj_t=proj_t)
    if temporal:
        ins.update(mask=mask)
    outs = dict(
        dx=sds(x_own.shape),
        dqkv_w=sds(qkv_w.shape),
        dproj=sds(proj_t.shape),
        dqkv_b=sds((1, c), F32),
        dshift=sds((2, d), F32),
        dscale=sds((2, d), F32),
    )

    def body(r):
        net = Narrow(r)
        net.barrier()

        def tile(i):
            dbranch = flat(tile_at(r.dbranch, i, temporal)[...])
            if not temporal:
                r.dbr[i] = dbranch
            da = kdot(dbranch, r.proj_t[...], NN).astype(BF16)
            dqkv = attend_back(r.qkv[i], da, r.mask[i // 2] if temporal else None, heads)
            r.dqkv[i] = dqkv
            add_rows(r.dqkv_b, pl.ds(0, 1), column_sum(dqkv.astype(F32)), i == 0)
            part = kdot(dqkv, r.qkv_w[...], NT).astype(BF16)
            target = tile_at(r.part, i, temporal)
            target[...] = part.reshape(target.shape)
            for j in after_tiles(temporal, i):
                net.sum_start(j)

        def middle(i):
            m = i // 2
            dh = net.sum_end(i)
            v, rs = norm_rows(r.x_own[i].astype(F32))
            add_rows(r.dshift, pl.ds(m, 1), column_sum(dh), i % 2 == 0)
            add_rows(r.dscale, pl.ds(m, 1), column_sum(dh * v), i % 2 == 0)
            r.dx[i] = (r.dmixed[i] + norm_back(dh, v, rs, r.mod[m, 1:2])).astype(BF16)

        late = 1 if temporal else 0
        pipeline(4, [(0, tile), (1 + late, net.sum_cross), (2 + late, middle)])
        r.dqkv_w[...] = kdot(flat(r.h1[...]), flat(r.dqkv[...]), TN).astype(BF16)
        source = r.dbranch if temporal else r.dbr
        r.dproj[...] = kdot(flat(source[...]), flat(r.att[...]), TN).astype(BF16)
        net.sum_drain()

    scratch = Narrow.sum_scratch(rows, d)
    scratch.update(dqkv=pltpu.VMEM((4, tokens, c), BF16))
    if not temporal:
        scratch.update(dbr=pltpu.VMEM((4, tokens, d), BF16))
    return call("attention_back", body, ins, outs, scratch, cid)


def wide_gather(shard):
    size = lax.axis_size("wide")
    if size != 8:
        return lax.all_gather(shard, "wide", axis=0, tiled=True)
    rows = shard.shape[0]
    pair = [(i, i ^ 1) for i in range(8)]
    ring = [(i, (i + 2) % 8) for i in range(8)]
    w = lax.axis_index("wide")
    z, x = w // 2, w % 2
    full = jnp.zeros((8 * rows,) + shard.shape[1:], shard.dtype)
    here = shard
    for step in range(4):
        owner = lax.rem(z - step + 4, 4)
        other = lax.ppermute(here, "wide", pair)
        full = lax.dynamic_update_slice_in_dim(full, here, (owner * 2 + x) * rows, 0)
        full = lax.dynamic_update_slice_in_dim(full, other, (owner * 2 + 1 - x) * rows, 0)
        if step < 3:
            here = lax.ppermute(here, "wide", ring)
    return full


def wide_scatter(grad):
    size = lax.axis_size("wide")
    rows = grad.shape[0] // size
    if size != 8:
        moved = lax.all_to_all(grad, "wide", split_axis=0, concat_axis=0, tiled=True)
        return jnp.sum(moved.reshape((size, rows) + grad.shape[1:]).astype(F32), axis=0)
    pair = [(i, i ^ 1) for i in range(8)]
    ring = [(i, (i + 2) % 8) for i in range(8)]
    w = lax.axis_index("wide")
    z, x = w // 2, w % 2
    parts = grad.reshape((4, 2, rows) + grad.shape[1:])
    mine = lax.dynamic_index_in_dim(parts, x, 1, keepdims=False)
    theirs = lax.dynamic_index_in_dim(parts, 1 - x, 1, keepdims=False)
    column = mine.astype(F32) + lax.ppermute(theirs, "wide", pair).astype(F32)
    total = None
    for step in range(4):
        owner = lax.rem(z - step + 7, 4)
        term = lax.dynamic_index_in_dim(column, owner, 0, keepdims=False)
        total = term if total is None else term + total.astype(F32)
        if step < 3:
            total = lax.ppermute(total.astype(BF16), "wide", ring)
    return total


def exchange(rows_in, seq_group):
    mb, half, count, d = rows_in.shape
    v = rows_in.reshape(mb, half, seq_group, count // seq_group, d)
    v = group_all_to_all(jnp.moveaxis(v, 2, 0), seq_group)
    return jnp.moveaxis(v, 0, 1).reshape(mb, half, count, d)


def exchange_back(rows_in, seq_group):
    mb, half, count, d = rows_in.shape
    v = rows_in.reshape(mb, seq_group, half, count // seq_group, d)
    v = group_all_to_all(jnp.moveaxis(v, 1, 0), seq_group)
    return jnp.moveaxis(v, 0, 2).reshape(mb, half, count, d)


def group_all_to_all(v, seq_group):
    size = lax.axis_size("wide")
    groups = None
    if seq_group != size:
        groups = [
            list(range(first, first + seq_group)) for first in range(0, size, seq_group)
        ]
    return lax.all_to_all(
        v, "wide", split_axis=0, concat_axis=0, tiled=True, axis_index_groups=groups
    )


def shards(
    tokens,
    conditioning,
    frame_segments,
    cotangent,
    qkv_weight,
    qkv_bias,
    proj_weight,
    proj_bias,
    up_weight,
    up_bias,
    down_weight,
    down_bias,
    ada_weight,
    ada_bias,
):
    mb, half, patches, d = tokens.shape
    parts = lax.axis_size("narrow")
    seq_frames = frame_segments.shape[2]
    seqs = frame_segments.shape[1]
    seq_group = seq_frames // half
    n = lax.axis_index("narrow")
    w = lax.axis_index("wide")
    seq_here = w // seq_group
    blocks = qkv_weight.shape[0]
    rows = patches // parts
    local = qkv_bias.shape[-1]
    shard_rows = ada_weight.shape[1]
    own_shape = (mb, half, rows, d)
    chunk_shape = (mb * half, rows, d)

    weights = []
    for b in range(blocks):
        weights.append(
            tuple(
                lax.all_gather(piece, "wide", axis=0, tiled=True)
                for piece in (
                    qkv_weight[b].reshape(shard_rows, -1),
                    proj_weight[b].T,
                    up_weight[b],
                    down_weight[b].T,
                )
            )
        )
    qkv_b = jnp.concatenate(
        [qkv_bias[:, 0], jnp.zeros_like(qkv_bias[:, 0]), qkv_bias[:, 1]], axis=1
    ).astype(F32)[:, None]
    proj_b, up_b, down_b = (v.astype(F32)[:, None] for v in (proj_bias, up_bias, down_bias))

    silu = jax.nn.silu(conditioning.astype(F32)).astype(BF16)
    silu_rows = lax.dynamic_slice_in_dim(silu, w * shard_rows, shard_rows, 2)
    partial = jnp.einsum(
        "msr,brck->bmsck", silu_rows, ada_weight, preferred_element_type=F32
    )
    total = lax.psum(partial, "wide")
    here = lax.dynamic_index_in_dim(total, seq_here, 2, keepdims=False)
    here = here + ada_bias.astype(F32)[:, None]
    modulation = lax.all_gather(here, "narrow", axis=3, tiled=True)
    mod0, mod1 = modulation[0], modulation[1]

    frame_ids = lax.dynamic_index_in_dim(frame_segments, seq_here, 1, keepdims=False)
    count = rows // seq_group
    index = jnp.arange(seq_frames * count)
    clip = frame_ids[:, index // count]
    seen = (index[:, None] % count == index[None, :] % count) & (
        clip[:, :, None] == clip[:, None, :]
    )
    mask = jnp.where(seen, 0.0, MASKED).astype(F32)

    def own_of(full):
        return lax.dynamic_slice_in_dim(full, n * rows, rows, 2).reshape(chunk_shape)

    x0 = own_of(tokens)
    up0 = attention_up(
        tokens.reshape(mb * half, patches, d),
        x0,
        mod0,
        weights[0][:2],
        (qkv_b[0], proj_b[0]),
        None,
        0,
    )
    ff0 = feed_forward(
        up0["full"], up0["mixed"], mod0, weights[0][2:], (up_b[0], down_b[0]), 1
    )

    x1 = exchange(ff0["y"].reshape(own_shape), seq_group).reshape(chunk_shape)
    h1 = gather_normed(x1, mod1, 2).reshape(4, patches, d)
    up1 = attention_up(h1, x1, mod1, weights[1][:2], (qkv_b[1], proj_b[1]), mask, 3)
    ff1 = feed_forward(
        up1["full"], up1["mixed"], mod1, weights[1][2:], (up_b[1], down_b[1]), 4
    )
    out_own = exchange_back(ff1["y"].reshape(own_shape), seq_group).reshape(chunk_shape)
    layer_out = gather_plain(out_own, 5)
    layer_out = jnp.swapaxes(layer_out, 1, 2).reshape(mb, half, patches, d)

    dy1 = exchange(own_of(cotangent).reshape(own_shape), seq_group).reshape(chunk_shape)
    dfeed, dgate2_1, ddown_b1 = gather_gated(dy1, ff1["feed"], mod1, down_b[1], 6)
    fb1 = feed_back(
        dfeed, ff1["before"], up1["full"], up1["mixed"], dy1, up1["branch"], mod1,
        weights[1][2:], proj_b[1], 7,
    )
    ab1 = attention_back(
        fb1["full"], up1["qkv"], up1["att"], h1, x1, fb1["dmixed"], mod1, weights[1][:2], mask, 8
    )
    dy0 = exchange_back(ab1["dx"].reshape(own_shape), seq_group).reshape(chunk_shape)
    dfeed, dgate2_0, ddown_b0 = gather_gated(dy0, ff0["feed"], mod0, down_b[0], 9)
    fb0 = feed_back(
        dfeed, ff0["before"], up0["full"], up0["mixed"], dy0, up0["branch"], mod0,
        weights[0][2:], proj_b[0], 10,
    )
    ab0 = attention_back(
        fb0["full"], up0["qkv"], up0["att"], up0["h1"], x0, fb0["dmixed"], mod0,
        weights[0][:2], None, 11,
    )
    input_grad = gather_plain(ab0["dx"], 12)
    input_grad = jnp.swapaxes(input_grad, 1, 2).astype(F32).reshape(mb, half, patches, d)

    grads = [
        [wide_scatter(v) for v in (ab["dqkv_w"], ab["dproj"], fb["dup"], fb["ddown"])]
        for ab, fb in ((ab0, fb0), (ab1, fb1))
    ]

    dmod = jnp.stack(
        [
            jnp.stack(
                [ab["dshift"], ab["dscale"], fb["dgate"], fb["dshift"], fb["dscale"], dgate2],
                axis=1,
            )
            for ab, fb, dgate2 in ((ab0, fb0, dgate2_0), (ab1, fb1, dgate2_1))
        ]
    )
    slot = (jnp.arange(seqs) == seq_here).astype(F32)
    dmod = dmod[:, :, None] * slot[None, None, :, None, None]
    model_b = jnp.stack(
        [
            jnp.concatenate([fb0["dproj_b"], ddown_b0]),
            jnp.concatenate([fb1["dproj_b"], ddown_b1]),
        ]
    )
    hidden_b = jnp.concatenate(
        [
            jnp.concatenate([ab0["dqkv_b"], fb0["dup_b"]], axis=1),
            jnp.concatenate([ab1["dqkv_b"], fb1["dup_b"]], axis=1),
        ]
    )
    dmod, model_b = lax.psum((dmod, model_b), ("wide", "narrow"))
    hidden_b = lax.psum(hidden_b, "wide")
    dmod = lax.dynamic_slice_in_dim(dmod, n * local, local, 4)
    silu_f = silu_rows.astype(F32)
    ada_wgrad = sum(
        silu_f[m, s][None, :, None, None] * dmod[:, m, s][:, None]
        for m in range(mb)
        for s in range(seqs)
    )
    ada_bgrad = jnp.sum(dmod, axis=(1, 2))
    return (
        layer_out,
        input_grad,
        jnp.stack([g[0] for g in grads]).reshape(qkv_weight.shape),
        jnp.stack([hidden_b[:, :local], hidden_b[:, 2 * local : 3 * local]], axis=1),
        jnp.stack([g[1].T for g in grads]),
        model_b[:, 0],
        jnp.stack([g[2] for g in grads]),
        hidden_b[:, 3 * local :],
        jnp.stack([g[3].T for g in grads]),
        model_b[:, 1],
        ada_wgrad,
        ada_bgrad,
    )


def solution(mesh):
    return jax.shard_map(
        shards,
        mesh=mesh,
        in_specs=(
            P(None, "wide", None, None),
            P(),
            P(),
            P(None, "wide", None, None),
            P(None, "wide", None, "narrow"),
            P(None, None, "narrow"),
            P(None, "narrow", "wide"),
            P(),
            P(None, "wide", "narrow"),
            P(None, "narrow"),
            P(None, "narrow", "wide"),
            P(),
            P(None, "wide", None, "narrow"),
            P(None, None, "narrow"),
        ),
        out_specs=(
            P(None, "wide", None, None),
            P(None, "wide", None, None),
            P(None, "wide", None, "narrow"),
            P(None, None, "narrow"),
            P(None, "narrow", "wide"),
            P(),
            P(None, "wide", "narrow"),
            P(None, "narrow"),
            P(None, "narrow", "wide"),
            P(),
            P(None, "wide", None, "narrow"),
            P(None, None, "narrow"),
        ),
        check_vma=False,
    )
```

```python
import functools
import types

import jax
import jax.numpy as jnp
from jax import lax
from jax.experimental import pallas as pl
from jax.experimental.pallas import tpu as pltpu
from jax.sharding import PartitionSpec as P

HEAD_DIM = 72
NORM_EPS = 1e-06
MASKED = -1e30
BF16 = jnp.bfloat16
F32 = jnp.float32


PLANS = dict(
    up0=(2, 3, 5, 6),
    ff0=(1, 4, 6),
    up1=(2, 3, 5, 6),
    fb1=(4, 5, 6, 7, 8),
    ab1=(1, 2, 4, 5, 7),
    fb0=(1, 2, 3, 4, 5, 5, 6, 7, 8),
    ab0=(1, 2, 4),
)
NN, NT, TN = ((1,), (0,)), ((1,), (1,)), ((0,), (0,))
CHUNKS = 4
GELU_C = 0.7978845608028654
GELU_A = 0.044715


def kdot(a, b, dims):
    return lax.dot_general(a, b, (dims, ((), ())), preferred_element_type=F32)


def call(name, body, ins, outs, scratch, cid=None, hbm=(), hosts=()):
    ins, outs, scratch, hbm = dict(ins), dict(outs), dict(scratch), set(hbm)
    for host in hosts:
        ins.update(host.ins())
        outs.update(host.outs())
        scratch.update(host.scratch())
        hbm.update(host.hbm())
    names = list(ins) + list(outs) + list(scratch)

    def spec(key):
        return pl.BlockSpec(memory_space=pl.ANY if key in hbm else pltpu.VMEM)

    def kernel(*refs):
        r = types.SimpleNamespace(**dict(zip(names, refs)))
        for host in hosts:
            host.bind(r)
        body(r)

    results = pl.pallas_call(
        kernel,
        in_specs=[spec(key) for key in ins],
        out_specs=[spec(key) for key in outs],
        out_shape=list(outs.values()),
        scratch_shapes=list(scratch.values()),
        compiler_params=pltpu.CompilerParams(
            vmem_limit_bytes=60 << 20,
            collective_id=cid,
            has_side_effects=cid is not None,
        ),
        name=name,
    )(*ins.values())
    return dict(zip(outs, results))


def pipeline(count, stages, hosts=(), plan=()):
    every = all_phases(hosts)
    phases, left = list(zip(plan, every)), every[len(plan) :]
    for step in range(count + max(lag for lag, _ in stages)):
        for lag, stage in stages:
            if 0 <= step - lag < count:
                stage(step - lag)
        for at, phase in phases:
            if at == step:
                phase()
    for phase in left:
        phase()
    for host in hosts:
        host.drain()


def all_phases(hosts):
    early = [host.phases() for host in hosts if not host.late]
    turns = [p for turn in zip(*early) for p in turn]
    return turns + [p for host in hosts if host.late for p in [host.begin] + host.phases()]


def wide_pair(w):
    return w + 1 - 2 * lax.rem(w, 2)


class Host:
    late = False

    def bind(self, refs):
        w = lax.axis_index("wide")
        self.x, self.z = lax.rem(w, 2), lax.div(w, 2)
        self.pair, self.up = wide_pair(w), lax.rem(w + 2, 8)
        self.r = refs

    def get(self, key):
        return getattr(self.r, self.tag + key)

    def block(self, z, x):
        return pl.ds(pl.multiple_of((z * 2 + x) * self.rows, self.rows), self.rows)

    def remote(self, src, dst, sems, k, other):
        return pltpu.make_async_remote_copy(
            src_ref=src,
            dst_ref=dst,
            send_sem=sems.at[0, k],
            recv_sem=sems.at[1, k],
            device_id={"wide": other},
        )


def column_parts(cols):
    cut = (cols // 128 + 1) // 2 * 128
    return (pl.ds(0, cut), pl.ds(cut, cols - cut))


class WideGather(Host):
    def __init__(self, tag, shard):
        self.tag, self.shard = tag, shard
        self.rows, self.cols = shard.shape
        self.parts = column_parts(self.cols)

    def ins(self):
        return {self.tag + "shard": self.shard}

    def outs(self):
        return {self.tag + "all": sds((8 * self.rows, self.cols))}

    def scratch(self):
        return {
            self.tag + "zsem": pltpu.SemaphoreType.DMA((2, 6)),
            self.tag + "xsem": pltpu.SemaphoreType.DMA((2, 8)),
            self.tag + "sem": pltpu.SemaphoreType.DMA,
        }

    def hbm(self):
        return [self.tag + "all"]

    def rows_of(self, k, part):
        here = self.block(lax.rem(self.z - k + 4, 4), self.x)
        place = self.get("all").at[here, self.parts[part]]
        return (self.get("shard").at[:, self.parts[part]] if k == 0 else place), place

    def z_copy(self, k, part):
        return self.remote(*self.rows_of(k, part), self.get("zsem"), 2 * k + part, self.up)

    def x_copy(self, k, part):
        return self.remote(*self.rows_of(k, part), self.get("xsem"), 2 * k + part, self.pair)

    def local_copy(self):
        here = self.block(self.z, self.x)
        return pltpu.make_async_copy(
            self.get("shard"), self.get("all").at[here], self.get("sem")
        )

    def start(self):
        for part in range(2):
            self.z_copy(0, part).start()
            self.x_copy(0, part).start()
        self.local_copy().start()

    def phases(self):
        def step(k):
            for part in range(2):
                self.z_copy(k - 1, part).wait_recv()
                if k < 3:
                    self.z_copy(k, part).start()
                self.x_copy(k, part).start()

        return [lambda k=k: step(k) for k in (1, 2, 3)]

    def drain(self):
        self.local_copy().wait()
        for k in range(4):
            for part in range(2):
                self.x_copy(k, part).wait()
                if k < 3:
                    self.z_copy(k, part).wait_send()


class WideScatter(Host):
    def __init__(self, tag, grad, source=None):
        self.tag, self.grad, self.source = tag, grad, source
        self.late = source is not None
        self.rows, self.cols = grad.shape[0] // 8, grad.shape[1]
        self.parts = column_parts(self.cols)

    def ins(self):
        return {} if self.late else {self.tag + "grad": self.grad}

    def outs(self):
        return {self.tag + "sum": sds((self.rows, self.cols), F32)}

    def scratch(self):
        size = (self.rows, self.cols)
        return {
            self.tag + "got": pltpu.VMEM((4,) + size, BF16),
            self.tag + "send": pltpu.VMEM((3,) + size, BF16),
            self.tag + "ring": pltpu.VMEM((3,) + size, BF16),
            self.tag + "xsem": pltpu.SemaphoreType.DMA((2, 8)),
            self.tag + "zsem": pltpu.SemaphoreType.DMA((2, 6)),
        }

    def hbm(self):
        return []

    def rows_of(self, s, x, part):
        grad = getattr(self.r, self.source) if self.late else self.get("grad")
        return grad.at[self.block(lax.rem(self.z - s + 7, 4), x), self.parts[part]]

    def x_copy(self, s, part):
        return self.remote(
            self.rows_of(s, 1 - self.x, part),
            self.get("got").at[s, :, self.parts[part]],
            self.get("xsem"),
            2 * s + part,
            self.pair,
        )

    def z_copy(self, s, part):
        cols = self.parts[part]
        return self.remote(
            self.get("send").at[s, :, cols],
            self.get("ring").at[s, :, cols],
            self.get("zsem"),
            2 * s + part,
            self.up,
        )

    def start(self):
        if not self.late:
            self.begin()

    def begin(self):
        for s in range(4):
            for part in range(2):
                self.x_copy(s, part).start()

    def phases(self):
        def step(s):
            for part in range(2):
                cols = self.parts[part]
                self.x_copy(s, part).wait_recv()
                total = self.rows_of(s, self.x, part)[...].astype(F32)
                total = total + self.get("got")[s, :, cols].astype(F32)
                if s:
                    self.z_copy(s - 1, part).wait_recv()
                    total = total + self.get("ring")[s - 1, :, cols].astype(F32)
                if s < 3:
                    self.get("send")[s, :, cols] = total.astype(BF16)
                    self.z_copy(s, part).start()
                else:
                    self.get("sum")[:, cols] = total

        return [lambda s=s: step(s) for s in range(4)]

    def drain(self):
        for s in range(4):
            for part in range(2):
                self.x_copy(s, part).wait_send()
                if s < 3:
                    self.z_copy(s, part).wait_send()


class Narrow:
    def __init__(self, refs):
        n = lax.axis_index("narrow")
        self.n, self.core, self.across, self.far = (
            n,
            n + 1 - 2 * lax.rem(n, 2),
            lax.rem(n + 2, 4),
            3 - n,
        )
        self.r = refs

    def barrier(self, hosts=(), cross=False):
        sem = pltpu.get_barrier_semaphore()
        for other in (self.core, self.across):
            pl.semaphore_signal(sem, inc=1, device_id={"narrow": other})
        if cross:
            w = lax.axis_index("wide")
            for k in range(1, 8):
                pl.semaphore_signal(sem, inc=1, device_id={"wide": lax.rem(w + k, 8)})
        elif hosts:
            w = lax.axis_index("wide")
            for other in (wide_pair(w), lax.rem(w + 6, 8)):
                pl.semaphore_signal(sem, inc=1, device_id={"wide": other})
        pl.semaphore_wait(sem, 9 if cross else 4 if hosts else 2)
        for host in hosts:
            host.start()

    def remote(self, src, dst, sems, index, other):
        return pltpu.make_async_remote_copy(
            src_ref=src,
            dst_ref=dst,
            send_sem=sems.at[(0,) + index],
            recv_sem=sems.at[(1,) + index],
            device_id={"narrow": other},
        )

    def sum_scratch(rows, d):
        return dict(
            part=pltpu.VMEM((CHUNKS // 2, 4, 2, rows, d), BF16),
            near=pltpu.VMEM((CHUNKS, 2, rows, d), BF16),
            pair=pltpu.VMEM((CHUNKS, rows, d), BF16),
            cross=pltpu.VMEM((CHUNKS, rows, d), BF16),
            near_sem=pltpu.SemaphoreType.DMA((2, CHUNKS, 2)),
            cross_sem=pltpu.SemaphoreType.DMA((2, CHUNKS)),
        )

    def near_copy(self, i, which):
        owner = self.core if which == 0 else self.far
        return self.remote(
            self.r.part.at[i // 2, owner, i % 2],
            self.r.near.at[i, which],
            self.r.near_sem,
            (i, which),
            self.core,
        )

    def cross_copy(self, i):
        return self.remote(
            self.r.pair.at[i], self.r.cross.at[i], self.r.cross_sem, (i,), self.across
        )

    def sum_start(self, i):
        self.near_copy(i, 1).start()
        self.near_copy(i, 0).start()

    def sum_cross(self, i):
        self.near_copy(i, 1).wait_recv()
        mine = self.r.part[i // 2, self.across, i % 2].astype(F32)
        self.r.pair[i] = (mine + self.r.near[i, 1].astype(F32)).astype(BF16)
        self.cross_copy(i).start()

    def sum_end(self, i):
        self.near_copy(i, 0).wait_recv()
        total = self.r.part[i // 2, self.n, i % 2].astype(F32) + self.r.near[i, 0].astype(F32)
        self.cross_copy(i).wait_recv()
        return total + self.r.cross[i].astype(F32)

    def sum_drain(self):
        for i in range(CHUNKS):
            self.near_copy(i, 0).wait_send()
            self.near_copy(i, 1).wait_send()
            self.cross_copy(i).wait_send()

    def gather_scratch(rows, d):
        return dict(
            own=pltpu.VMEM((CHUNKS, rows, d), BF16),
            own_sem=pltpu.SemaphoreType.DMA((CHUNKS,)),
            out_sem=pltpu.SemaphoreType.DMA((2, CHUNKS, 3)),
        )

    def place(self, i, n):
        return self.r.full.at[i // 2, n, i % 2]

    def out_copy(self, i, which):
        if which == 2:
            rows = self.place(i, self.across)
            return self.remote(rows, rows, self.r.out_sem, (i, 2), self.core)
        other = self.across if which == 0 else self.core
        return self.remote(
            self.r.own.at[i], self.place(i, self.n), self.r.out_sem, (i, which), other
        )

    def own_copy(self, i):
        return pltpu.make_async_copy(
            self.r.own.at[i], self.place(i, self.n), self.r.own_sem.at[i]
        )

    def gather_start(self, i, value):
        self.r.own[i] = value
        self.out_copy(i, 0).start()
        self.out_copy(i, 1).start()
        self.own_copy(i).start()

    def gather_forward(self, i):
        self.out_copy(i, 0).wait_recv()
        self.out_copy(i, 2).start()

    def gather_drain(self):
        for i in range(CHUNKS):
            self.own_copy(i).wait()
            for which in range(3):
                self.out_copy(i, which).wait_send()
                if which:
                    self.out_copy(i, which).wait_recv()


class Cross:
    def __init__(self, refs):
        self.r, self.w = refs, lax.axis_index("wide")

    def scratch(count, d):
        return dict(
            cross_out=pltpu.VMEM((2, 2, 8, count, d), BF16),
            cross_in=pltpu.VMEM((2, 8, 2, count, d), BF16),
            cross_sems=pltpu.SemaphoreType.DMA((2, CHUNKS, 8)),
        )

    def back_scratch(count, d):
        return dict(
            cross_out=pltpu.VMEM((2, 8, 2, count, d), BF16),
            cross_in=pltpu.VMEM((2, 2, 8, count, d), BF16),
            cross_sems=pltpu.SemaphoreType.DMA((2, CHUNKS, 8)),
        )

    def copy(self, src, dst, i, k):
        return pltpu.make_async_remote_copy(
            src_ref=src,
            dst_ref=dst,
            send_sem=self.r.cross_sems.at[0, i, k],
            recv_sem=self.r.cross_sems.at[1, i, k],
            device_id={"wide": lax.rem(self.w + k, 8)},
        )

    def to_patches(self, i, k):
        m, f, other = i // 2, i % 2, lax.rem(self.w + k, 8)
        return self.copy(
            self.r.cross_out.at[m, f, other], self.r.cross_in.at[m, self.w, f], i, k
        )

    def send(self, i, value):
        m, f = i // 2, i % 2
        out = self.r.cross_out
        out[m, f] = value.reshape(out.shape[2:]).astype(BF16)
        for k in range(1, 8):
            self.to_patches(i, k).start()
        self.r.cross_in[m, self.w, f] = out[m, f, self.w]

    def received(self, c):
        m, h = c // 2, c % 2
        if h == 0:
            for i in (2 * m, 2 * m + 1):
                for k in range(1, 8):
                    self.to_patches(i, k).wait_recv()
        return self.r.cross_in[m, 4 * h : 4 * h + 4]

    def to_frames(self, m, k):
        other = lax.rem(self.w + k, 8)
        return self.copy(
            self.r.cross_out.at[m, other], self.r.cross_in.at[m, :, self.w], m, k
        )

    def send_back(self, c, value):
        m, h = c // 2, c % 2
        out = self.r.cross_out
        out[m, 4 * h : 4 * h + 4] = value.reshape((4,) + out.shape[2:]).astype(BF16)
        if h:
            for k in range(1, 8):
                self.to_frames(m, k).start()
            self.r.cross_in[m, :, self.w] = out[m, self.w]

    def received_back(self, i):
        m, f = i // 2, i % 2
        if f == 0:
            for k in range(1, 8):
                self.to_frames(m, k).wait_recv()
        return self.r.cross_in[m, f]

    def drain(self):
        for i in range(CHUNKS):
            for k in range(1, 8):
                self.to_patches(i, k).wait_send()

    def drain_back(self):
        for m in range(2):
            for k in range(1, 8):
                self.to_frames(m, k).wait_send()


def norm_rows(v):
    centred = v - jnp.mean(v, axis=-1, keepdims=True)
    r = lax.rsqrt(jnp.mean(centred * centred, axis=-1, keepdims=True) + NORM_EPS)
    return centred * r, r


def norm_back(grad, n, r, scale):
    dn = grad * (1.0 + scale)
    return r * (
        dn
        - jnp.mean(dn, axis=-1, keepdims=True)
        - n * jnp.mean(dn * n, axis=-1, keepdims=True)
    )


def column_sum(v):
    return jnp.sum(v, axis=0, keepdims=True)


def sds(shape, dtype=BF16):
    return jax.ShapeDtypeStruct(shape, dtype)


def softmax_rows(q, k, mask):
    s = kdot(q, k, NT) * HEAD_DIM ** (-0.5)
    if mask is not None:
        s = s + mask
    p = jnp.exp(s - jnp.max(s, axis=-1, keepdims=True))
    return p * (1.0 / jnp.sum(p, axis=-1, keepdims=True))


def attend(qkv, mask, heads):
    rows = qkv.shape[0]
    size = rows if mask is None else mask.shape[0]
    width = heads * HEAD_DIM
    tiles = []
    for t in range(rows // size):
        here = qkv[t * size : (t + 1) * size]
        outs = []
        for h in range(heads):
            q, k, v = (
                here[:, j * width + h * HEAD_DIM : j * width + (h + 1) * HEAD_DIM] for j in range(3)
            )
            outs.append(kdot(softmax_rows(q, k, mask).astype(BF16), v, NN).astype(BF16))
        tiles.append(jnp.concatenate(outs, axis=1))
    return tiles[0] if len(tiles) == 1 else jnp.concatenate(tiles, axis=0)


def attend_back(qkv, grad, mask, heads):
    rows = qkv.shape[0]
    size = rows if mask is None else mask.shape[0]
    width = heads * HEAD_DIM
    tiles = []
    for t in range(rows // size):
        here, grad_here = qkv[t * size : (t + 1) * size], grad[t * size : (t + 1) * size]
        dq, dk, dv = [], [], []
        for h in range(heads):
            q, k, v = (
                here[:, j * width + h * HEAD_DIM : j * width + (h + 1) * HEAD_DIM] for j in range(3)
            )
            g = grad_here[:, h * HEAD_DIM : (h + 1) * HEAD_DIM]
            p = softmax_rows(q, k, mask)
            dv.append(kdot(p.astype(BF16), g, TN).astype(BF16))
            dp = kdot(g, v, NT)
            ds = p * (dp - jnp.sum(p * dp, axis=-1, keepdims=True)) * HEAD_DIM ** (-0.5)
            ds = ds.astype(BF16)
            dq.append(kdot(ds, k, NN).astype(BF16))
            dk.append(kdot(ds, q, TN).astype(BF16))
        tiles.append(jnp.concatenate(dq + dk + dv, axis=1))
    return tiles[0] if len(tiles) == 1 else jnp.concatenate(tiles, axis=0)


def gelu_tanh(v):
    return jnp.tanh(GELU_C * (v + GELU_A * v * v * v))


def tile_at(ref, i, temporal):
    if temporal:
        return ref.at[i // 2, pl.ds(i % 2 * 2, 2)]
    return ref.at[i // 2, :, i % 2]


def flat(v):
    return v.reshape(-1, v.shape[-1])


def after_tiles(temporal, i):
    if not temporal:
        return (i,)
    return (i - 1, i) if i % 2 else ()


def attention_up(x_or_h, x_own, mod, pack, biases, mask, cid, hosts=(), plan=()):
    temporal = mask is not None
    d, hc = pack.shape[0], pack.shape[1] // 4
    c = 3 * hc
    heads = hc // HEAD_DIM
    _, rows, _ = x_own.shape
    tokens = 4 * rows
    ins = dict(src=x_or_h, x_own=x_own, mod=mod, pack=pack)
    ins.update(qkv_b=biases[0], proj_b=biases[1])
    if temporal:
        ins.update(mask=mask)
    outs = dict(
        qkv=sds((4, tokens, c)),
        att=sds((4, tokens, hc)),
        branch=sds(x_own.shape),
        mixed=sds(x_own.shape, F32),
        full=sds((2, 4, 2, rows, d)),
    )
    if not temporal:
        outs.update(h1=sds((4, tokens, d)))

    def body(r):
        net = Narrow(r)
        net.barrier(hosts)
        r.proj_t[...] = r.pack[:, c:]

        def tile(i):
            if temporal:
                h = r.src[i]
            else:
                v, _ = norm_rows(r.src[i].astype(F32))
                h = (v * (1.0 + r.mod[i // 2, 1:2]) + r.mod[i // 2, 0:1]).astype(BF16)
                r.h1[i] = h
            qkv = (kdot(h, r.pack[:, :c], NN) + r.qkv_b[...]).astype(BF16)
            r.qkv[i] = qkv
            att = attend(qkv, r.mask[i // 2] if temporal else None, heads)
            r.att[i] = att
            part = kdot(att, r.proj_t[...], NT).astype(BF16)
            target = tile_at(r.part, i, temporal)
            target[...] = part.reshape(target.shape)
            for j in after_tiles(temporal, i):
                net.sum_start(j)

        def middle(i):
            m = i // 2
            branch = net.sum_end(i)
            r.branch[i] = branch.astype(BF16)
            mixed = r.x_own[i].astype(F32) + r.mod[m, 2:3] * (branch + r.proj_b[...])
            r.mixed[i] = mixed
            v, _ = norm_rows(mixed)
            net.gather_start(i, (v * (1.0 + r.mod[m, 4:5]) + r.mod[m, 3:4]).astype(BF16))

        late = 1 if temporal else 0
        pipeline(
            4,
            [(0, tile), (1 + late, net.sum_cross), (2 + late, middle), (3 + late, net.gather_forward)],
            hosts,
            plan,
        )
        net.sum_drain()
        net.gather_drain()

    scratch = dict(Narrow.sum_scratch(rows, d), **Narrow.gather_scratch(rows, d))
    scratch.update(proj_t=pltpu.VMEM((d, hc), BF16))
    return call("attention_up", body, ins, outs, scratch, cid, ("full",), hosts)


def feed_forward(
    h2, mixed, mod, weights, biases, dy, cid, hosts=(), plan=(), next_mod=None
):
    d, c = weights[0].shape
    _, rows, _ = mixed.shape
    ins = dict(h2=h2, mixed=mixed, mod=mod, up_w=weights[0], down_t=weights[1])
    ins.update(up_b=biases[0], down_b=biases[1])
    outs = dict(before=sds((4, 4 * rows, c)), feed=sds(mixed.shape), y=sds(mixed.shape))
    scratch = Narrow.sum_scratch(rows, d)
    cross = next_mod is not None
    if cross:
        ins.update(next_mod=next_mod)
        outs.update(full=sds((2, 4, 2, rows, d)))
        scratch.update(Narrow.gather_scratch(rows, d), **Cross.scratch(rows // 8, d))
    if dy is not None:
        ins.update(dy=dy)
        outs.update(
            full=sds((2, 4, 2, rows, d)), dgate=sds((2, d), F32), dbias=sds((1, d), F32)
        )
        scratch.update(Narrow.gather_scratch(rows, d))

    def body(r):
        net = Narrow(r)
        net.barrier(hosts, cross)
        way = Cross(r)

        def normed(i):
            x = way.received(i)
            v = x.astype(F32).reshape(rows, d)
            r.y[i] = v.astype(BF16)
            v, _ = norm_rows(v)
            m = i // 2
            h = v * (1.0 + r.next_mod[m, 1:2]) + r.next_mod[m, 0:1]
            net.gather_start(i, h.astype(BF16))

        def gated(i):
            v = r.mod[i // 2, 5:6] * r.dy[i].astype(F32)
            add_rows(r.dbias, pl.ds(0, 1), column_sum(v), i == 0)
            net.gather_start(i, v.astype(BF16))

        def tile(i):
            v = kdot(flat(r.h2[i // 2, :, i % 2]), r.up_w[...], NN) + r.up_b[...]
            r.before[i] = v.astype(BF16)
            active = (0.5 * v * (1.0 + gelu_tanh(v))).astype(BF16)
            part = kdot(active, r.down_t[...], NT).astype(BF16)
            r.part[i // 2, :, i % 2] = part.reshape(4, rows, d)
            net.sum_start(i)

        def middle(i):
            m = i // 2
            feed = net.sum_end(i)
            r.feed[i] = feed.astype(BF16)
            full_feed = feed + r.down_b[...]
            y = r.mixed[i] + r.mod[m, 5:6] * full_feed
            if cross:
                way.send(i, y)
            else:
                r.y[i] = y.astype(BF16)
            if dy is not None:
                dgate = column_sum(r.dy[i].astype(F32) * full_feed)
                add_rows(r.dgate, pl.ds(m, 1), dgate, i % 2 == 0)

        stages = [(0, tile), (1, net.sum_cross), (2, middle)]
        if dy is not None:
            stages = [(0, gated)] + stages + [(2, net.gather_forward)]
        if cross:
            stages = stages + [(5, normed), (7, net.gather_forward)]
        pipeline(4, stages, hosts, plan)
        net.sum_drain()
        if dy is not None or cross:
            net.gather_drain()
        if cross:
            way.drain()

    hbm = ("full",) if dy is not None or cross else ()
    return call("feed_forward", body, ins, outs, scratch, cid, hbm, hosts)


def gather_own(name, value_of, ins, more_outs, rows, d, cid, hosts=(), plan=()):
    def body(r):
        net = Narrow(r)
        net.barrier(hosts)
        pipeline(
            4,
            [(0, lambda i: net.gather_start(i, value_of(r, i))), (2, net.gather_forward)],
            hosts,
            plan,
        )
        net.gather_drain()

    outs = dict(full=sds((2, 4, 2, rows, d)), **more_outs)
    return call(name, body, ins, outs, Narrow.gather_scratch(rows, d), cid, ("full",), hosts)


def gather_normed(x_own, mod, cid, hosts=(), plan=()):
    def value(r, i):
        v, _ = norm_rows(r.x[i].astype(F32))
        return (v * (1.0 + r.mod[i // 2, 1:2]) + r.mod[i // 2, 0:1]).astype(BF16)

    _, rows, d = x_own.shape
    ins = dict(x=x_own, mod=mod)
    return gather_own("gather_normed", value, ins, {}, rows, d, cid, hosts, plan)


def add_rows(ref, index, v, first):
    if first:
        ref[index] = v
    else:
        ref[index] += v


def gather_gated(dy, feed, mod, down_b, cid, hosts=(), plan=()):
    def value(r, i):
        m = i // 2
        v = r.dy[i].astype(F32)
        gated = r.mod[m, 5:6] * v
        dgate = column_sum(v * (r.feed[i].astype(F32) + r.down_b[...]))
        add_rows(r.dgate, pl.ds(m, 1), dgate, i % 2 == 0)
        add_rows(r.dbias, pl.ds(0, 1), column_sum(gated), i == 0)
        return gated.astype(BF16)

    _, rows, d = dy.shape
    return gather_own(
        "gather_gated",
        value,
        dict(dy=dy, feed=feed, mod=mod, down_b=down_b),
        dict(dgate=sds((2, d), F32), dbias=sds((1, d), F32)),
        rows,
        d,
        cid,
        hosts,
        plan,
    )


def gather_plain(own, cid):
    _, rows, d = own.shape
    out = gather_own("gather_plain", lambda r, i: r.x[i], dict(x=own), {}, rows, d, cid)
    return out["full"]


def feed_back(
    dfeed, before, h2, mixed, dy, branch, mod, weights, proj_b, cid, hosts=(), plan=()
):
    d, c = weights[0].shape
    _, rows, _ = mixed.shape
    tokens = 4 * rows
    ins = dict(dfeed=dfeed, before=before, h2=h2, mixed=mixed, dy=dy, branch=branch, mod=mod)
    ins.update(up_w=weights[0], down_t=weights[1], proj_b=proj_b)
    outs = dict(
        full=sds((2, 4, 2, rows, d)),
        dmixed=sds(mixed.shape, F32),
        dup=sds((d, c)),
        dup_b=sds((1, c), F32),
        dshift=sds((2, d), F32),
        dscale=sds((2, d), F32),
        dgate=sds((2, d), F32),
        dproj_b=sds((1, d), F32),
    )
    if not any(host.late for host in hosts):
        outs.update(ddown=sds((d, c)))
    strip = c // 3

    def body(r):
        net = Narrow(r)
        net.barrier(hosts)

        def tile(i):
            da = kdot(flat(r.dfeed[i // 2, :, i % 2]), r.down_t[...], NN)
            v = r.before[i].astype(F32)
            t = gelu_tanh(v)
            r.active[i // 2, :, i % 2] = (0.5 * v * (1.0 + t)).astype(BF16).reshape(4, rows, c)
            slope = 0.5 * (1.0 + t) + 0.5 * v * (1.0 - t * t) * (
                GELU_C * (1.0 + 3.0 * GELU_A * v * v)
            )
            db = (da * slope).astype(BF16)
            r.dbefore[i // 2, :, i % 2] = db.reshape(4, rows, c)
            add_rows(r.dup_b, pl.ds(0, 1), column_sum(db.astype(F32)), i == 0)
            part = kdot(db, r.up_w[...], NT).astype(BF16)
            r.part[i // 2, :, i % 2] = part.reshape(4, rows, d)
            net.sum_start(i)

        def middle(i):
            m = i // 2
            dh = net.sum_end(i)
            v, rs = norm_rows(r.mixed[i])
            add_rows(r.dshift, pl.ds(m, 1), column_sum(dh), i % 2 == 0)
            add_rows(r.dscale, pl.ds(m, 1), column_sum(dh * v), i % 2 == 0)
            dmixed = r.dy[i].astype(F32) + norm_back(dh, v, rs, r.mod[m, 4:5])
            r.dmixed[i] = dmixed
            gated = r.mod[m, 2:3] * dmixed
            dgate = column_sum(dmixed * (r.branch[i].astype(F32) + r.proj_b[...]))
            add_rows(r.dgate, pl.ds(m, 1), dgate, i % 2 == 0)
            add_rows(r.dproj_b, pl.ds(0, 1), column_sum(gated), i == 0)
            net.gather_start(i, gated.astype(BF16))

        def strip_of(out, left, right, j):
            cols = pl.ds(j * strip, strip)
            right = right[:, :, :, :, cols].reshape(4 * tokens, strip)
            out[:, cols] = kdot(flat(left[...]), right, TN).astype(BF16)

        def weight_strip(j):
            if j == 0:
                for k in range(3):
                    strip_of(r.ddown, r.dfeed, r.active, k)
            elif j < 4:
                strip_of(r.dup, r.h2, r.dbefore, j - 1)

        def only(stage):
            return lambda i: stage(i) if i < 4 else None

        pipeline(
            5,
            [
                (0, only(tile)),
                (1, only(net.sum_cross)),
                (4, weight_strip),
                (2, only(middle)),
                (4, only(net.gather_forward)),
            ],
            hosts,
            plan,
        )
        net.sum_drain()
        net.gather_drain()

    scratch = dict(Narrow.sum_scratch(rows, d), **Narrow.gather_scratch(rows, d))
    scratch.update(
        dbefore=pltpu.VMEM((2, 4, 2, rows, c), BF16), active=pltpu.VMEM((2, 4, 2, rows, c), BF16)
    )
    if "ddown" not in outs:
        scratch.update(ddown=pltpu.VMEM((d, c), BF16))
    return call("feed_back", body, ins, outs, scratch, cid, ("full",), hosts)


def attention_back(
    dbranch, qkv, att, h1, x_own, dmixed, mod, pack, mask, cid, hosts=(), plan=(), below=None, extra=None
):
    temporal = mask is not None
    d, hc = pack.shape[0], pack.shape[1] // 4
    c = 3 * hc
    heads = hc // HEAD_DIM
    _, rows, _ = x_own.shape
    tokens = 4 * rows
    ins = dict(dbranch=dbranch, qkv=qkv, att=att, h1=h1, x_own=x_own, dmixed=dmixed, mod=mod)
    ins.update(pack=pack)
    if temporal:
        ins.update(mask=mask)
    outs = dict(
        **({} if below else dict(dx=sds(x_own.shape))),
        dpack=sds(pack.shape),
        dqkv_b=sds((1, c), F32),
        dshift=sds((2, d), F32),
        dscale=sds((2, d), F32),
    )

    if below:
        ins.update(feed=below[0], mod_below=below[1], down_b=below[2])
        outs.update(dgate=sds((2, d), F32), dbias=sds((1, d), F32), dy=sds(x_own.shape))
    if extra is not None:
        ins.update(extra=extra)
    if below or extra is not None:
        outs.update(full=sds((2, 4, 2, rows, d)))

    def body(r):
        net = Narrow(r)
        net.barrier(hosts, below is not None)
        way = Cross(r)
        r.proj_t[...] = r.pack[:, c:]

        def gated(i):
            m = i // 2
            v = way.received_back(i).astype(F32).reshape(rows, d)
            r.dy[i] = v.astype(BF16)
            out = r.mod_below[m, 5:6] * v
            dgate = column_sum(v * (r.feed[i].astype(F32) + r.down_b[...]))
            add_rows(r.dgate, pl.ds(m, 1), dgate, i % 2 == 0)
            add_rows(r.dbias, pl.ds(0, 1), column_sum(out), i == 0)
            net.gather_start(i, out.astype(BF16))

        def weight_grads(i):
            source = r.dbranch if temporal else r.dbr
            if i == 0:
                r.dpack[:, c:] = kdot(flat(source[...]), flat(r.att[...]), TN).astype(BF16)
            elif i == 1:
                r.dpack[:, :c] = kdot(flat(r.h1[...]), flat(r.dqkv[...]), TN).astype(BF16)

        def tile(i):
            dbranch = flat(tile_at(r.dbranch, i, temporal)[...])
            if not temporal:
                r.dbr[i] = dbranch
            da = kdot(dbranch, r.proj_t[...], NN).astype(BF16)
            dqkv = attend_back(r.qkv[i], da, r.mask[i // 2] if temporal else None, heads)
            r.dqkv[i] = dqkv
            add_rows(r.dqkv_b, pl.ds(0, 1), column_sum(dqkv.astype(F32)), i == 0)
            part = kdot(dqkv, r.pack[:, :c], NT).astype(BF16)
            target = tile_at(r.part, i, temporal)
            target[...] = part.reshape(target.shape)
            for j in after_tiles(temporal, i):
                net.sum_start(j)

        def middle(i):
            m = i // 2
            dh = net.sum_end(i)
            v, rs = norm_rows(r.x_own[i].astype(F32))
            add_rows(r.dshift, pl.ds(m, 1), column_sum(dh), i % 2 == 0)
            add_rows(r.dscale, pl.ds(m, 1), column_sum(dh * v), i % 2 == 0)
            dx = r.dmixed[i] + norm_back(dh, v, rs, r.mod[m, 1:2])
            if below:
                way.send_back(i, dx)
            else:
                r.dx[i] = dx.astype(BF16)

        late = 1 if temporal else 0
        stages = [(0, tile), (1 + late, net.sum_cross), (4, weight_grads), (2 + late, middle)]
        if extra is not None:
            stages = [(0, lambda i: net.gather_start(i, r.extra[i]))] + stages
            stages += [(2, net.gather_forward)]
        if below:
            stages += [(6, gated), (8, net.gather_forward)]
        pipeline(4, stages, hosts, plan)
        net.sum_drain()
        if below or extra is not None:
            net.gather_drain()
        if below:
            way.drain_back()

    scratch = Narrow.sum_scratch(rows, d)
    scratch.update(dqkv=pltpu.VMEM((4, tokens, c), BF16), proj_t=pltpu.VMEM((d, hc), BF16))
    if not temporal:
        scratch.update(dbr=pltpu.VMEM((4, tokens, d), BF16))
    if below or extra is not None:
        scratch.update(Narrow.gather_scratch(rows, d))
    if below:
        scratch.update(Cross.back_scratch(rows // 8, d))
    hbm = ("full",) if "full" in outs else ()
    return call("attention_back", body, ins, outs, scratch, cid, hbm, hosts)


def start_up(partial, bias, cid, hosts):
    rows, width = partial.shape
    outs = dict(mod=sds((rows, 4 * width), F32))
    scratch = dict(
        terms=pltpu.VMEM((8, rows, width), F32),
        parts=pltpu.VMEM((4, rows, width), F32),
        term_sem=pltpu.SemaphoreType.DMA((2, 8)),
        part_sem=pltpu.SemaphoreType.DMA((2, 4)),
    )

    def body(r):
        w, n = lax.axis_index("wide"), lax.axis_index("narrow")
        sem = pltpu.get_barrier_semaphore()
        for k in range(1, 8):
            pl.semaphore_signal(sem, inc=1, device_id={"wide": lax.rem(w + k, 8)})
        for k in range(1, 4):
            pl.semaphore_signal(sem, inc=1, device_id={"narrow": lax.rem(n + k, 4)})
        pl.semaphore_wait(sem, 10)

        def term(k):
            return pltpu.make_async_remote_copy(
                src_ref=r.partial,
                dst_ref=r.terms.at[k],
                send_sem=r.term_sem.at[0, k],
                recv_sem=r.term_sem.at[1, k],
                device_id={"wide": lax.rem(w + k, 8)},
            )

        def part(k):
            return pltpu.make_async_remote_copy(
                src_ref=r.parts.at[0],
                dst_ref=r.parts.at[k],
                send_sem=r.part_sem.at[0, k],
                recv_sem=r.part_sem.at[1, k],
                device_id={"narrow": lax.rem(n + k, 4)},
            )

        for k in range(1, 8):
            term(k).start()
        for host in hosts:
            host.start()
        total = r.partial[...] + r.bias[...]
        for k in range(1, 8):
            term(k).wait_recv()
            total = total + r.terms[k]
        r.parts[0] = total
        for k in range(1, 4):
            part(k).start()
        phases = all_phases(hosts)
        for phase in phases[:1]:
            phase()
        for k in range(1, 4):
            part(k).wait_recv()
        r.mod[...] = jnp.concatenate(
            [r.parts[lax.rem(n - owner + 4, 4)] for owner in range(4)], axis=1
        )
        for phase in phases[1:]:
            phase()
        for k in range(1, 8):
            term(k).wait_send()
        for k in range(1, 4):
            part(k).wait_send()
        for host in hosts:
            host.drain()

    return call("start_up", body, dict(partial=partial, bias=bias), outs, scratch, cid, (), hosts)


def finish(dx_own, sums, cid, hosts):
    _, rows, d = dx_own.shape
    outs = dict(full=sds((2, 4, 2, rows, d)), total=sds(sums.shape, F32))
    piece = sums.shape[1:]
    scratch = Narrow.gather_scratch(rows, d)
    scratch.update(
        terms=pltpu.VMEM((8,) + piece, F32),
        parts=pltpu.VMEM((4,) + piece, F32),
        mine=pltpu.VMEM(piece, F32),
        term_sem=pltpu.SemaphoreType.DMA((2, 8)),
        part_sem=pltpu.SemaphoreType.DMA((2, 4)),
        back_sem=pltpu.SemaphoreType.DMA((2, 8)),
        keep_sem=pltpu.SemaphoreType.DMA,
    )

    def body(r):
        w, n = lax.axis_index("wide"), lax.axis_index("narrow")
        sem = pltpu.get_barrier_semaphore()
        for k in range(1, 8):
            pl.semaphore_signal(sem, inc=1, device_id={"wide": lax.rem(w + k, 8)})
        for k in range(1, 4):
            pl.semaphore_signal(sem, inc=1, device_id={"narrow": lax.rem(n + k, 4)})
        pl.semaphore_wait(sem, 10)
        net = Narrow(r)

        def wide_copy(src, dst, sems, k):
            return pltpu.make_async_remote_copy(
                src_ref=src,
                dst_ref=dst,
                send_sem=sems.at[0, k],
                recv_sem=sems.at[1, k],
                device_id={"wide": lax.rem(w + k, 8)},
            )

        def term(k):
            return wide_copy(r.sums.at[lax.rem(w + k, 8)], r.terms.at[k], r.term_sem, k)

        def back(k):
            return wide_copy(r.mine, r.total.at[w], r.back_sem, k)

        def part(k):
            return pltpu.make_async_remote_copy(
                src_ref=r.parts.at[0],
                dst_ref=r.parts.at[k],
                send_sem=r.part_sem.at[0, k],
                recv_sem=r.part_sem.at[1, k],
                device_id={"narrow": lax.rem(n + k, 4)},
            )

        for k in range(1, 8):
            term(k).start()
        for host in hosts:
            host.start()
        phases = all_phases(hosts)
        total = r.sums[w]
        for k in range(1, 8):
            term(k).wait_recv()
            total = total + r.terms[k]
        r.parts[0] = total
        for k in range(1, 4):
            part(k).start()
        for i in range(CHUNKS):
            net.gather_start(i, r.dx_own[i])
        for phase in phases[:1]:
            phase()
        everywhere = total
        for k in range(1, 4):
            part(k).wait_recv()
            everywhere = everywhere + r.parts[k]
        r.mine[...] = jnp.where(w == 7, total, everywhere)
        for k in range(1, 8):
            back(k).start()
        keep = pltpu.make_async_copy(r.mine, r.total.at[w], r.keep_sem)
        keep.start()
        net.gather_forward(0)
        net.gather_forward(1)
        for phase in phases[1:2]:
            phase()
        net.gather_forward(2)
        net.gather_forward(3)
        for phase in phases[2:]:
            phase()
        keep.wait()
        for k in range(1, 8):
            term(k).wait_send()
            back(k).wait()
        for k in range(1, 4):
            part(k).wait_send()
        net.gather_drain()
        for host in hosts:
            host.drain()

    ins = dict(dx_own=dx_own, sums=sums)
    return call("finish", body, ins, outs, scratch, cid, ("full",), hosts)


def wide_scatter(grad):
    size = lax.axis_size("wide")
    rows = grad.shape[0] // size
    moved = lax.all_to_all(grad, "wide", split_axis=0, concat_axis=0, tiled=True)
    return jnp.sum(moved.reshape((size, rows) + grad.shape[1:]).astype(F32), axis=0)


def exchange(rows_in, seq_group):
    mb, half, count, d = rows_in.shape
    v = rows_in.reshape(mb, half, seq_group, count // seq_group, d)
    v = group_all_to_all(jnp.moveaxis(v, 2, 0), seq_group)
    return jnp.moveaxis(v, 0, 1).reshape(mb, half, count, d)


def exchange_back(rows_in, seq_group):
    mb, half, count, d = rows_in.shape
    v = rows_in.reshape(mb, seq_group, half, count // seq_group, d)
    v = group_all_to_all(jnp.moveaxis(v, 1, 0), seq_group)
    return jnp.moveaxis(v, 0, 2).reshape(mb, half, count, d)


def group_all_to_all(v, seq_group):
    size = lax.axis_size("wide")
    groups = None
    if seq_group != size:
        groups = [
            list(range(first, first + seq_group)) for first in range(0, size, seq_group)
        ]
    return lax.all_to_all(
        v, "wide", split_axis=0, concat_axis=0, tiled=True, axis_index_groups=groups
    )


def shards(
    tokens,
    conditioning,
    frame_segments,
    cotangent,
    qkv_weight,
    qkv_bias,
    proj_weight,
    proj_bias,
    up_weight,
    up_bias,
    down_weight,
    down_bias,
    ada_weight,
    ada_bias,
):
    mb, half, patches, d = tokens.shape
    parts = lax.axis_size("narrow")
    seq_frames = frame_segments.shape[2]
    seqs = frame_segments.shape[1]
    seq_group = seq_frames // half
    n = lax.axis_index("narrow")
    w = lax.axis_index("wide")
    seq_here = w // seq_group
    blocks = qkv_weight.shape[0]
    rows = patches // parts
    local = qkv_bias.shape[-1]
    shard_rows = ada_weight.shape[1]
    own_shape = (mb, half, rows, d)
    chunk_shape = (mb * half, rows, d)

    hosted = lax.axis_size("wide") == 8 and seqs == 1
    first = [
        jnp.concatenate([qkv_weight[b].reshape(shard_rows, -1), proj_weight[b].T], axis=1)
        for b in range(blocks)
    ]
    packs = {}

    def gather(key, shard):
        if hosted:
            return (WideGather(key, shard),)
        packs[key] = lax.all_gather(shard, "wide", axis=0, tiled=True)
        return ()

    def scatter(key, grad):
        if hosted:
            return (WideScatter(key, grad),)
        grads[key] = wide_scatter(grad)
        return ()

    def take(result):
        for key, value in result.items():
            if key.endswith("all"):
                packs[key[:-3]] = value
            if key.endswith("sum"):
                grads[key[:-3]] = value
        return result

    def scatter_inside(key, source="ddown"):
        shape = sds((shard_rows * lax.axis_size("wide"), up_weight.shape[2]))
        return (WideScatter(key, shape, source),) if hosted else ()

    grads = {}
    qkv_b = jnp.concatenate(
        [qkv_bias[:, 0], jnp.zeros_like(qkv_bias[:, 0]), qkv_bias[:, 1]], axis=1
    ).astype(F32)[:, None]
    proj_b, up_b, down_b = (v.astype(F32)[:, None] for v in (proj_bias, up_bias, down_bias))

    silu = jax.nn.silu(conditioning.astype(F32)).astype(BF16)
    silu_rows = lax.dynamic_slice_in_dim(silu, w * shard_rows, shard_rows, 2)
    partial = jnp.einsum(
        "msr,brck->bmsck", silu_rows, ada_weight, preferred_element_type=F32
    )
    bias = jnp.broadcast_to(ada_bias.astype(F32)[:, None], (blocks, mb, 6, local))
    first0 = gather("a0", first[0])
    if hosted:
        started = take(
            start_up(partial.reshape(-1, local), bias.reshape(-1, local), 13, first0)
        )
        modulation = started["mod"].reshape(blocks, mb, 6, d)
    else:
        total = lax.psum(partial, "wide")
        here = lax.dynamic_index_in_dim(total, seq_here, 2, keepdims=False)
        modulation = lax.all_gather(here + bias, "narrow", axis=3, tiled=True)
    mod0, mod1 = modulation[0], modulation[1]

    frame_ids = lax.dynamic_index_in_dim(frame_segments, seq_here, 1, keepdims=False)
    count = rows // seq_group
    index = jnp.arange(seq_frames * count)
    clip = frame_ids[:, index // count]
    seen = (index[:, None] % count == index[None, :] % count) & (
        clip[:, :, None] == clip[:, None, :]
    )
    mask = jnp.where(seen, 0.0, MASKED).astype(F32)

    def own_of(full):
        return lax.dynamic_slice_in_dim(full, n * rows, rows, 2).reshape(chunk_shape)

    x0 = own_of(tokens)
    up0 = take(
        attention_up(
            tokens.reshape(mb * half, patches, d), x0, mod0, packs["a0"], (qkv_b[0], proj_b[0]),
            None, 0, gather("u0", up_weight[0]) + gather("d0", down_weight[0].T), PLANS["up0"],
        )
    )
    ff0 = take(
        feed_forward(
            up0["full"], up0["mixed"], mod0, (packs["u0"], packs["d0"]), (up_b[0], down_b[0]), None, 1,
            gather("a1", first[1]), PLANS["ff0"],
            mod1 if hosted else None,
        )
    )

    if hosted:
        x1, h1 = ff0["y"], ff0["full"]
    else:
        x1 = exchange(ff0["y"].reshape(own_shape), seq_group).reshape(chunk_shape)
        h1 = gather_normed(x1, mod1, 2)["full"]
    h1 = h1.reshape(4, patches, d)
    dy1 = exchange(own_of(cotangent).reshape(own_shape), seq_group).reshape(chunk_shape)
    up1 = take(
        attention_up(
            h1, x1, mod1, packs["a1"], (qkv_b[1], proj_b[1]), mask, 3,
            gather("u1", up_weight[1]) + gather("d1", down_weight[1].T), PLANS["up1"],
        )
    )
    ff1 = feed_forward(
        up1["full"], up1["mixed"], mod1, (packs["u1"], packs["d1"]), (up_b[1], down_b[1]), dy1, 4
    )
    out_own = exchange_back(ff1["y"].reshape(own_shape), seq_group).reshape(chunk_shape)
    fb1 = take(
        feed_back(
            ff1["full"], ff1["before"], up1["full"], up1["mixed"], dy1, up1["branch"], mod1,
            (packs["u1"], packs["d1"]), proj_b[1], 7, scatter_inside("d1"), PLANS["fb1"],
        )
    )
    if not hosted:
        scatter("d1", fb1["ddown"])
    ab1 = take(
        attention_back(
            fb1["full"], up1["qkv"], up1["att"], h1, x1, fb1["dmixed"], mod1, packs["a1"], mask, 8,
            scatter("u1", fb1["dup"]), PLANS["ab1"],
            (ff0["feed"], mod0, down_b[0]) if hosted else None,
        )
    )
    if hosted:
        dy0, gg0 = ab1["dy"], ab1
    else:
        dy0 = exchange_back(ab1["dx"].reshape(own_shape), seq_group).reshape(chunk_shape)
        gg0 = gather_gated(dy0, ff0["feed"], mod0, down_b[0], 9)
    fb0 = take(
        feed_back(
            gg0["full"], ff0["before"], up0["full"], up0["mixed"], dy0, up0["branch"], mod0,
            (packs["u0"], packs["d0"]), proj_b[0], 10,
            scatter("p1", ab1["dpack"]) + scatter_inside("d0"), PLANS["fb0"],
        )
    )
    if not hosted:
        scatter("d0", fb0["ddown"])
    ab0 = take(
        attention_back(
            fb0["full"], up0["qkv"], up0["att"], up0["h1"], x0, fb0["dmixed"], mod0, packs["a0"],
            None, 11, scatter("u0", fb0["dup"]), PLANS["ab0"], None, out_own,
        )
    )
    layer_out = ab0["full"]

    dmod = jnp.stack(
        [
            jnp.stack(
                [ab["dshift"], ab["dscale"], fb["dgate"], fb["dshift"], fb["dscale"], dgate2],
                axis=1,
            )
            for ab, fb, dgate2 in ((ab0, fb0, gg0["dgate"]), (ab1, fb1, ff1["dgate"]))
        ]
    )
    model_b = jnp.concatenate([fb0["dproj_b"], fb1["dproj_b"], gg0["dbias"], ff1["dbias"]])
    hidden_b = jnp.concatenate(
        [
            jnp.concatenate([ab0["dqkv_b"], fb0["dup_b"]], axis=1),
            jnp.concatenate([ab1["dqkv_b"], fb1["dup_b"]], axis=1),
        ]
    )
    ending = scatter("p0", ab0["dpack"])
    if hosted:
        hidden_rows = jnp.pad(hidden_b.reshape(-1), (0, 4 * d - hidden_b.size)).reshape(4, d)
        sums = jnp.concatenate([dmod.reshape(-1, d), model_b, hidden_rows])
        ended = take(finish(ab0["dx"], sums.reshape(8, -1, d), 12, ending))
        input_grad = ended["full"]
        total = ended["total"].reshape(-1, d)
        count = dmod.size // d
        dmod = total[:count].reshape(blocks, mb, seqs, 6, d)
        model_b = total[count : count + 4].reshape(2, blocks, d)
        hidden_b = total[count + 4 :].reshape(-1)[: hidden_b.size].reshape(hidden_b.shape)
    else:
        input_grad = gather_plain(ab0["dx"], 12)
        slot = (jnp.arange(seqs) == seq_here).astype(F32)
        dmod = dmod[:, :, None] * slot[None, None, :, None, None]
        dmod, model_b = lax.psum((dmod, model_b), ("wide", "narrow"))
        model_b = model_b.reshape(2, blocks, d)
        hidden_b = lax.psum(hidden_b, "wide")
    layer_out = jnp.swapaxes(layer_out, 1, 2).reshape(mb, half, patches, d)
    input_grad = jnp.swapaxes(input_grad, 1, 2).astype(F32).reshape(mb, half, patches, d)
    dmod = lax.dynamic_slice_in_dim(dmod, n * local, local, 4)
    silu_f = silu_rows.astype(F32)
    ada_wgrad = sum(
        silu_f[m, s][None, :, None, None] * dmod[:, m, s][:, None]
        for m in range(mb)
        for s in range(seqs)
    )
    ada_bgrad = jnp.sum(dmod, axis=(1, 2))
    return (
        layer_out,
        input_grad,
        jnp.stack([grads[k][:, : 3 * local] for k in ("p0", "p1")]).reshape(qkv_weight.shape),
        jnp.stack([hidden_b[:, :local], hidden_b[:, 2 * local : 3 * local]], axis=1),
        jnp.stack([grads[k][:, 3 * local :].T for k in ("p0", "p1")]),
        model_b[0],
        jnp.stack([grads[k] for k in ("u0", "u1")]),
        hidden_b[:, 3 * local :],
        jnp.stack([grads[k].T for k in ("d0", "d1")]),
        model_b[1],
        ada_wgrad,
        ada_bgrad,
    )


def solution(mesh):
    return jax.shard_map(
        shards,
        mesh=mesh,
        in_specs=(
            P(None, "wide", None, None),
            P(),
            P(),
            P(None, "wide", None, None),
            P(None, "wide", None, "narrow"),
            P(None, None, "narrow"),
            P(None, "narrow", "wide"),
            P(),
            P(None, "wide", "narrow"),
            P(None, "narrow"),
            P(None, "narrow", "wide"),
            P(),
            P(None, "wide", None, "narrow"),
            P(None, None, "narrow"),
        ),
        out_specs=(
            P(None, "wide", None, None),
            P(None, "wide", None, None),
            P(None, "wide", None, "narrow"),
            P(None, None, "narrow"),
            P(None, "narrow", "wide"),
            P(),
            P(None, "wide", "narrow"),
            P(None, "narrow"),
            P(None, "narrow", "wide"),
            P(),
            P(None, "wide", None, "narrow"),
            P(None, None, "narrow"),
        ),
        check_vma=False,
    )
```

```python
import functools
import types

import jax
import jax.numpy as jnp
from jax import lax
from jax.experimental import pallas as pl
from jax.experimental.pallas import tpu as pltpu
from jax.sharding import PartitionSpec as P

HEAD_DIM = 72
NORM_EPS = 1e-06
WIDE, NARROW = "wide", "narrow"
MASKED = -1e30
BF16 = jnp.bfloat16
F32 = jnp.float32


NN, NT, TN = ((1,), (0,)), ((1,), (1,)), ((0,), (0,))
CHUNKS = 4
GELU_C = 0.7978845608028654
GELU_A = 0.044715
FULL = ("full",)
GROUP = 0
END = 99
PLANS = dict(
    up0=((0, 0, 0), (0, 1, 0), (2, 0, 1), (2, 1, 1), (4, 0, 2), (4, 1, 2)),
    ff0=((1, 0, 0), (2, 1, 0), (4, 0, 1), (5, 1, 1), (6, 0, 2), (7, 1, 2)),
    up1=((1, 0, 0), (2, 1, 0), (3, 0, 1), (4, 1, 1), (5, 0, 2), (5, 1, 2)),
    fb1=((4, 0, 0), (5, 0, 1), (6, 0, 2), (7, 0, 3)),
    ab1=(
        (-1, 0, 0), (-1, 1, 0), (0, 0, 1), (1, 0, 2), (2, 0, 3), (2, 1, 1), (3, 0, 4), (5, 1, 2), (8, 1, 3),
    ),
    fb0=(
        (-1, 0, 0), (1, 0, 1), (3, 0, 2), (4, 1, 0), (5, 0, 3), (6, 0, 4), (7, 1, 1),
    ),
    ab0=(
        (-1, 0, 0), (-1, 1, 0), (0, 0, 1), (1, 0, 2), (2, 0, 3), (2, 1, 1), (3, 0, 4), (3, 1, 2), (5, 1, 3),
        (6, 3, 0), (6, 2, 0), (7, 1, 4), (7, 3, 1), (END, 2, 1), (END, 3, 2), (END, 2, 2),
    ),
)


def kdot(a, b, dims):
    return lax.dot_general(a, b, (dims, ((), ())), preferred_element_type=F32)


def call(name, body, ins, outs, scratch, cid=None, hbm=(), hosts=()):
    ins, outs, scratch, hbm = dict(ins), dict(outs), dict(scratch), set(hbm)
    for host in hosts:
        ins.update(host.ins())
        outs.update(host.outs())
        scratch.update(host.scratch())
        hbm.update(host.hbm())
    names = list(ins) + list(outs) + list(scratch)

    def spec(key):
        return pl.BlockSpec(memory_space=pl.ANY if key in hbm else pltpu.VMEM)

    def kernel(*refs):
        r = types.SimpleNamespace(**dict(zip(names, refs)))
        for host in hosts:
            host.bind(r)
        body(r)

    results = pl.pallas_call(
        kernel,
        in_specs=[spec(key) for key in ins],
        out_specs=[spec(key) for key in outs],
        out_shape=list(outs.values()),
        scratch_shapes=list(scratch.values()),
        compiler_params=pltpu.CompilerParams(
            vmem_limit_bytes=60 << 20,
            collective_id=cid,
            has_side_effects=cid is not None,
        ),
        name=name,
    )(*ins.values())
    return types.SimpleNamespace(**dict(zip(outs, results)))


def pipeline(count, stages, hosts=(), plan=()):
    phases = [host.phases() for host in hosts]
    for step in range(-1, count + max(lag for lag, _ in stages)):
        for lag, stage in stages:
            if step >= 0 and 0 <= step - lag < count:
                stage(step - lag)
        for at, host, phase in plan:
            if at == step and host < len(hosts):
                phases[host][phase]()
    for at, host, phase in plan:
        if at == END and host < len(hosts):
            phases[host][phase]()
    for phase in all_phases(hosts, plan):
        phase()
    for host in hosts:
        host.drain()


def all_phases(hosts, plan=()):
    done = [(host, phase) for _, host, phase in plan]
    left = [
        (k if host.in_turn else 0, h, k, phase)
        for h, host in enumerate(hosts)
        for k, phase in enumerate(host.phases())
        if (h, k) not in done
    ]
    return [item[3] for item in sorted(left, key=lambda item: item[:3])]


def wide_pair(w):
    return w + 1 - 2 * lax.rem(w, 2)


class Host:
    in_turn = True

    def bind(self, refs):
        w = lax.axis_index(WIDE)
        self.x, self.z = lax.rem(w, 2), lax.div(w, 2)
        self.pair, self.up = wide_pair(w), lax.rem(w + 2, 8)
        self.r = refs
        size = len(self.tag)
        self.own_refs = types.SimpleNamespace(
            **{key[size:]: ref for key, ref in vars(refs).items() if key[:size] == self.tag}
        )


    def block(self, z, x):
        return pl.ds(pl.multiple_of((z * 2 + x) * self.rows, self.rows), self.rows)

    def remote(self, src, dst, sems, k, other):
        return pltpu.make_async_remote_copy(
            src_ref=src,
            dst_ref=dst,
            send_sem=sems.at[0, k],
            recv_sem=sems.at[1, k],
            device_id={WIDE: other},
        )


def column_parts(cols):
    cut = (cols // 128 + 1) // 2 * 128
    return (pl.ds(0, cut), pl.ds(cut, cols - cut))


class WideGather(Host):
    def __init__(self, tag, shard, block=None, low=0, cols=None, vmem=False, turn=True):
        self.tag, self.shard, self.index, self.low, self.vmem = tag, shard, block, low, vmem
        self.rows, self.cols = shard.shape[-2], cols or shard.shape[-1]
        turned = 128 if turn and self.cols >= 1024 else 0
        self.parts = column_parts(self.cols - turned)
        self.turned = pl.ds(self.cols - turned, turned) if turned else None

    def ins(self):
        return {self.tag + "shard": self.shard}

    def outs(self):
        return {self.tag + "all": sds((8 * self.rows, self.cols))}

    def scratch(self):
        return {
            self.tag + "zsem": pltpu.SemaphoreType.DMA((2, 12)),
            self.tag + "xsem": pltpu.SemaphoreType.DMA((2, 9)),
            self.tag + "sem": pltpu.SemaphoreType.DMA,
        }

    def hbm(self):
        return [] if self.vmem else [self.tag + "all"]

    def own(self, cols):
        cols = pl.ds(self.low + cols.start, cols.size)
        shard = self.own_refs.shard
        return shard.at[:, cols] if self.index is None else shard.at[self.index, :, cols]

    def rows_of(self, k, part):
        here = self.block(lax.rem(self.z - k + 4, 4), self.x)
        place = self.own_refs.all.at[here, self.parts[part]]
        return (self.own(self.parts[part]) if k == 0 else place), place

    def z_copy(self, k, part):
        return self.remote(*self.rows_of(k, part), self.own_refs.zsem, 2 * k + part, self.up)

    def x_copy(self, k, part):
        return self.remote(*self.rows_of(k, part), self.own_refs.xsem, 2 * k + part, self.pair)

    def turned_rows(self, k, x):
        here = self.block(lax.rem(self.z - k + 4, 4), lax.rem(self.x + x, 2))
        place = self.own_refs.all.at[here, self.turned]
        return (self.own(self.turned) if k == 0 and x == 0 else place), place

    def turned_x(self):
        return self.remote(*self.turned_rows(0, 0), self.own_refs.xsem, 8, self.pair)

    def turned_z(self, k, x):
        return self.remote(*self.turned_rows(k, x), self.own_refs.zsem, 6 + 2 * k + x, self.up)

    def local_copy(self):
        here = self.block(self.z, self.x)
        return pltpu.make_async_copy(
            self.own(pl.ds(0, self.cols)), self.own_refs.all.at[here], self.own_refs.sem
        )

    def start(self):
        if self.turned:
            self.turned_x().start()
            self.turned_z(0, 0).start()
        for part in range(2):
            self.z_copy(0, part).start()
            self.x_copy(0, part).start()
        self.local_copy().start()

    def phases(self):
        def step(k):
            for part in range(2):
                self.z_copy(k - 1, part).wait_recv()
                if k < 3:
                    self.z_copy(k, part).start()
                self.x_copy(k, part).start()
            if self.turned:
                self.turned_z(k - 1, 0).wait_recv()
                if k < 3:
                    self.turned_z(k, 0).start()
                if k == 1:
                    self.turned_x().wait_recv()
                else:
                    self.turned_z(k - 2, 1).wait_recv()
                self.turned_z(k - 1, 1).start()

        return [lambda k=k: step(k) for k in (1, 2, 3)]

    def drain(self):
        self.local_copy().wait()
        if self.turned:
            self.turned_z(2, 1).wait_recv()
            self.turned_x().wait_send()
            for k in range(3):
                for x in range(2):
                    self.turned_z(k, x).wait_send()
        for k in range(4):
            for part in range(2):
                self.x_copy(k, part).wait()
                if k < 3:
                    self.z_copy(k, part).wait_send()


class WideScatter(Host):
    in_turn = False

    def __init__(self, tag, grad, source=None, low=0, cols=None, depth=2):
        self.tag, self.grad, self.source, self.low = tag, grad, source, low
        self.late, self.depth = source is not None, depth
        self.rows, self.cols = grad.shape[0] // 8, cols or grad.shape[1]
        self.parts = column_parts(self.cols)

    def ins(self):
        return {} if self.late else {self.tag + "grad": self.grad}

    def outs(self):
        return {self.tag + "sum": sds((self.rows, self.cols), F32)}

    def scratch(self):
        size = (self.rows, self.cols)
        return {
            self.tag + "got": pltpu.VMEM((4,) + size, BF16),
            self.tag + "send": pltpu.VMEM((3,) + size, BF16),
            self.tag + "ring": pltpu.VMEM((3,) + size, BF16),
            self.tag + "xsem": pltpu.SemaphoreType.DMA((2, 8)),
            self.tag + "zsem": pltpu.SemaphoreType.DMA((2, 6)),
        }

    def hbm(self):
        return []

    def rows_of(self, s, x, part):
        grad = getattr(self.r, self.source) if self.late else self.own_refs.grad
        cols = pl.ds(self.low + self.parts[part].start, self.parts[part].size)
        return grad.at[self.block(lax.rem(self.z - s + 7, 4), x), cols]

    def x_copy(self, s, part):
        return self.remote(
            self.rows_of(s, 1 - self.x, part),
            self.own_refs.got.at[s, :, self.parts[part]],
            self.own_refs.xsem,
            2 * s + part,
            self.pair,
        )

    def z_copy(self, s, part):
        cols = self.parts[part]
        return self.remote(
            self.own_refs.send.at[s, :, cols],
            self.own_refs.ring.at[s, :, cols],
            self.own_refs.zsem,
            2 * s + part,
            self.up,
        )

    def start(self):
        pass

    def begin(self):
        for s in range(self.depth):
            for part in range(2):
                self.x_copy(s, part).start()

    def phases(self):
        def step(s):
            for part in range(2):
                cols = self.parts[part]
                self.x_copy(s, part).wait_recv()
                if s + self.depth < 4:
                    self.x_copy(s + self.depth, part).start()
                total = self.rows_of(s, self.x, part)[...].astype(F32)
                total = total + self.own_refs.got[s, :, cols].astype(F32)
                if s:
                    self.z_copy(s - 1, part).wait_recv()
                    total = total + self.own_refs.ring[s - 1, :, cols].astype(F32)
                if s < 3:
                    self.own_refs.send[s, :, cols] = total.astype(BF16)
                    self.z_copy(s, part).start()
                else:
                    self.own_refs.sum[:, cols] = total

        return [self.begin] + [lambda s=s: step(s) for s in range(4)]

    def drain(self):
        for s in range(4):
            for part in range(2):
                self.x_copy(s, part).wait_send()
                if s < 3:
                    self.z_copy(s, part).wait_send()


class Narrow:
    def __init__(self, refs, frames=False):
        n = lax.axis_index(NARROW)
        self.frames = frames
        self.n, self.core, self.across, self.far = (
            n,
            n + 1 - 2 * lax.rem(n, 2),
            lax.rem(n + 2, 4),
            3 - n,
        )
        self.r = refs

    def barrier(self, hosts=(), cross=False, everyone=False):
        sem = pltpu.get_barrier_semaphore()
        for other in (self.core, self.across) + ((self.far,) if everyone else ()):
            pl.semaphore_signal(sem, inc=1, device_id={NARROW: other})
        if cross or everyone:
            w = lax.axis_index(WIDE)
            for k in range(1, 8):
                pl.semaphore_signal(sem, inc=1, device_id={WIDE: lax.rem(w + k, 8)})
        elif hosts:
            w = lax.axis_index(WIDE)
            for other in (wide_pair(w), lax.rem(w + 6, 8)):
                pl.semaphore_signal(sem, inc=1, device_id={WIDE: other})
        count = 10 if everyone else 9 if cross else 4 if hosts else 2
        pl.semaphore_wait(sem, count)
        for host in hosts:
            host.start()

    def remote(self, src, dst, sems, index, other):
        return pltpu.make_async_remote_copy(
            src_ref=src,
            dst_ref=dst,
            send_sem=sems.at[(0,) + index],
            recv_sem=sems.at[(1,) + index],
            device_id={NARROW: other},
        )

    def sum_scratch(rows, d):
        return dict(
            part=pltpu.VMEM((CHUNKS // 2, 4, 2, rows, d), BF16),
            near=pltpu.VMEM((CHUNKS, 2, rows, d), BF16),
            pair=pltpu.VMEM((CHUNKS, rows, d), BF16),
            cross=pltpu.VMEM((CHUNKS, rows, d), BF16),
            near_sem=pltpu.SemaphoreType.DMA((2, CHUNKS, 2)),
            cross_sem=pltpu.SemaphoreType.DMA((2, CHUNKS)),
        )

    def near_copy(self, i, which):
        owner = self.core if which == 0 else self.far
        return self.remote(
            self.r.part.at[i // 2, owner, i % 2],
            self.r.near.at[i, which],
            self.r.near_sem,
            (i, which),
            self.core,
        )

    def cross_copy(self, i):
        return self.remote(
            self.r.pair.at[i], self.r.cross.at[i], self.r.cross_sem, (i,), self.across
        )

    def sum_far(self, i):
        self.near_copy(i, 1).start()

    def sum_near(self, i):
        self.near_copy(i, 0).start()

    def sum_start(self, i):
        self.sum_far(i)
        self.sum_near(i)

    def sum_cross(self, i):
        self.near_copy(i, 1).wait_recv()
        mine = self.r.part[i // 2, self.across, i % 2].astype(F32)
        self.r.pair[i] = (mine + self.r.near[i, 1].astype(F32)).astype(BF16)
        self.cross_copy(i).start()

    def sum_end(self, i):
        self.near_copy(i, 0).wait_recv()
        total = self.r.part[i // 2, self.n, i % 2].astype(F32) + self.r.near[i, 0].astype(F32)
        self.cross_copy(i).wait_recv()
        return total + self.r.cross[i].astype(F32)

    def sum_drain(self):
        for i in range(CHUNKS):
            self.near_copy(i, 0).wait_send()
            self.near_copy(i, 1).wait_send()
            self.cross_copy(i).wait_send()

    def gather_scratch(rows, d):
        return dict(
            own=pltpu.VMEM((CHUNKS, rows, d), BF16),
            own_sem=pltpu.SemaphoreType.DMA((CHUNKS,)),
            out_sem=pltpu.SemaphoreType.DMA((2, CHUNKS, 3)),
        )

    def place(self, i, n):
        if self.frames:
            return self.r.full.at[i // 2, i % 2, n]
        return self.r.full.at[i // 2, n, i % 2]

    def out_copy(self, i, which):
        if which == 2:
            rows = self.place(i, self.across)
            return self.remote(rows, rows, self.r.out_sem, (i, 2), self.core)
        other = self.across if which == 0 else self.core
        return self.remote(
            self.r.own.at[i], self.place(i, self.n), self.r.out_sem, (i, which), other
        )

    def own_copy(self, i):
        return pltpu.make_async_copy(
            self.r.own.at[i], self.place(i, self.n), self.r.own_sem.at[i]
        )

    def gather_start(self, i, value):
        self.r.own[i] = value
        self.out_copy(i, 0).start()
        self.out_copy(i, 1).start()
        self.own_copy(i).start()

    def gather_forward(self, i):
        self.out_copy(i, 0).wait_recv()
        self.out_copy(i, 2).start()

    def gather_drain(self):
        for i in range(CHUNKS):
            self.own_copy(i).wait()
            for which in range(3):
                self.out_copy(i, which).wait_send()
                if which:
                    self.out_copy(i, which).wait_recv()


def second_gather(r):
    refs = types.SimpleNamespace(full=r.full2, own=r.own2, own_sem=r.own_sem2, out_sem=r.out_sem2)
    return Narrow(refs, frames=True)


def second_scratch(rows, d):
    return {key + "2": value for key, value in Narrow.gather_scratch(rows, d).items()}


class Cross:
    def __init__(self, refs):
        self.r, self.w = refs, lax.axis_index(WIDE)

    def scratch(count, d):
        return dict(
            cross_out=pltpu.VMEM((2, 2, 8, count, d), BF16),
            cross_in=pltpu.VMEM((2, 8, 2, count, d), BF16),
            cross_sems=pltpu.SemaphoreType.DMA((2, CHUNKS, 8)),
        )

    def back_scratch(count, d):
        return dict(
            cross_out=pltpu.VMEM((2, 8, 2, count, d), BF16),
            cross_in=pltpu.VMEM((2, 2, 8, count, d), BF16),
            cross_sems=pltpu.SemaphoreType.DMA((2, CHUNKS, 8)),
        )

    def copy(self, src, dst, i, k):
        return pltpu.make_async_remote_copy(
            src_ref=src,
            dst_ref=dst,
            send_sem=self.r.cross_sems.at[0, i, k],
            recv_sem=self.r.cross_sems.at[1, i, k],
            device_id={WIDE: lax.rem(self.w + k, 8)},
        )

    def to_patches(self, i, k):
        m, f, other = i // 2, i % 2, lax.rem(self.w + k, 8)
        return self.copy(
            self.r.cross_out.at[m, f, other], self.r.cross_in.at[m, self.w, f], i, k
        )

    def send(self, i, value):
        m, f = i // 2, i % 2
        out = self.r.cross_out
        out[m, f] = value.reshape(out.shape[2:]).astype(BF16)
        for k in range(1, 8):
            self.to_patches(i, k).start()
        self.r.cross_in[m, self.w, f] = out[m, f, self.w]

    def received(self, c):
        m, h = c // 2, c % 2
        if h == 0:
            for i in (2 * m, 2 * m + 1):
                for k in range(1, 8):
                    self.to_patches(i, k).wait_recv()
        return self.r.cross_in[m, 4 * h : 4 * h + 4]

    def to_frames(self, m, k):
        other = lax.rem(self.w + k, 8)
        return self.copy(
            self.r.cross_out.at[m, other], self.r.cross_in.at[m, :, self.w], m, k
        )

    def send_back(self, c, value):
        m, h = c // 2, c % 2
        out = self.r.cross_out
        out[m, 4 * h : 4 * h + 4] = value.reshape((4,) + out.shape[2:]).astype(BF16)
        if h:
            for k in range(1, 8):
                self.to_frames(m, k).start()
            self.r.cross_in[m, :, self.w] = out[m, self.w]

    def received_back(self, i):
        m, f = i // 2, i % 2
        if f == 0:
            for k in range(1, 8):
                self.to_frames(m, k).wait_recv()
        return self.r.cross_in[m, f]

    def drain(self):
        for i in range(CHUNKS):
            for k in range(1, 8):
                self.to_patches(i, k).wait_send()

    def drain_back(self):
        for m in range(2):
            for k in range(1, 8):
                self.to_frames(m, k).wait_send()


def norm_rows(v):
    centred = v - jnp.mean(v, axis=-1, keepdims=True)
    r = lax.rsqrt(jnp.mean(centred * centred, axis=-1, keepdims=True) + NORM_EPS)
    return centred * r, r


def norm_back(grad, n, r, scale):
    dn = grad * (1.0 + scale)
    return r * (
        dn
        - jnp.mean(dn, axis=-1, keepdims=True)
        - n * jnp.mean(dn * n, axis=-1, keepdims=True)
    )


def column_sum(v):
    return jnp.sum(v, axis=0, keepdims=True)


def sds(shape, dtype=BF16):
    return jax.ShapeDtypeStruct(shape, dtype)


def softmax_of(s, mask):
    s = s * HEAD_DIM ** (-0.5)
    if mask is not None:
        s = s + mask
    p = jnp.exp(s - jnp.max(s, axis=-1, keepdims=True))
    return p * (1.0 / jnp.sum(p, axis=-1, keepdims=True))


def head_parts(v, heads, offset, size):
    return [
        v[t : t + size, offset + h * HEAD_DIM : offset + (h + 1) * HEAD_DIM]
        for t in range(0, v.shape[0], size)
        for h in range(heads)
    ]


def join_heads(pieces, heads):
    rows = [
        jnp.concatenate(pieces[t : t + heads], axis=1) for t in range(0, len(pieces), heads)
    ]
    return rows[0] if len(rows) == 1 else jnp.concatenate(rows, axis=0)


def attend(qkv, mask, heads):
    size = qkv.shape[0] if mask is None else mask.shape[0]
    width = heads * HEAD_DIM
    q, k, v = (head_parts(qkv, heads, j * width, size) for j in range(3))
    scores = [kdot(a, b, NT) for a, b in zip(q, k)]
    probs = [softmax_of(s, mask).astype(BF16) for s in scores]
    return join_heads([kdot(p, b, NN).astype(BF16) for p, b in zip(probs, v)], heads)


def attend_back(qkv, grad, mask, heads):
    size = qkv.shape[0] if mask is None else mask.shape[0]
    width = heads * HEAD_DIM
    q, k, v = (head_parts(qkv, heads, j * width, size) for j in range(3))
    g = head_parts(grad, heads, 0, size)
    group = GROUP or len(q)
    dq, dk, dv = [], [], []
    for low in range(0, len(q), group):
        part = slice(low, low + group)
        scores = [kdot(a, b, NT) for a, b in zip(q[part], k[part])]
        dps = [kdot(a, b, NT) for a, b in zip(g[part], v[part])]
        probs = [softmax_of(s, mask) for s in scores]
        dv += [kdot(p.astype(BF16), a, TN).astype(BF16) for p, a in zip(probs, g[part])]
        ds = [
            (p * (dp - jnp.sum(p * dp, axis=-1, keepdims=True)) * HEAD_DIM ** (-0.5)).astype(BF16)
            for p, dp in zip(probs, dps)
        ]
        dq += [kdot(a, b, NN).astype(BF16) for a, b in zip(ds, k[part])]
        dk += [kdot(a, b, TN).astype(BF16) for a, b in zip(ds, q[part])]
    return jnp.concatenate([join_heads(m, heads) for m in (dq, dk, dv)], axis=1)


def gelu_tanh(v):
    return jnp.tanh(GELU_C * (v + GELU_A * v * v * v))


def tile_at(ref, i, temporal):
    if temporal:
        return ref.at[lax.div(i, 2), pl.ds(lax.rem(i, 2) * 2, 2)]
    return ref.at[i // 2, :, i % 2]


def tile_order(net, i, temporal):
    if not temporal:
        return i
    across = lax.div(net.n, 2)
    return i // 2 * 2 + (across if i % 2 else 1 - across)


def send_tile(net, i, temporal):
    if not temporal:
        net.sum_start(i)
        return
    for j in (i // 2 * 2, i // 2 * 2 + 1):
        if i % 2:
            net.sum_near(j)
        else:
            net.sum_far(j)


def cross_stages(net, temporal):
    if not temporal:
        return [], [(1, net.sum_cross)]

    def both(i):
        if i % 2:
            net.sum_cross(i - 1)
            net.sum_cross(i)

    return [(0, both)], []


def flat(v):
    return v.reshape(-1, v.shape[-1])


def row_of(ref, b):
    return ref[...].astype(F32)[b : b + 1]


def fill_bias(out, qkv_b, hc):
    out[...] = jnp.zeros_like(out)
    rows = qkv_b.astype(F32)
    out[:, :hc] = rows[0:1]
    out[:, 2 * hc :] = rows[1:2]


def fill_mask(out, r):
    for m in range(2):
        out[m] = jnp.where(r.key_rows[m] == r.key_columns[m], 0.0, MASKED)


class Modulation:
    def __init__(self, partial, bias):
        self.partial, self.bias = partial, bias

    def ins(self):
        return dict(partial=self.partial, ada_b=self.bias)

    def scratch(self):
        _, rows, width = self.partial.shape
        return dict(
            terms=pltpu.VMEM((8, rows, width), F32),
            mine=pltpu.VMEM((rows, width), F32),
            every=pltpu.VMEM((8, rows, width), F32),
            parts=pltpu.VMEM((4, 8, rows, width), F32),
            term_sem=pltpu.SemaphoreType.DMA((2, 8)),
            back_sem=pltpu.SemaphoreType.DMA((2, 8)),
            part_sem=pltpu.SemaphoreType.DMA((2, 4)),
        )

    def bind(self, r):
        self.r, self.w, self.n = r, lax.axis_index(WIDE), lax.axis_index(NARROW)

    def wide_copy(self, src, dst, sems, k):
        return pltpu.make_async_remote_copy(
            src_ref=src,
            dst_ref=dst,
            send_sem=sems.at[0, k],
            recv_sem=sems.at[1, k],
            device_id={WIDE: lax.rem(self.w + k, 8)},
        )

    def term(self, k):
        r = self.r
        return self.wide_copy(
            r.partial.at[lax.rem(self.w + k, 8)], r.terms.at[k], r.term_sem, k
        )

    def back(self, k):
        return self.wide_copy(self.r.mine, self.r.every.at[self.w], self.r.back_sem, k)

    def part(self, k):
        r = self.r
        return pltpu.make_async_remote_copy(
            src_ref=r.every,
            dst_ref=r.parts.at[k],
            send_sem=r.part_sem.at[0, k],
            recv_sem=r.part_sem.at[1, k],
            device_id={NARROW: lax.rem(self.n + k, 4)},
        )

    def start(self):
        for k in range(1, 8):
            self.term(k).start()

    def sum(self):
        r, w = self.r, self.w
        total = r.partial[w] + r.ada_b[lax.div(w, 4), lax.rem(w, 2)]
        for k in range(1, 8):
            self.term(k).wait_recv()
            total = total + r.terms[k]
        r.mine[...] = total
        for k in range(1, 8):
            self.back(k).start()
        r.every[w] = total

    def spread(self):
        for k in range(1, 8):
            self.back(k).wait_recv()
        for k in range(1, 4):
            self.part(k).start()
        self.r.parts[0] = self.r.every[...]

    def store(self, out):
        for k in range(1, 4):
            self.part(k).wait_recv()
        for piece in range(8):
            low = piece % 2 * 3
            out[piece // 4, piece // 2 % 2, low : low + 3] = jnp.concatenate(
                [self.r.parts[lax.rem(self.n - owner + 4, 4), piece] for owner in range(4)], axis=1
            )

    def drain(self):
        for k in range(1, 8):
            self.term(k).wait_send()
            self.back(k).wait_send()
        for k in range(1, 4):
            self.part(k).wait_send()


def attention_up(
    x_or_h, x_own, mod, pack, biases, b, keys, cid, hosts=(), plan=(), first=None, modulation=None
):
    temporal = keys is not None
    starting = first is not None
    d = x_or_h.shape[-1]
    hc = biases[0].shape[-1]
    c = 3 * hc
    heads = hc // HEAD_DIM
    tokens = x_or_h.shape[1]
    rows = tokens // 4
    own = (4, rows, d)
    ins = dict(src=x_or_h, qkv_b=biases[0], proj_b=biases[1])
    if temporal:
        ins.update(key_rows=keys[0], key_columns=keys[1], x_own=x_own)
    if starting:
        ins.update(modulation.ins())
    else:
        ins.update(mod=mod, pack=pack)
    outs = dict(
        qkv=sds((4, tokens, c)),
        att=sds((4, tokens, hc)),
        branch=sds(own),
        mixed=sds(own, F32),
        full=sds((2, 4, 2, rows, d)),
    )
    if not temporal:
        outs.update(h1=sds((4, tokens, d)), x_own=sds(own))
    if starting:
        outs.update(mod=sds((2, 2, 6, d), F32))

    def body(r):
        net = Narrow(r)
        fill_bias(r.qb, r.qkv_b[b], hc)
        if temporal:
            fill_mask(r.mask, r)

        def prepare(i):
            v, _ = norm_rows(r.src[i].astype(F32))
            r.h1[i] = (v * (1.0 + r.mod[b, i // 2, 1:2]) + r.mod[b, i // 2, 0:1]).astype(BF16)
            r.x_own[i] = r.src[i, pl.ds(pl.multiple_of(net.n * rows, rows), rows)]

        if starting:
            net.barrier(everyone=True)
            modulation.bind(r)
            modulation.start()
            for host in (first,) + tuple(hosts):
                host.start()
            steps = first.phases()
            modulation.sum()
            steps[0]()
            modulation.spread()
            steps[1]()
            modulation.store(r.mod)
            for i in range(2):
                prepare(i)
            steps[2]()
            for i in range(2, 4):
                prepare(i)
            first.drain()
            weights = first.own_refs.all
        else:
            net.barrier(hosts)
            weights = r.pack
        r.proj_t[...] = weights[:, c:]

        def tile(i):
            t = tile_order(net, i, temporal)
            if temporal:
                h = r.src[t]
            else:
                if not starting:
                    prepare(i)
                h = r.h1[i]
            qkv = (kdot(h, weights[:, :c], NN) + r.qb[...]).astype(BF16)
            r.qkv[t] = qkv
            att = attend(qkv, r.mask[i // 2] if temporal else None, heads)
            r.att[t] = att
            part = kdot(att, r.proj_t[...], NT).astype(BF16)
            target = tile_at(r.part, t, temporal)
            target[...] = part.reshape(target.shape)
            send_tile(net, i, temporal)

        def middle(i):
            m = i // 2
            branch = net.sum_end(i)
            r.branch[i] = branch.astype(BF16)
            mixed = r.x_own[i].astype(F32) + r.mod[b, m, 2:3] * (branch + row_of(r.proj_b, b))
            r.mixed[i] = mixed
            v, _ = norm_rows(mixed)
            net.gather_start(i, (v * (1.0 + r.mod[b, m, 4:5]) + r.mod[b, m, 3:4]).astype(BF16))

        before, after = cross_stages(net, temporal)
        pipeline(
            4,
            before + [(0, tile)] + after + [(2, middle), (3, net.gather_forward)],
            hosts,
            plan,
        )
        net.sum_drain()
        net.gather_drain()
        if starting:
            modulation.drain()

    scratch = dict(Narrow.sum_scratch(rows, d), **Narrow.gather_scratch(rows, d))
    scratch.update(proj_t=pltpu.VMEM((d, hc), BF16), qb=pltpu.VMEM((1, c), F32))
    if temporal:
        scratch.update(mask=pltpu.VMEM((2, tokens // 2, tokens // 2), F32))
    if starting:
        scratch.update(modulation.scratch())
    carried = ((first,) if starting else ()) + tuple(hosts)
    return call("attention_up", body, ins, outs, scratch, cid, FULL, carried)


def up_pieces(pieces):
    return {f"up{k}": piece for k, piece in enumerate(pieces)}


def up_refs(r):
    low = 0
    for key in ("up0", "up1"):
        if hasattr(r, key):
            ref = getattr(r, key)
            yield low, ref
            low += ref.shape[1]


def times_up(r, h):
    parts = [kdot(h, ref[...], NN) for _, ref in up_refs(r)]
    return parts[0] if len(parts) == 1 else jnp.concatenate(parts, axis=1)


def feed_forward(
    h2, mixed, mod, weights, biases, dy, b, cid, hosts=(), plan=(), cross=False, cross_dy=False
):
    d, c = weights[1].shape
    _, rows, _ = mixed.shape
    ins = dict(h2=h2, mixed=mixed, mod=mod, down_t=weights[1], **up_pieces(weights[0]))
    ins.update(up_b=biases[0], down_b=biases[1])
    outs = dict(before=sds((4, 4 * rows, c)), feed=sds(mixed.shape), y=sds(mixed.shape))
    scratch = Narrow.sum_scratch(rows, d)
    if cross:
        outs.update(full=sds((2, 4, 2, rows, d)))
        scratch.update(Narrow.gather_scratch(rows, d), **Cross.scratch(rows // 8, d))
    if dy is not None:
        ins.update(dy=dy)
        outs.update(
            full=sds((2, 4, 2, rows, d)), dgate=sds((2, d), F32), dbias=sds((1, d), F32)
        )
        scratch.update(Narrow.gather_scratch(rows, d))
        if cross_dy:
            outs.update(dy_here=sds(mixed.shape))
            scratch.update(Cross.scratch(rows // 8, d))
            scratch.update(
                cot=pltpu.VMEM(mixed.shape, BF16), cot_sem=pltpu.SemaphoreType.DMA((CHUNKS,))
            )

    def body(r):
        net = Narrow(r)
        net.barrier(hosts, cross or cross_dy)
        way = Cross(r)

        def own_cot(i):
            here = pl.ds(pl.multiple_of(net.n * rows, rows), rows)
            return pltpu.make_async_copy(r.dy.at[i, here], r.cot.at[i], r.cot_sem.at[i])

        def leave(i):
            own_cot(i).wait()
            way.send(i, r.cot[i].astype(F32))

        if cross_dy:
            for i in range(CHUNKS):
                own_cot(i).start()

        def normed(i):
            x = way.received(i)
            v = x.astype(F32).reshape(rows, d)
            r.y[i] = v.astype(BF16)
            v, _ = norm_rows(v)
            m = i // 2
            h = v * (1.0 + r.mod[b + 1, m, 1:2]) + r.mod[b + 1, m, 0:1]
            net.gather_start(i, h.astype(BF16))

        def gated(i):
            m = i // 2
            if cross_dy:
                v = way.received(i).astype(F32).reshape(rows, d)
                r.dy_here[i] = v.astype(BF16)
            else:
                v = r.dy[i].astype(F32)
            dgate = column_sum(v * (r.feed[i].astype(F32) + row_of(r.down_b, b)))
            add_rows(r.dgate, pl.ds(m, 1), dgate, i % 2 == 0)
            v = r.mod[b, m, 5:6] * v
            add_rows(r.dbias, pl.ds(0, 1), column_sum(v), i == 0)
            net.gather_start(i, v.astype(BF16))

        def tile(i):
            v = times_up(r, flat(r.h2[i // 2, :, i % 2])) + row_of(r.up_b, b)
            r.before[i] = v.astype(BF16)
            active = (0.5 * v * (1.0 + gelu_tanh(v))).astype(BF16)
            part = kdot(active, r.down_t[...], NT).astype(BF16)
            r.part[i // 2, :, i % 2] = part.reshape(4, rows, d)
            net.sum_start(i)

        def middle(i):
            m = i // 2
            feed = net.sum_end(i)
            r.feed[i] = feed.astype(BF16)
            full_feed = feed + row_of(r.down_b, b)
            y = r.mixed[i] + r.mod[b, m, 5:6] * full_feed
            if cross:
                way.send(i, y)
            else:
                r.y[i] = y.astype(BF16)

        stages = [(0, tile), (1, net.sum_cross), (2, middle)]
        if dy is not None:
            stages = stages + [(2, gated), (4, net.gather_forward)]
            if cross_dy:
                stages = [(0, leave)] + stages
        if cross:
            stages = stages + [(5, normed), (7, net.gather_forward)]
        pipeline(4, stages, hosts, plan)
        net.sum_drain()
        if dy is not None or cross:
            net.gather_drain()
        if cross or cross_dy:
            way.drain()

    hbm = (FULL if dy is not None or cross else ()) + (("dy",) if cross_dy else ())
    return call("feed_forward", body, ins, outs, scratch, cid, hbm, hosts)


def gather_own(
    name, value_of, ins, more_outs, rows, d, cid, hosts=(), plan=(), frames=False
):
    def body(r):
        net = Narrow(r, frames)
        net.barrier(hosts)
        pipeline(
            4,
            [(0, lambda i: net.gather_start(i, value_of(r, i))), (2, net.gather_forward)],
            hosts,
            plan,
        )
        net.gather_drain()

    shape = (2, 2, 4, rows, d) if frames else (2, 4, 2, rows, d)
    outs = dict(full=sds(shape), **more_outs)
    return call(name, body, ins, outs, Narrow.gather_scratch(rows, d), cid, FULL, hosts)


def gather_normed(x_own, mod, b, cid, hosts=(), plan=()):
    def value(r, i):
        v, _ = norm_rows(r.x[i].astype(F32))
        return (v * (1.0 + r.mod[b, i // 2, 1:2]) + r.mod[b, i // 2, 0:1]).astype(BF16)

    _, rows, d = x_own.shape
    ins = dict(x=x_own, mod=mod)
    return gather_own("gather_normed", value, ins, {}, rows, d, cid, hosts, plan)


def add_rows(ref, index, v, first):
    if first:
        ref[index] = v
    else:
        ref[index] += v


def gather_gated(dy, feed, mod, down_b, b, cid, hosts=(), plan=()):
    def value(r, i):
        m = i // 2
        v = r.dy[i].astype(F32)
        gated = r.mod[b, m, 5:6] * v
        dgate = column_sum(v * (r.feed[i].astype(F32) + row_of(r.down_b, b)))
        add_rows(r.dgate, pl.ds(m, 1), dgate, i % 2 == 0)
        add_rows(r.dbias, pl.ds(0, 1), column_sum(gated), i == 0)
        return gated.astype(BF16)

    _, rows, d = dy.shape
    return gather_own(
        "gather_gated",
        value,
        dict(dy=dy, feed=feed, mod=mod, down_b=down_b),
        dict(dgate=sds((2, d), F32), dbias=sds((1, d), F32)),
        rows,
        d,
        cid,
        hosts,
        plan,
    )


def gather_plain(own, cid):
    _, rows, d = own.shape
    out = gather_own(
        "gather_plain", lambda r, i: r.x[i], dict(x=own), {}, rows, d, cid, frames=True
    )
    return out.full


def feed_back(
    dfeed, before, h2, mixed, dy, branch, mod, weights, proj_b, b, cid, hosts=(), plan=(), leaving=None,
    extra=None
):
    d, c = weights[1].shape
    _, rows, _ = mixed.shape
    tokens = 4 * rows
    ins = dict(dfeed=dfeed, before=before, h2=h2, mixed=mixed, dy=dy, branch=branch, mod=mod)
    ins.update(down_t=weights[1], proj_b=proj_b, **up_pieces(weights[0]))
    if leaving is not None:
        ins.update(leaving=leaving)
    outs = dict(
        full=sds((2, 4, 2, rows, d)),
        dmixed=sds(mixed.shape, F32),
        dup=sds((d, c)),
        dup_b=sds((1, c), F32),
        dshift=sds((2, d), F32),
        dscale=sds((2, d), F32),
        dgate=sds((2, d), F32),
        dproj_b=sds((1, d), F32),
    )
    strip = c // 3
    outs.update(ddown_b=sds((d, strip)))
    if not any(host.tag.startswith("da") for host in hosts):
        outs.update(ddown_a=sds((d, 2 * strip)))
    if leaving is not None:
        outs.update(left=sds(leaving.shape))
    if extra is not None:
        ins.update(extra=extra)
        outs.update(full2=sds((2, 2, 4, rows, d)))

    def body(r):
        net = Narrow(r)
        if extra is not None:
            second = second_gather(r)
        way = Cross(r)
        net.barrier(hosts, leaving is not None)

        def leave(i):
            way.send_back(i, r.leaving[i].astype(F32))

        def arrive(i):
            r.left[i] = way.received_back(i).astype(F32).reshape(rows, d).astype(BF16)

        def tile(i):
            da = kdot(flat(r.dfeed[i // 2, :, i % 2]), r.down_t[...], NN)
            v = r.before[i].astype(F32)
            t = gelu_tanh(v)
            r.active[i // 2, :, i % 2] = (0.5 * v * (1.0 + t)).astype(BF16).reshape(4, rows, c)
            slope = 0.5 * (1.0 + t) + 0.5 * v * (1.0 - t * t) * (
                GELU_C * (1.0 + 3.0 * GELU_A * v * v)
            )
            db = (da * slope).astype(BF16)
            r.dbefore[i // 2, :, i % 2] = db.reshape(4, rows, c)
            add_rows(r.dup_b, pl.ds(0, 1), column_sum(db.astype(F32)), i == 0)
            part = sum(
                kdot(db[:, low : low + ref.shape[1]], ref[...], NT) for low, ref in up_refs(r)
            )
            r.part[i // 2, :, i % 2] = part.astype(BF16).reshape(4, rows, d)
            net.sum_start(i)

        def middle(i):
            m = i // 2
            dh = net.sum_end(i)
            v, rs = norm_rows(r.mixed[i])
            add_rows(r.dshift, pl.ds(m, 1), column_sum(dh), i % 2 == 0)
            add_rows(r.dscale, pl.ds(m, 1), column_sum(dh * v), i % 2 == 0)
            dmixed = r.dy[i].astype(F32) + norm_back(dh, v, rs, r.mod[b, m, 4:5])
            r.dmixed[i] = dmixed
            gated = r.mod[b, m, 2:3] * dmixed
            dgate = column_sum(dmixed * (r.branch[i].astype(F32) + row_of(r.proj_b, b)))
            add_rows(r.dgate, pl.ds(m, 1), dgate, i % 2 == 0)
            add_rows(r.dproj_b, pl.ds(0, 1), column_sum(gated), i == 0)
            net.gather_start(i, gated.astype(BF16))

        def strip_of(out, at, left, right, j):
            right = right[:, :, :, :, pl.ds(j * strip, strip)].reshape(4 * tokens, strip)
            out[:, pl.ds(at * strip, strip)] = kdot(flat(left[...]), right, TN).astype(BF16)

        def weight_strip(j):
            if j == 0:
                strip_of(r.ddown_a, 0, r.dfeed, r.active, 0)
                strip_of(r.ddown_a, 1, r.dfeed, r.active, 1)
            elif j == 1:
                strip_of(r.ddown_b, 0, r.dfeed, r.active, 2)
                strip_of(r.dup, 0, r.h2, r.dbefore, 0)
            elif j < 4:
                strip_of(r.dup, j - 1, r.h2, r.dbefore, j - 1)

        stages = [(0, tile), (1, net.sum_cross), (4, weight_strip), (2, middle), (4, net.gather_forward)]
        if leaving is not None:
            stages = [(0, leave)] + stages + [(4, arrive)]
        if extra is not None:
            stages = [(0, lambda i: second.gather_start(i, r.extra[i]))] + stages
            stages += [(2, second.gather_forward)]
        pipeline(4, stages, hosts, plan)
        net.sum_drain()
        net.gather_drain()
        if leaving is not None:
            way.drain_back()
        if extra is not None:
            second.gather_drain()

    scratch = dict(Narrow.sum_scratch(rows, d), **Narrow.gather_scratch(rows, d))
    if leaving is not None:
        scratch.update(Cross.back_scratch(rows // 8, d))
    if extra is not None:
        scratch.update(second_scratch(rows, d))
    scratch.update(
        dbefore=pltpu.VMEM((2, 4, 2, rows, c), BF16), active=pltpu.VMEM((2, 4, 2, rows, c), BF16)
    )
    if "ddown_a" not in outs:
        scratch.update(ddown_a=pltpu.VMEM((d, 2 * strip), BF16))
    return call("feed_back", body, ins, outs, scratch, cid, FULL + ("full2",), hosts)


class Totals:
    in_turn = False

    def __init__(self, vectors, d):
        self.vectors, self.piece = vectors, (4, d)

    def phases(self):
        return [self.start, self.sum, self.spread]

    def ins(self):
        return {
            f"vector{k}": v for k, (v, _) in enumerate(self.vectors) if not isinstance(v, str)
        }

    def scratch(self):
        return dict(
            sums=pltpu.VMEM((8,) + self.piece, F32),
            terms=pltpu.VMEM((8,) + self.piece, F32),
            parts=pltpu.VMEM((4,) + self.piece, F32),
            mine=pltpu.VMEM(self.piece, F32),
            term_sem=pltpu.SemaphoreType.DMA((2, 8)),
            part_sem=pltpu.SemaphoreType.DMA((2, 4)),
            back_sem=pltpu.SemaphoreType.DMA((2, 8)),
        )

    def bind(self, r):
        self.r, self.w, self.n = r, lax.axis_index(WIDE), lax.axis_index(NARROW)

    def wide_copy(self, src, dst, sems, k):
        return pltpu.make_async_remote_copy(
            src_ref=src,
            dst_ref=dst,
            send_sem=sems.at[0, k],
            recv_sem=sems.at[1, k],
            device_id={WIDE: lax.rem(self.w + k, 8)},
        )

    def term(self, k):
        r = self.r
        return self.wide_copy(r.sums.at[lax.rem(self.w + k, 8)], r.terms.at[k], r.term_sem, k)

    def back(self, k):
        return self.wide_copy(self.r.mine, self.r.total.at[self.w], self.r.back_sem, k)

    def part(self, k):
        r = self.r
        return pltpu.make_async_remote_copy(
            src_ref=r.parts.at[0],
            dst_ref=r.parts.at[k],
            send_sem=r.part_sem.at[0, k],
            recv_sem=r.part_sem.at[1, k],
            device_id={NARROW: lax.rem(self.n + k, 4)},
        )

    def start(self):
        r = self.r
        r.sums[7] = jnp.zeros(self.piece, F32)
        for k, (vector, places) in enumerate(self.vectors):
            value = getattr(r, vector if isinstance(vector, str) else f"vector{k}")[...]
            for j, place in enumerate(places):
                width = value.shape[1]
                r.sums[place // 4, place % 4 : place % 4 + 1, :width] = value[j : j + 1]
        for k in range(1, 8):
            self.term(k).start()

    def sum(self):
        r = self.r
        total = r.sums[self.w]
        for k in range(1, 8):
            self.term(k).wait_recv()
            total = total + r.terms[k]
        r.parts[0] = total
        for k in range(1, 4):
            self.part(k).start()

    def spread(self):
        r = self.r
        total = r.parts[0]
        everywhere = total
        for k in range(1, 4):
            self.part(k).wait_recv()
            everywhere = everywhere + r.parts[k]
        total = jnp.where(self.w == 7, total, everywhere)
        r.mine[...] = total
        for k in range(1, 8):
            self.back(k).start()
        r.total[self.w] = total

    def drain(self):
        for k in range(1, 8):
            self.term(k).wait_send()
            self.back(k).wait()
        for k in range(1, 4):
            self.part(k).wait_send()


def attention_back(
    dbranch, qkv, att, h1, x_own, dmixed, mod, pack, b, keys, cid, hosts=(), plan=(), below=None, totals=None
):
    temporal = keys is not None
    d, hc = pack.shape[0], pack.shape[1] // 4
    c = 3 * hc
    heads = hc // HEAD_DIM
    _, rows, _ = x_own.shape
    tokens = 4 * rows
    ins = dict(dbranch=dbranch, qkv=qkv, att=att, h1=h1, x_own=x_own, dmixed=dmixed, mod=mod)
    ins.update(pack=pack)
    if temporal:
        ins.update(key_rows=keys[0], key_columns=keys[1])
    outs = dict(
        **({} if below or totals else dict(dx=sds(x_own.shape))),
        **({} if totals else dict(dpack=sds(pack.shape))),
        dqkv_b=sds((1, c), F32),
        dshift=sds((2, d), F32),
        dscale=sds((2, d), F32),
    )

    if below:
        ins.update(feed=below[0], down_b=below[1])
        outs.update(dgate=sds((2, d), F32), dbias=sds((1, d), F32), dy=sds(x_own.shape))
    if below:
        outs.update(full=sds((2, 4, 2, rows, d)))
    if totals:
        ins.update(totals.ins())
        outs.update(full2=sds((2, 2, 4, rows, d)), total=sds((8, 4, d), F32))

    def body(r):
        net = Narrow(r)
        net.barrier(hosts, below is not None, totals is not None)
        if totals:
            totals.bind(r)
            second = second_gather(r)
        way = Cross(r)
        r.proj_t[...] = r.pack[:, c:]
        if temporal:
            fill_mask(r.mask, r)

        def gated(i):
            m = i // 2
            v = way.received_back(i).astype(F32).reshape(rows, d)
            r.dy[i] = v.astype(BF16)
            out = r.mod[b - 1, m, 5:6] * v
            dgate = column_sum(v * (r.feed[i].astype(F32) + row_of(r.down_b, b - 1)))
            add_rows(r.dgate, pl.ds(m, 1), dgate, i % 2 == 0)
            add_rows(r.dbias, pl.ds(0, 1), column_sum(out), i == 0)
            net.gather_start(i, out.astype(BF16))

        def weight_grads(i):
            source = r.dbranch if temporal else r.dbr
            if i == 0:
                r.dpack[:, c:] = kdot(flat(source[...]), flat(r.att[...]), TN).astype(BF16)
            elif i == 1:
                r.dpack[:, :c] = kdot(flat(r.h1[...]), flat(r.dqkv[...]), TN).astype(BF16)

        def tile(i):
            t = tile_order(net, i, temporal)
            dbranch = flat(tile_at(r.dbranch, t, temporal)[...])
            if not temporal:
                r.dbr[i] = dbranch
            da = kdot(dbranch, r.proj_t[...], NN).astype(BF16)
            dqkv = attend_back(r.qkv[t], da, r.mask[i // 2] if temporal else None, heads)
            r.dqkv[t] = dqkv
            add_rows(r.dqkv_b, pl.ds(0, 1), column_sum(dqkv.astype(F32)), i == 0)
            part = kdot(dqkv, r.pack[:, :c], NT).astype(BF16)
            target = tile_at(r.part, t, temporal)
            target[...] = part.reshape(target.shape)
            send_tile(net, i, temporal)

        def middle(i):
            m = i // 2
            dh = net.sum_end(i)
            v, rs = norm_rows(r.x_own[i].astype(F32))
            add_rows(r.dshift, pl.ds(m, 1), column_sum(dh), i % 2 == 0)
            add_rows(r.dscale, pl.ds(m, 1), column_sum(dh * v), i % 2 == 0)
            dx = r.dmixed[i] + norm_back(dh, v, rs, r.mod[b, m, 1:2])
            if below:
                way.send_back(i, dx)
            elif totals:
                second.gather_start(i, dx.astype(BF16))
            else:
                r.dx[i] = dx.astype(BF16)

        before, after = cross_stages(net, temporal)
        stages = before + [(0, tile)] + after + [(2, middle)]
        if below:
            stages += [(5, weight_grads), (5, gated), (7, net.gather_forward)]
        else:
            stages += [(3, weight_grads)]
        if totals:
            stages += [(4, second.gather_forward)]
        pipeline(4, stages, tuple(hosts) + ((totals,) if totals else ()), plan)
        if totals:
            second.gather_drain()
        net.sum_drain()
        if below:
            net.gather_drain()
            way.drain_back()

    scratch = Narrow.sum_scratch(rows, d)
    scratch.update(dqkv=pltpu.VMEM((4, tokens, c), BF16), proj_t=pltpu.VMEM((d, hc), BF16))
    if temporal:
        scratch.update(mask=pltpu.VMEM((2, tokens // 2, tokens // 2), F32))
    else:
        scratch.update(dbr=pltpu.VMEM((4, tokens, d), BF16))
    if below:
        scratch.update(Narrow.gather_scratch(rows, d), **Cross.back_scratch(rows // 8, d))
    if totals:
        scratch.update(totals.scratch(), dpack=pltpu.VMEM(pack.shape, BF16))
        scratch.update(second_scratch(rows, d))
    hbm = ("full2",) if totals else FULL if below else ()
    return call("attention_back", body, ins, outs, scratch, cid, hbm, hosts)


def assemble(total, silu, grads):
    rows, d = grads["u0"].shape[0], total.shape[-1]
    hc, hidden = d // 4, grads["u0"].shape[1]
    outs = dict(
        qkv=sds((2, 3, rows, hc), F32),
        proj=sds((2, rows, hc), F32),
        up=sds((2, rows, hidden), F32),
        down=sds((2, rows, hidden), F32),
        ada=sds((2, 6, rows, hc), F32),
        qkv_b=sds((2, 2, hc), F32),
        proj_b=sds((2, d), F32),
        up_b=sds((2, hidden), F32),
        down_b=sds((2, d), F32),
        ada_b=sds((2, 6, hc), F32),
    )

    def body(r):
        n = lax.axis_index(NARROW)

        def line(k):
            return r.total[k // 4, k % 4 : k % 4 + 1]

        for b in range(2):
            pack = getattr(r, f"p{b}")[...]
            for j in range(3):
                r.qkv[b, j] = pack[:, j * hc : (j + 1) * hc]
            r.proj[b] = pack[:, 3 * hc :]
            r.up[b] = getattr(r, f"u{b}")[...]
            cut = getattr(r, f"da{b}").shape[1]
            r.down[b, :, :cut] = getattr(r, f"da{b}")[...]
            r.down[b, :, cut:] = getattr(r, f"db{b}")[...]
            for k in range(6):
                mine = []
                for m in range(2):
                    every = line(b * 12 + m * 6 + k)
                    pick = every[:, :hc]
                    for j in range(1, 4):
                        pick = jnp.where(n == j, every[:, j * hc : (j + 1) * hc], pick)
                    mine.append(pick)
                r.ada[b, k] = r.silu[0] * mine[0] + r.silu[1] * mine[1]
                r.ada_b[b, k : k + 1] = mine[0] + mine[1]
            hidden_row = line(28 + 2 * b)
            r.qkv_b[b, 0:1] = hidden_row[:, :hc]
            r.qkv_b[b, 1:2] = hidden_row[:, 2 * hc : 3 * hc]
            r.up_b[b : b + 1] = line(29 + 2 * b)
            r.proj_b[b : b + 1] = line(24 + b)
            r.down_b[b : b + 1] = line(26 + b)

    ins = dict(total=total, silu=silu, **grads)
    return call("assemble", body, ins, outs, {})


def wide_scatter(grad):
    size = lax.axis_size(WIDE)
    rows = grad.shape[0] // size
    moved = lax.all_to_all(grad, WIDE, split_axis=0, concat_axis=0, tiled=True)
    return jnp.sum(moved.reshape((size, rows) + grad.shape[1:]).astype(F32), axis=0)


def exchange(rows_in, seq_group):
    mb, half, count, d = rows_in.shape
    v = rows_in.reshape(mb, half, seq_group, count // seq_group, d)
    v = group_all_to_all(jnp.moveaxis(v, 2, 0), seq_group)
    return jnp.moveaxis(v, 0, 1).reshape(mb, half, count, d)


def exchange_back(rows_in, seq_group):
    mb, half, count, d = rows_in.shape
    v = rows_in.reshape(mb, seq_group, half, count // seq_group, d)
    v = group_all_to_all(jnp.moveaxis(v, 1, 0), seq_group)
    return jnp.moveaxis(v, 0, 2).reshape(mb, half, count, d)


def group_all_to_all(v, seq_group):
    size = lax.axis_size(WIDE)
    groups = None
    if seq_group != size:
        groups = [
            list(range(first, first + seq_group)) for first in range(0, size, seq_group)
        ]
    return lax.all_to_all(
        v, WIDE, split_axis=0, concat_axis=0, tiled=True, axis_index_groups=groups
    )


def shards(
    tokens,
    conditioning,
    frame_segments,
    cotangent,
    qkv_weight,
    qkv_bias,
    proj_weight,
    proj_bias,
    up_weight,
    up_bias,
    down_weight,
    down_bias,
    ada_weight,
    ada_bias,
):
    mb, half, patches, d = tokens.shape
    parts = lax.axis_size(NARROW)
    seq_frames = frame_segments.shape[2]
    seqs = frame_segments.shape[1]
    seq_group = seq_frames // half
    n = lax.axis_index(NARROW)
    w = lax.axis_index(WIDE)
    seq_here = w // seq_group
    blocks = qkv_weight.shape[0]
    rows = patches // parts
    local = qkv_bias.shape[-1]
    shard_rows = ada_weight.shape[1]
    own_shape = (mb, half, rows, d)
    chunk_shape = (mb * half, rows, d)

    hosted = lax.axis_size(WIDE) == 8 and seqs == 1 and blocks == 2 and mb == 2
    first = [
        jnp.concatenate([qkv_weight[b].reshape(shard_rows, -1), proj_weight[b].T], axis=1)
        for b in range(blocks)
    ]
    down_rows = jnp.swapaxes(down_weight, 1, 2)
    hidden = up_weight.shape[2]
    cut = hidden // 128 * 4 // 9 * 128
    packs, grads = types.SimpleNamespace(), {}

    def gather(key, shard, b=None, low=0, cols=None, vmem=False, turn=True):
        if hosted:
            return (WideGather(key, shard, b, low, cols, vmem, turn),)
        shard = shard if b is None else shard[b]
        shard = shard[:, low : low + (cols or shard.shape[1])]
        setattr(packs, key, lax.all_gather(shard, WIDE, axis=0, tiled=True))
        return ()

    def scatter(key, grad, low=0, cols=None, depth=2):
        if hosted:
            return (WideScatter(key, grad, None, low, cols, depth),)
        grads[key] = wide_scatter(grad)
        return ()

    def take(result):
        for key, value in vars(result).items():
            if key.endswith("all"):
                setattr(packs, key[:-3], value)
            if key.endswith("sum"):
                grads[key[:-3]] = value
        return result

    def scatter_inside(key, source, cols, depth=2):
        shape = sds((shard_rows * lax.axis_size(WIDE), d))
        return (WideScatter(key, shape, source, 0, cols, depth),) if hosted else ()

    silu = jax.nn.silu(conditioning.astype(F32)).astype(BF16)
    silu_rows = lax.dynamic_slice_in_dim(silu, w * shard_rows, shard_rows, 2)
    partial = jnp.einsum(
        "msr,brck->bmsck", silu_rows, ada_weight, preferred_element_type=F32
    )
    modulation = mod = None
    first0 = gather("a0", first[0], vmem=True)
    if hosted:
        modulation = Modulation(
            partial.reshape(8, -1, local), ada_bias.astype(F32).reshape(blocks, 2, -1, local)
        )
    else:
        total = lax.psum(partial, WIDE)
        here = lax.dynamic_index_in_dim(total, seq_here, 2, keepdims=False)
        mod = lax.all_gather(
            here + ada_bias.astype(F32)[:, None], NARROW, axis=3, tiled=True
        )

    frame_ids = lax.dynamic_index_in_dim(frame_segments, seq_here, 1, keepdims=False)
    count = rows // seq_group
    keys = (frame_ids[:, :, None] * count + jnp.arange(count)).reshape(mb, -1).astype(F32)
    keys = (keys[:, None, :], keys[:, :, None])

    def own_of(full):
        return lax.dynamic_slice_in_dim(full, n * rows, rows, 2).reshape(chunk_shape)

    up0 = take(
        attention_up(
            tokens.reshape(mb * half, patches, d), None, mod, getattr(packs, "a0", None),
            (qkv_bias, proj_bias), 0, None, 0,
            gather("u0", up_weight, 0) + gather("d0", down_rows, 0), PLANS["up0"],
            first0[0] if hosted else None, modulation,
        )
    )
    mod = getattr(up0, "mod", mod)
    x0 = up0.x_own
    ff0 = take(
        feed_forward(
            up0.full, up0.mixed, mod, ((packs.u0,), packs.d0), (up_bias, down_bias),
            None, 0, 1, gather("a1", first[1], turn=False) + gather("ua1", up_weight, 1, 0, cut), PLANS["ff0"],
            cross=hosted,
        )
    )

    if hosted:
        x1, h1 = ff0.y, ff0.full
        dy1 = cotangent.reshape(mb * half, patches, d)
    else:
        x1 = exchange(ff0.y.reshape(own_shape), seq_group).reshape(chunk_shape)
        h1 = gather_normed(x1, mod, 1, 2).full
        dy1 = exchange(own_of(cotangent).reshape(own_shape), seq_group).reshape(chunk_shape)
    h1 = h1.reshape(4, patches, d)
    up1 = take(
        attention_up(
            h1, x1, mod, packs.a1, (qkv_bias, proj_bias), 1, keys, 3,
            gather("ub1", up_weight, 1, cut, hidden - cut) + gather("d1", down_rows, 1),
            PLANS["up1"],
        )
    )
    feed_weights = ((packs.ua1, packs.ub1), packs.d1)
    ff1 = feed_forward(
        up1.full, up1.mixed, mod, feed_weights, (up_bias, down_bias), dy1, 1, 4,
        cross_dy=hosted,
    )
    if hosted:
        dy1 = ff1.dy_here
    else:
        out_own = exchange_back(ff1.y.reshape(own_shape), seq_group).reshape(chunk_shape)
    fb1 = take(
        feed_back(
            ff1.full, ff1.before, up1.full, up1.mixed, dy1, up1.branch, mod,
            feed_weights, proj_bias, 1, 7, scatter_inside("da1", "ddown_a", hidden // 3 * 2), PLANS["fb1"],
            ff1.y if hosted else None,
        )
    )
    if hosted:
        out_own = fb1.left
    else:
        scatter("da1", fb1.ddown_a)
    ab1 = take(
        attention_back(
            fb1.full, up1.qkv, up1.att, h1, x1, fb1.dmixed, mod, packs.a1, 1, keys,
            8, scatter("db1", fb1.ddown_b, 0, None, 4) + scatter("u1", fb1.dup, 0, None, 1), PLANS["ab1"],
            (ff0.feed, down_bias) if hosted else None,
        )
    )
    if hosted:
        dy0, gg0 = ab1.dy, ab1
    else:
        dy0 = exchange_back(ab1.dx.reshape(own_shape), seq_group).reshape(chunk_shape)
        gg0 = gather_gated(dy0, ff0.feed, mod, down_bias, 0, 9)
    fb0 = take(
        feed_back(
            gg0.full, ff0.before, up0.full, up0.mixed, dy0, up0.branch, mod,
            ((packs.u0,), packs.d0), proj_bias, 0, 10,
            scatter("p1", ab1.dpack) + scatter_inside("da0", "ddown_a", hidden // 3 * 2), PLANS["fb0"],
            None, out_own,
        )
    )
    if not hosted:
        scatter("da0", fb0.ddown_a)
    mine = ("dshift", "dscale", "dqkv_b")
    hidden_rows = [mine[2], fb0.dup_b, ab1.dqkv_b, fb1.dup_b]
    model_rows = [fb0.dproj_b, fb1.dproj_b, gg0.dbias, ff1.dbias]
    mod_rows = [
        [shift, scale, fb.dgate, fb.dshift, fb.dscale, dgate2]
        for shift, scale, fb, dgate2 in (
            mine[:2] + (fb0, gg0.dgate),
            (ab1.dshift, ab1.dscale, fb1, ff1.dgate),
        )
    ]
    vectors = [
        (v, (b * 12 + k, b * 12 + 6 + k)) for b, group in enumerate(mod_rows) for k, v in enumerate(group)
    ]
    vectors += [(v, (24 + k,)) for k, v in enumerate(model_rows + hidden_rows)]
    ab0 = take(
        attention_back(
            fb0.full, up0.qkv, up0.att, up0.h1, x0, fb0.dmixed, mod, packs.a0, 0,
            None, 11, scatter("db0", fb0.ddown_b, 0, None, 4) + scatter("u0", fb0.dup, 0, None, 2)
            + scatter_inside("p0", "dpack", d, 4), PLANS["ab0"],
            None, Totals(vectors, d) if hosted else None,
        )
    )
    layer_out = fb0.full2.reshape(mb, half, patches, d)
    if hosted:
        input_grad = ab0.full2.astype(F32).reshape(mb, half, patches, d)
        done = assemble(
            ab0.total, silu_rows.astype(F32).reshape(mb, shard_rows, 1), grads
        )
        return (
            layer_out,
            input_grad,
            jnp.moveaxis(done.qkv, 1, 2),
            done.qkv_b,
            jnp.swapaxes(done.proj, 1, 2),
            done.proj_b,
            done.up,
            done.up_b,
            jnp.swapaxes(done.down, 1, 2),
            done.down_b,
            jnp.moveaxis(done.ada, 1, 2),
            done.ada_b,
        )
    scatter("p0", ab0.dpack)
    mod_rows[0][:2] = ab0.dshift, ab0.dscale
    hidden_rows[0] = ab0.dqkv_b
    input_grad = gather_plain(ab0.dx, 12).astype(F32).reshape(mb, half, patches, d)
    dmod = jnp.stack([jnp.stack(group, axis=1) for group in mod_rows])
    slot = (jnp.arange(seqs) == seq_here).astype(F32)
    dmod = dmod[:, :, None] * slot[None, None, :, None, None]
    model_b = jnp.concatenate(model_rows)
    dmod, model_b = lax.psum((dmod, model_b), (WIDE, NARROW))
    model_b = model_b.reshape(2, blocks, d)
    hidden_b = lax.psum(
        jnp.stack([jnp.concatenate(hidden_rows[2 * b : 2 * b + 2], axis=1)[0] for b in range(2)]),
        WIDE,
    )
    dmod = lax.dynamic_slice_in_dim(dmod, n * local, local, 4)
    silu_f = silu_rows.astype(F32)
    ada_wgrad = sum(
        silu_f[m, s][None, :, None, None] * dmod[:, m, s][:, None]
        for m in range(mb)
        for s in range(seqs)
    )
    return (
        layer_out,
        input_grad,
        jnp.stack([grads[k][:, : 3 * local] for k in ("p0", "p1")]).reshape(qkv_weight.shape),
        jnp.stack([hidden_b[:, :local], hidden_b[:, 2 * local : 3 * local]], axis=1),
        jnp.stack([grads[k][:, 3 * local :].T for k in ("p0", "p1")]),
        model_b[0],
        jnp.stack([grads[k] for k in ("u0", "u1")]),
        hidden_b[:, 3 * local :],
        jnp.stack([jnp.concatenate([grads["da" + b], grads["db" + b]], 1).T for b in "01"]),
        model_b[1],
        ada_wgrad,
        jnp.sum(dmod, axis=(1, 2)),
    )


def solution(mesh):
    return jax.shard_map(
        shards,
        mesh=mesh,
        in_specs=(
            P(None, WIDE, None, None),
            P(),
            P(),
            P(None, WIDE, None, None),
            P(None, WIDE, None, NARROW),
            P(None, None, NARROW),
            P(None, NARROW, WIDE),
            P(),
            P(None, WIDE, NARROW),
            P(None, NARROW),
            P(None, NARROW, WIDE),
            P(),
            P(None, WIDE, None, NARROW),
            P(None, None, NARROW),
        ),
        out_specs=(
            P(None, WIDE, None, None),
            P(None, WIDE, None, None),
            P(None, WIDE, None, NARROW),
            P(None, None, NARROW),
            P(None, NARROW, WIDE),
            P(),
            P(None, WIDE, NARROW),
            P(None, NARROW),
            P(None, NARROW, WIDE),
            P(),
            P(None, WIDE, None, NARROW),
            P(None, None, NARROW),
        ),
        check_vma=False,
    )
```

```python
import functools
import types

import jax
import jax.numpy as jnp
from jax import lax
from jax.experimental import pallas as pl
from jax.experimental.pallas import tpu as pltpu
from jax.sharding import PartitionSpec as P

HEAD_DIM = 72
NORM_EPS = 1e-06
WIDE, NARROW = "wide", "narrow"
MASKED = -1e30
BF16 = jnp.bfloat16
F32 = jnp.float32


NN, NT, TN = ((1,), (0,)), ((1,), (1,)), ((0,), (0,))
CHUNKS = 4
GELU_C = 0.7978845608028654
GELU_A = 0.044715
FULL = ("full",)
GROUP = 0
END = 99
PLANS = dict(
    up0=((0, 0, 0), (0, 1, 0), (2, 0, 1), (2, 1, 1), (4, 0, 2), (4, 1, 2)),
    ff0=((1, 0, 0), (2, 1, 0), (4, 0, 1), (5, 1, 1), (6, 0, 2), (7, 1, 2)),
    up1=((1, 0, 0), (2, 1, 0), (3, 0, 1), (4, 1, 1), (5, 0, 2), (5, 1, 2)),
    fb1=((4, 0, 0), (5, 0, 1), (6, 0, 2), (7, 0, 3)),
    ab1=(
        (-1, 0, 0), (-1, 1, 0), (0, 0, 1), (1, 0, 2), (2, 0, 3), (2, 1, 1), (3, 0, 4), (5, 1, 2), (8, 1, 3),
    ),
    fb0=(
        (-1, 0, 0), (1, 0, 1), (3, 0, 2), (4, 1, 0), (5, 0, 3), (6, 0, 4), (7, 1, 1),
    ),
    ab0=(
        (-1, 0, 0), (-1, 1, 0), (0, 0, 1), (1, 0, 2), (2, 0, 3), (2, 1, 1), (3, 0, 4), (3, 1, 2), (5, 1, 3),
        (6, 3, 0), (6, 2, 0), (7, 1, 4), (7, 3, 1), (END, 2, 1), (END, 3, 2), (END, 2, 2),
    ),
)


def kdot(a, b, dims):
    return lax.dot_general(a, b, (dims, ((), ())), preferred_element_type=F32)


class Loads:
    def __init__(self, refs, keys):
        self.waited = set()
        self.copies = {}
        for key in keys:
            source, target, sems = refs[key + "_hbm"], refs[key], refs[key + "_load"]
            self.copies[key] = [
                pltpu.make_async_copy(source.at[i], target.at[i], sems.at[i])
                for i in range(target.shape[0])
            ] if len(target.shape) > 2 else [
                pltpu.make_async_copy(source, target, sems.at[0])
            ]
            for copy in self.copies[key]:
                copy.start()

    def need(self, key, *chunks):
        for i in chunks or range(len(self.copies.get(key, ()))):
            if key in self.copies and (key, i) not in self.waited:
                self.waited.add((key, i))
                self.copies[key][i].wait()

    def rest(self):
        for key in self.copies:
            self.need(key)


def call(name, body, ins, outs, scratch, cid=None, hbm=(), hosts=(), loads=()):
    ins, outs, scratch, hbm = dict(ins), dict(outs), dict(scratch), set(hbm)
    for host in hosts:
        ins.update(host.ins())
        outs.update(host.outs())
        scratch.update(host.scratch())
        hbm.update(host.hbm())
        loads = tuple(loads) + tuple(host.loads())
    for key in loads:
        shape = ins[key].shape
        scratch[key] = pltpu.VMEM(shape, ins[key].dtype)
        scratch[key + "_load"] = pltpu.SemaphoreType.DMA((shape[0] if len(shape) > 2 else 1,))
        hbm.add(key + "_hbm")
    names = [key + "_hbm" if key in loads else key for key in ins] + list(outs) + list(scratch)

    def spec(key):
        return pl.BlockSpec(memory_space=pl.ANY if key in hbm else pltpu.VMEM)

    def kernel(*refs):
        named = dict(zip(names, refs))
        r = types.SimpleNamespace(**named)
        r.loads = Loads(named, loads)
        for host in hosts:
            host.bind(r)
        body(r)
        r.loads.rest()

    results = pl.pallas_call(
        kernel,
        in_specs=[spec(key) for key in names[: len(ins)]],
        out_specs=[spec(key) for key in outs],
        out_shape=list(outs.values()),
        scratch_shapes=list(scratch.values()),
        compiler_params=pltpu.CompilerParams(
            vmem_limit_bytes=60 << 20,
            collective_id=cid,
            has_side_effects=cid is not None,
        ),
        name=name,
    )(*ins.values())
    return types.SimpleNamespace(**dict(zip(outs, results)))


def pipeline(count, stages, hosts=(), plan=()):
    phases = [host.phases() for host in hosts]
    for step in range(-1, count + max(lag for lag, _ in stages)):
        for lag, stage in stages:
            if step >= 0 and 0 <= step - lag < count:
                stage(step - lag)
        for at, host, phase in plan:
            if at == step and host < len(hosts):
                phases[host][phase]()
    for at, host, phase in plan:
        if at == END and host < len(hosts):
            phases[host][phase]()
    for phase in all_phases(hosts, plan):
        phase()
    for host in hosts:
        host.drain()


def all_phases(hosts, plan=()):
    done = [(host, phase) for _, host, phase in plan]
    left = [
        (k if host.in_turn else 0, h, k, phase)
        for h, host in enumerate(hosts)
        for k, phase in enumerate(host.phases())
        if (h, k) not in done
    ]
    return [item[3] for item in sorted(left, key=lambda item: item[:3])]


def wide_pair(w):
    return w + 1 - 2 * lax.rem(w, 2)


class Host:
    in_turn = True

    def loads(self):
        return ()

    def bind(self, refs):
        w = lax.axis_index(WIDE)
        self.x, self.z = lax.rem(w, 2), lax.div(w, 2)
        self.pair, self.up = wide_pair(w), lax.rem(w + 2, 8)
        self.r = refs
        size = len(self.tag)
        self.own_refs = types.SimpleNamespace(
            **{key[size:]: ref for key, ref in vars(refs).items() if key[:size] == self.tag}
        )


    def block(self, z, x):
        return pl.ds(pl.multiple_of((z * 2 + x) * self.rows, self.rows), self.rows)

    def remote(self, src, dst, sems, k, other):
        return pltpu.make_async_remote_copy(
            src_ref=src,
            dst_ref=dst,
            send_sem=sems.at[0, k],
            recv_sem=sems.at[1, k],
            device_id={WIDE: other},
        )


def column_parts(cols):
    cut = (cols // 128 + 1) // 2 * 128
    return (pl.ds(0, cut), pl.ds(cut, cols - cut))


class WideGather(Host):
    def __init__(self, tag, shard, block=None, low=0, cols=None, vmem=False, turn=True):
        self.tag, self.shard, self.index, self.low, self.vmem = tag, shard, block, low, vmem
        self.rows, self.cols = shard.shape[-2], cols or shard.shape[-1]
        turned = 128 if turn and self.cols >= 1024 else 0
        self.parts = column_parts(self.cols - turned)
        self.turned = pl.ds(self.cols - turned, turned) if turned else None

    def ins(self):
        return {self.tag + "shard": self.shard}

    def outs(self):
        return {self.tag + "all": sds((8 * self.rows, self.cols))}

    def scratch(self):
        return {
            self.tag + "zsem": pltpu.SemaphoreType.DMA((2, 12)),
            self.tag + "xsem": pltpu.SemaphoreType.DMA((2, 9)),
            self.tag + "sem": pltpu.SemaphoreType.DMA,
        }

    def hbm(self):
        return [] if self.vmem else [self.tag + "all"]

    def own(self, cols):
        cols = pl.ds(self.low + cols.start, cols.size)
        shard = self.own_refs.shard
        return shard.at[:, cols] if self.index is None else shard.at[self.index, :, cols]

    def rows_of(self, k, part):
        here = self.block(lax.rem(self.z - k + 4, 4), self.x)
        place = self.own_refs.all.at[here, self.parts[part]]
        return (self.own(self.parts[part]) if k == 0 else place), place

    def z_copy(self, k, part):
        return self.remote(*self.rows_of(k, part), self.own_refs.zsem, 2 * k + part, self.up)

    def x_copy(self, k, part):
        return self.remote(*self.rows_of(k, part), self.own_refs.xsem, 2 * k + part, self.pair)

    def turned_rows(self, k, x):
        here = self.block(lax.rem(self.z - k + 4, 4), lax.rem(self.x + x, 2))
        place = self.own_refs.all.at[here, self.turned]
        return (self.own(self.turned) if k == 0 and x == 0 else place), place

    def turned_x(self):
        return self.remote(*self.turned_rows(0, 0), self.own_refs.xsem, 8, self.pair)

    def turned_z(self, k, x):
        return self.remote(*self.turned_rows(k, x), self.own_refs.zsem, 6 + 2 * k + x, self.up)

    def local_copy(self):
        here = self.block(self.z, self.x)
        return pltpu.make_async_copy(
            self.own(pl.ds(0, self.cols)), self.own_refs.all.at[here], self.own_refs.sem
        )

    def start(self):
        if self.turned:
            self.turned_x().start()
            self.turned_z(0, 0).start()
        for part in range(2):
            self.z_copy(0, part).start()
            self.x_copy(0, part).start()
        self.local_copy().start()

    def phases(self):
        def step(k):
            for part in range(2):
                self.z_copy(k - 1, part).wait_recv()
                if k < 3:
                    self.z_copy(k, part).start()
                self.x_copy(k, part).start()
            if self.turned:
                self.turned_z(k - 1, 0).wait_recv()
                if k < 3:
                    self.turned_z(k, 0).start()
                if k == 1:
                    self.turned_x().wait_recv()
                else:
                    self.turned_z(k - 2, 1).wait_recv()
                self.turned_z(k - 1, 1).start()

        return [lambda k=k: step(k) for k in (1, 2, 3)]

    def drain(self):
        self.local_copy().wait()
        if self.turned:
            self.turned_z(2, 1).wait_recv()
            self.turned_x().wait_send()
            for k in range(3):
                for x in range(2):
                    self.turned_z(k, x).wait_send()
        for k in range(4):
            for part in range(2):
                self.x_copy(k, part).wait()
                if k < 3:
                    self.z_copy(k, part).wait_send()


class WideScatter(Host):
    in_turn = False

    def __init__(self, tag, grad, source=None, low=0, cols=None, depth=2):
        self.tag, self.grad, self.source, self.low = tag, grad, source, low
        self.late, self.depth = source is not None, depth
        self.rows, self.cols = grad.shape[0] // 8, cols or grad.shape[1]
        self.parts = column_parts(self.cols)

    def ins(self):
        return {} if self.late else {self.tag + "grad": self.grad}

    def outs(self):
        return {self.tag + "sum": sds((self.rows, self.cols), F32)}

    def scratch(self):
        size = (self.rows, self.cols)
        return {
            self.tag + "got": pltpu.VMEM((4,) + size, BF16),
            self.tag + "send": pltpu.VMEM((3,) + size, BF16),
            self.tag + "ring": pltpu.VMEM((3,) + size, BF16),
            self.tag + "xsem": pltpu.SemaphoreType.DMA((2, 8)),
            self.tag + "zsem": pltpu.SemaphoreType.DMA((2, 6)),
        }

    def hbm(self):
        return []

    def loads(self):
        return () if self.late else (self.tag + "grad",)

    def rows_of(self, s, x, part):
        grad = getattr(self.r, self.source) if self.late else self.own_refs.grad
        cols = pl.ds(self.low + self.parts[part].start, self.parts[part].size)
        return grad.at[self.block(lax.rem(self.z - s + 7, 4), x), cols]

    def x_copy(self, s, part):
        return self.remote(
            self.rows_of(s, 1 - self.x, part),
            self.own_refs.got.at[s, :, self.parts[part]],
            self.own_refs.xsem,
            2 * s + part,
            self.pair,
        )

    def z_copy(self, s, part):
        cols = self.parts[part]
        return self.remote(
            self.own_refs.send.at[s, :, cols],
            self.own_refs.ring.at[s, :, cols],
            self.own_refs.zsem,
            2 * s + part,
            self.up,
        )

    def start(self):
        pass

    def begin(self):
        if not self.late:
            self.r.loads.need(self.tag + "grad")
        for s in range(self.depth):
            for part in range(2):
                self.x_copy(s, part).start()

    def phases(self):
        def step(s):
            for part in range(2):
                cols = self.parts[part]
                self.x_copy(s, part).wait_recv()
                if s + self.depth < 4:
                    self.x_copy(s + self.depth, part).start()
                total = self.rows_of(s, self.x, part)[...].astype(F32)
                total = total + self.own_refs.got[s, :, cols].astype(F32)
                if s:
                    self.z_copy(s - 1, part).wait_recv()
                    total = total + self.own_refs.ring[s - 1, :, cols].astype(F32)
                if s < 3:
                    self.own_refs.send[s, :, cols] = total.astype(BF16)
                    self.z_copy(s, part).start()
                else:
                    self.own_refs.sum[:, cols] = total

        return [self.begin] + [lambda s=s: step(s) for s in range(4)]

    def drain(self):
        for s in range(4):
            for part in range(2):
                self.x_copy(s, part).wait_send()
                if s < 3:
                    self.z_copy(s, part).wait_send()


class Narrow:
    def __init__(self, refs, frames=False):
        n = lax.axis_index(NARROW)
        self.frames = frames
        self.n, self.core, self.across, self.far = (
            n,
            n + 1 - 2 * lax.rem(n, 2),
            lax.rem(n + 2, 4),
            3 - n,
        )
        self.r = refs

    def barrier(self, hosts=(), cross=False, everyone=False):
        sem = pltpu.get_barrier_semaphore()
        for other in (self.core, self.across) + ((self.far,) if everyone else ()):
            pl.semaphore_signal(sem, inc=1, device_id={NARROW: other})
        if cross or everyone:
            w = lax.axis_index(WIDE)
            for k in range(1, 8):
                pl.semaphore_signal(sem, inc=1, device_id={WIDE: lax.rem(w + k, 8)})
        elif hosts:
            w = lax.axis_index(WIDE)
            for other in (wide_pair(w), lax.rem(w + 6, 8)):
                pl.semaphore_signal(sem, inc=1, device_id={WIDE: other})
        count = 10 if everyone else 9 if cross else 4 if hosts else 2
        pl.semaphore_wait(sem, count)
        for host in hosts:
            host.start()

    def remote(self, src, dst, sems, index, other):
        return pltpu.make_async_remote_copy(
            src_ref=src,
            dst_ref=dst,
            send_sem=sems.at[(0,) + index],
            recv_sem=sems.at[(1,) + index],
            device_id={NARROW: other},
        )

    def sum_scratch(rows, d):
        return dict(
            part=pltpu.VMEM((CHUNKS // 2, 4, 2, rows, d), BF16),
            near=pltpu.VMEM((CHUNKS, 2, rows, d), BF16),
            pair=pltpu.VMEM((CHUNKS, rows, d), BF16),
            cross=pltpu.VMEM((CHUNKS, rows, d), BF16),
            near_sem=pltpu.SemaphoreType.DMA((2, CHUNKS, 2)),
            cross_sem=pltpu.SemaphoreType.DMA((2, CHUNKS)),
        )

    def near_copy(self, i, which):
        owner = self.core if which == 0 else self.far
        return self.remote(
            self.r.part.at[i // 2, owner, i % 2],
            self.r.near.at[i, which],
            self.r.near_sem,
            (i, which),
            self.core,
        )

    def cross_copy(self, i):
        return self.remote(
            self.r.pair.at[i], self.r.cross.at[i], self.r.cross_sem, (i,), self.across
        )

    def sum_far(self, i):
        self.near_copy(i, 1).start()

    def sum_near(self, i):
        self.near_copy(i, 0).start()

    def sum_start(self, i):
        self.sum_far(i)
        self.sum_near(i)

    def sum_cross(self, i):
        self.near_copy(i, 1).wait_recv()
        mine = self.r.part[i // 2, self.across, i % 2].astype(F32)
        self.r.pair[i] = (mine + self.r.near[i, 1].astype(F32)).astype(BF16)
        self.cross_copy(i).start()

    def sum_end(self, i):
        self.near_copy(i, 0).wait_recv()
        total = self.r.part[i // 2, self.n, i % 2].astype(F32) + self.r.near[i, 0].astype(F32)
        self.cross_copy(i).wait_recv()
        return total + self.r.cross[i].astype(F32)

    def sum_drain(self):
        for i in range(CHUNKS):
            self.near_copy(i, 0).wait_send()
            self.near_copy(i, 1).wait_send()
            self.cross_copy(i).wait_send()

    def gather_scratch(rows, d):
        return dict(
            own=pltpu.VMEM((CHUNKS, rows, d), BF16),
            own_sem=pltpu.SemaphoreType.DMA((CHUNKS,)),
            out_sem=pltpu.SemaphoreType.DMA((2, CHUNKS, 3)),
        )

    def place(self, i, n):
        if self.frames:
            return self.r.full.at[i // 2, i % 2, n]
        return self.r.full.at[i // 2, n, i % 2]

    def out_copy(self, i, which):
        if which == 2:
            rows = self.place(i, self.across)
            return self.remote(rows, rows, self.r.out_sem, (i, 2), self.core)
        other = self.across if which == 0 else self.core
        return self.remote(
            self.r.own.at[i], self.place(i, self.n), self.r.out_sem, (i, which), other
        )

    def own_copy(self, i):
        return pltpu.make_async_copy(
            self.r.own.at[i], self.place(i, self.n), self.r.own_sem.at[i]
        )

    def gather_start(self, i, value):
        self.r.own[i] = value
        self.out_copy(i, 0).start()
        self.out_copy(i, 1).start()
        self.own_copy(i).start()

    def gather_forward(self, i):
        self.out_copy(i, 0).wait_recv()
        self.out_copy(i, 2).start()

    def gather_drain(self):
        for i in range(CHUNKS):
            self.own_copy(i).wait()
            for which in range(3):
                self.out_copy(i, which).wait_send()
                if which:
                    self.out_copy(i, which).wait_recv()


def second_gather(r):
    refs = types.SimpleNamespace(full=r.full2, own=r.own2, own_sem=r.own_sem2, out_sem=r.out_sem2)
    return Narrow(refs, frames=True)


def second_scratch(rows, d):
    return {key + "2": value for key, value in Narrow.gather_scratch(rows, d).items()}


class Cross:
    def __init__(self, refs):
        self.r, self.w = refs, lax.axis_index(WIDE)

    def scratch(count, d):
        return dict(
            cross_out=pltpu.VMEM((2, 2, 8, count, d), BF16),
            cross_in=pltpu.VMEM((2, 8, 2, count, d), BF16),
            cross_sems=pltpu.SemaphoreType.DMA((2, CHUNKS, 8)),
        )

    def back_scratch(count, d):
        return dict(
            cross_out=pltpu.VMEM((2, 8, 2, count, d), BF16),
            cross_in=pltpu.VMEM((2, 2, 8, count, d), BF16),
            cross_sems=pltpu.SemaphoreType.DMA((2, CHUNKS, 8)),
        )

    def copy(self, src, dst, i, k):
        return pltpu.make_async_remote_copy(
            src_ref=src,
            dst_ref=dst,
            send_sem=self.r.cross_sems.at[0, i, k],
            recv_sem=self.r.cross_sems.at[1, i, k],
            device_id={WIDE: lax.rem(self.w + k, 8)},
        )

    def to_patches(self, i, k):
        m, f, other = i // 2, i % 2, lax.rem(self.w + k, 8)
        return self.copy(
            self.r.cross_out.at[m, f, other], self.r.cross_in.at[m, self.w, f], i, k
        )

    def send(self, i, value):
        m, f = i // 2, i % 2
        out = self.r.cross_out
        out[m, f] = value.reshape(out.shape[2:]).astype(BF16)
        for k in range(1, 8):
            self.to_patches(i, k).start()
        self.r.cross_in[m, self.w, f] = out[m, f, self.w]

    def received(self, c):
        m, h = c // 2, c % 2
        if h == 0:
            for i in (2 * m, 2 * m + 1):
                for k in range(1, 8):
                    self.to_patches(i, k).wait_recv()
        return self.r.cross_in[m, 4 * h : 4 * h + 4]

    def to_frames(self, m, k):
        other = lax.rem(self.w + k, 8)
        return self.copy(
            self.r.cross_out.at[m, other], self.r.cross_in.at[m, :, self.w], m, k
        )

    def send_back(self, c, value):
        m, h = c // 2, c % 2
        out = self.r.cross_out
        out[m, 4 * h : 4 * h + 4] = value.reshape((4,) + out.shape[2:]).astype(BF16)
        if h:
            for k in range(1, 8):
                self.to_frames(m, k).start()
            self.r.cross_in[m, :, self.w] = out[m, self.w]

    def received_back(self, i):
        m, f = i // 2, i % 2
        if f == 0:
            for k in range(1, 8):
                self.to_frames(m, k).wait_recv()
        return self.r.cross_in[m, f]

    def drain(self):
        for i in range(CHUNKS):
            for k in range(1, 8):
                self.to_patches(i, k).wait_send()

    def drain_back(self):
        for m in range(2):
            for k in range(1, 8):
                self.to_frames(m, k).wait_send()


def norm_rows(v):
    centred = v - jnp.mean(v, axis=-1, keepdims=True)
    r = lax.rsqrt(jnp.mean(centred * centred, axis=-1, keepdims=True) + NORM_EPS)
    return centred * r, r


def norm_back(grad, n, r, scale):
    dn = grad * (1.0 + scale)
    return r * (
        dn
        - jnp.mean(dn, axis=-1, keepdims=True)
        - n * jnp.mean(dn * n, axis=-1, keepdims=True)
    )


def column_sum(v):
    return jnp.sum(v, axis=0, keepdims=True)


def sds(shape, dtype=BF16):
    return jax.ShapeDtypeStruct(shape, dtype)


def softmax_of(s, mask):
    s = s * HEAD_DIM ** (-0.5)
    if mask is not None:
        s = s + mask
    p = jnp.exp(s - jnp.max(s, axis=-1, keepdims=True))
    return p * (1.0 / jnp.sum(p, axis=-1, keepdims=True))


def head_parts(v, heads, offset, size):
    return [
        v[t : t + size, offset + h * HEAD_DIM : offset + (h + 1) * HEAD_DIM]
        for t in range(0, v.shape[0], size)
        for h in range(heads)
    ]


def join_heads(pieces, heads):
    rows = [
        jnp.concatenate(pieces[t : t + heads], axis=1) for t in range(0, len(pieces), heads)
    ]
    return rows[0] if len(rows) == 1 else jnp.concatenate(rows, axis=0)


def attend(qkv, mask, heads):
    size = qkv.shape[0] if mask is None else mask.shape[0]
    width = heads * HEAD_DIM
    q, k, v = (head_parts(qkv, heads, j * width, size) for j in range(3))
    scores = [kdot(a, b, NT) for a, b in zip(q, k)]
    probs = [softmax_of(s, mask).astype(BF16) for s in scores]
    return join_heads([kdot(p, b, NN).astype(BF16) for p, b in zip(probs, v)], heads)


def attend_back(qkv, grad, mask, heads):
    size = qkv.shape[0] if mask is None else mask.shape[0]
    width = heads * HEAD_DIM
    q, k, v = (head_parts(qkv, heads, j * width, size) for j in range(3))
    g = head_parts(grad, heads, 0, size)
    group = GROUP or len(q)
    dq, dk, dv = [], [], []
    for low in range(0, len(q), group):
        part = slice(low, low + group)
        scores = [kdot(a, b, NT) for a, b in zip(q[part], k[part])]
        dps = [kdot(a, b, NT) for a, b in zip(g[part], v[part])]
        probs = [softmax_of(s, mask) for s in scores]
        dv += [kdot(p.astype(BF16), a, TN).astype(BF16) for p, a in zip(probs, g[part])]
        ds = [
            (p * (dp - jnp.sum(p * dp, axis=-1, keepdims=True)) * HEAD_DIM ** (-0.5)).astype(BF16)
            for p, dp in zip(probs, dps)
        ]
        dq += [kdot(a, b, NN).astype(BF16) for a, b in zip(ds, k[part])]
        dk += [kdot(a, b, TN).astype(BF16) for a, b in zip(ds, q[part])]
    return jnp.concatenate([join_heads(m, heads) for m in (dq, dk, dv)], axis=1)


def gelu_tanh(v):
    return jnp.tanh(GELU_C * (v + GELU_A * v * v * v))


def tile_at(ref, i, temporal):
    if temporal:
        return ref.at[lax.div(i, 2), pl.ds(lax.rem(i, 2) * 2, 2)]
    return ref.at[i // 2, :, i % 2]


def tile_order(net, i, temporal):
    if not temporal:
        return i
    across = lax.div(net.n, 2)
    return i // 2 * 2 + (across if i % 2 else 1 - across)


def send_tile(net, i, temporal):
    if not temporal:
        net.sum_start(i)
        return
    for j in (i // 2 * 2, i // 2 * 2 + 1):
        if i % 2:
            net.sum_near(j)
        else:
            net.sum_far(j)


def cross_stages(net, temporal):
    if not temporal:
        return [], [(1, net.sum_cross)]

    def both(i):
        if i % 2:
            net.sum_cross(i - 1)
            net.sum_cross(i)

    return [(0, both)], []


def flat(v):
    return v.reshape(-1, v.shape[-1])


def row_of(ref, b):
    return ref[...].astype(F32)[b : b + 1]


def fill_bias(out, qkv_b, hc):
    out[...] = jnp.zeros_like(out)
    rows = qkv_b.astype(F32)
    out[:, :hc] = rows[0:1]
    out[:, 2 * hc :] = rows[1:2]


def fill_mask(out, r):
    for m in range(2):
        out[m] = jnp.where(r.key_rows[m] == r.key_columns[m], 0.0, MASKED)


class Modulation:
    def __init__(self, partial, bias):
        self.partial, self.bias = partial, bias

    def ins(self):
        return dict(partial=self.partial, ada_b=self.bias)

    def scratch(self):
        _, rows, width = self.partial.shape
        return dict(
            terms=pltpu.VMEM((8, rows, width), F32),
            mine=pltpu.VMEM((rows, width), F32),
            every=pltpu.VMEM((8, rows, width), F32),
            parts=pltpu.VMEM((4, 8, rows, width), F32),
            term_sem=pltpu.SemaphoreType.DMA((2, 8)),
            back_sem=pltpu.SemaphoreType.DMA((2, 8)),
            part_sem=pltpu.SemaphoreType.DMA((2, 4)),
        )

    def bind(self, r):
        self.r, self.w, self.n = r, lax.axis_index(WIDE), lax.axis_index(NARROW)

    def wide_copy(self, src, dst, sems, k):
        return pltpu.make_async_remote_copy(
            src_ref=src,
            dst_ref=dst,
            send_sem=sems.at[0, k],
            recv_sem=sems.at[1, k],
            device_id={WIDE: lax.rem(self.w + k, 8)},
        )

    def term(self, k):
        r = self.r
        return self.wide_copy(
            r.partial.at[lax.rem(self.w + k, 8)], r.terms.at[k], r.term_sem, k
        )

    def back(self, k):
        return self.wide_copy(self.r.mine, self.r.every.at[self.w], self.r.back_sem, k)

    def part(self, k):
        r = self.r
        return pltpu.make_async_remote_copy(
            src_ref=r.every,
            dst_ref=r.parts.at[k],
            send_sem=r.part_sem.at[0, k],
            recv_sem=r.part_sem.at[1, k],
            device_id={NARROW: lax.rem(self.n + k, 4)},
        )

    def start(self):
        for k in range(1, 8):
            self.term(k).start()

    def sum(self):
        r, w = self.r, self.w
        total = r.partial[w] + r.ada_b[lax.div(w, 4), lax.rem(w, 2)]
        for k in range(1, 8):
            self.term(k).wait_recv()
            total = total + r.terms[k]
        r.mine[...] = total
        for k in range(1, 8):
            self.back(k).start()
        r.every[w] = total

    def spread(self):
        for k in range(1, 8):
            self.back(k).wait_recv()
        for k in range(1, 4):
            self.part(k).start()
        self.r.parts[0] = self.r.every[...]

    def store(self, out):
        for k in range(1, 4):
            self.part(k).wait_recv()
        for piece in range(8):
            low = piece % 2 * 3
            out[piece // 4, piece // 2 % 2, low : low + 3] = jnp.concatenate(
                [self.r.parts[lax.rem(self.n - owner + 4, 4), piece] for owner in range(4)], axis=1
            )

    def drain(self):
        for k in range(1, 8):
            self.term(k).wait_send()
            self.back(k).wait_send()
        for k in range(1, 4):
            self.part(k).wait_send()


def attention_up(
    x_or_h, x_own, mod, pack, biases, b, keys, cid, hosts=(), plan=(), first=None, modulation=None
):
    temporal = keys is not None
    starting = first is not None
    d = x_or_h.shape[-1]
    hc = biases[0].shape[-1]
    c = 3 * hc
    heads = hc // HEAD_DIM
    tokens = x_or_h.shape[1]
    rows = tokens // 4
    own = (4, rows, d)
    ins = dict(src=x_or_h, qkv_b=biases[0], proj_b=biases[1])
    if temporal:
        ins.update(key_rows=keys[0], key_columns=keys[1], x_own=x_own)
    if starting:
        ins.update(modulation.ins())
    else:
        ins.update(mod=mod, pack=pack)
    outs = dict(
        qkv=sds((4, tokens, c)),
        att=sds((4, tokens, hc)),
        branch=sds(own),
        mixed=sds(own, F32),
        full=sds((2, 4, 2, rows, d)),
    )
    if not temporal:
        outs.update(h1=sds((4, tokens, d)), x_own=sds(own))
    if starting:
        outs.update(mod=sds((2, 2, 6, d), F32))

    def body(r):
        net = Narrow(r)
        fill_bias(r.qb, r.qkv_b[b], hc)
        if temporal:
            fill_mask(r.mask, r)

        def prepare(i):
            r.loads.need("src", i)
            v, _ = norm_rows(r.src[i].astype(F32))
            r.h1[i] = (v * (1.0 + r.mod[b, i // 2, 1:2]) + r.mod[b, i // 2, 0:1]).astype(BF16)
            r.x_own[i] = r.src[i, pl.ds(pl.multiple_of(net.n * rows, rows), rows)]

        if starting:
            net.barrier(everyone=True)
            modulation.bind(r)
            modulation.start()
            for host in (first,) + tuple(hosts):
                host.start()
            steps = first.phases()
            modulation.sum()
            steps[0]()
            modulation.spread()
            steps[1]()
            modulation.store(r.mod)
            for i in range(2):
                prepare(i)
            steps[2]()
            for i in range(2, 4):
                prepare(i)
            first.drain()
            weights = first.own_refs.all
        else:
            net.barrier(hosts)
            weights = r.pack
        r.loads.need("pack")
        r.proj_t[...] = weights[:, c:]

        def tile(i):
            t = tile_order(net, i, temporal)
            if temporal:
                r.loads.need("src", i // 2 * 2, i // 2 * 2 + 1)
                h = r.src[t]
            else:
                if not starting:
                    prepare(i)
                h = r.h1[i]
            qkv = (kdot(h, weights[:, :c], NN) + r.qb[...]).astype(BF16)
            r.qkv[t] = qkv
            att = attend(qkv, r.mask[i // 2] if temporal else None, heads)
            r.att[t] = att
            part = kdot(att, r.proj_t[...], NT).astype(BF16)
            target = tile_at(r.part, t, temporal)
            target[...] = part.reshape(target.shape)
            send_tile(net, i, temporal)

        def middle(i):
            m = i // 2
            branch = net.sum_end(i)
            r.branch[i] = branch.astype(BF16)
            mixed = r.x_own[i].astype(F32) + r.mod[b, m, 2:3] * (branch + row_of(r.proj_b, b))
            r.mixed[i] = mixed
            v, _ = norm_rows(mixed)
            net.gather_start(i, (v * (1.0 + r.mod[b, m, 4:5]) + r.mod[b, m, 3:4]).astype(BF16))

        before, after = cross_stages(net, temporal)
        pipeline(
            4,
            before + [(0, tile)] + after + [(2, middle), (3, net.gather_forward)],
            hosts,
            plan,
        )
        net.sum_drain()
        net.gather_drain()
        if starting:
            modulation.drain()

    scratch = dict(Narrow.sum_scratch(rows, d), **Narrow.gather_scratch(rows, d))
    scratch.update(proj_t=pltpu.VMEM((d, hc), BF16), qb=pltpu.VMEM((1, c), F32))
    if temporal:
        scratch.update(mask=pltpu.VMEM((2, tokens // 2, tokens // 2), F32))
    if starting:
        scratch.update(modulation.scratch())
    carried = ((first,) if starting else ()) + tuple(hosts)
    loads = ("src",) if starting else ("pack", "src")
    return call("attention_up", body, ins, outs, scratch, cid, FULL, carried, loads)


def up_pieces(pieces):
    return {f"up{k}": piece for k, piece in enumerate(pieces)}


def up_refs(r):
    low = 0
    for key in ("up0", "up1"):
        if hasattr(r, key):
            ref = getattr(r, key)
            yield low, ref
            low += ref.shape[1]


def need_up(r):
    for key in ("up0", "up1", "down_t"):
        r.loads.need(key)


def times_up(r, h):
    need_up(r)
    parts = [kdot(h, ref[...], NN) for _, ref in up_refs(r)]
    return parts[0] if len(parts) == 1 else jnp.concatenate(parts, axis=1)


def feed_forward(
    h2, mixed, mod, weights, biases, dy, b, cid, hosts=(), plan=(), cross=False, cross_dy=False
):
    d, c = weights[1].shape
    _, rows, _ = mixed.shape
    ins = dict(h2=h2, mixed=mixed, mod=mod, down_t=weights[1], **up_pieces(weights[0]))
    ins.update(up_b=biases[0], down_b=biases[1])
    outs = dict(before=sds((4, 4 * rows, c)), feed=sds(mixed.shape), y=sds(mixed.shape))
    scratch = Narrow.sum_scratch(rows, d)
    if cross:
        outs.update(full=sds((2, 4, 2, rows, d)))
        scratch.update(Narrow.gather_scratch(rows, d), **Cross.scratch(rows // 8, d))
    if dy is not None:
        ins.update(dy=dy)
        outs.update(
            full=sds((2, 4, 2, rows, d)), dgate=sds((2, d), F32), dbias=sds((1, d), F32)
        )
        scratch.update(Narrow.gather_scratch(rows, d))
        if cross_dy:
            outs.update(dy_here=sds(mixed.shape))
            scratch.update(Cross.scratch(rows // 8, d))
            scratch.update(
                cot=pltpu.VMEM(mixed.shape, BF16), cot_sem=pltpu.SemaphoreType.DMA((CHUNKS,))
            )

    def body(r):
        net = Narrow(r)
        net.barrier(hosts, cross or cross_dy)
        way = Cross(r)

        def own_cot(i):
            here = pl.ds(pl.multiple_of(net.n * rows, rows), rows)
            return pltpu.make_async_copy(r.dy.at[i, here], r.cot.at[i], r.cot_sem.at[i])

        def leave(i):
            own_cot(i).wait()
            way.send(i, r.cot[i].astype(F32))

        if cross_dy:
            for i in range(CHUNKS):
                own_cot(i).start()

        def normed(i):
            x = way.received(i)
            v = x.astype(F32).reshape(rows, d)
            r.y[i] = v.astype(BF16)
            v, _ = norm_rows(v)
            m = i // 2
            h = v * (1.0 + r.mod[b + 1, m, 1:2]) + r.mod[b + 1, m, 0:1]
            net.gather_start(i, h.astype(BF16))

        def gated(i):
            m = i // 2
            if cross_dy:
                v = way.received(i).astype(F32).reshape(rows, d)
                r.dy_here[i] = v.astype(BF16)
            else:
                v = r.dy[i].astype(F32)
            dgate = column_sum(v * (r.feed[i].astype(F32) + row_of(r.down_b, b)))
            add_rows(r.dgate, pl.ds(m, 1), dgate, i % 2 == 0)
            v = r.mod[b, m, 5:6] * v
            add_rows(r.dbias, pl.ds(0, 1), column_sum(v), i == 0)
            net.gather_start(i, v.astype(BF16))

        def tile(i):
            r.loads.need("h2", i // 2)
            v = times_up(r, flat(r.h2[i // 2, :, i % 2])) + row_of(r.up_b, b)
            r.before[i] = v.astype(BF16)
            active = (0.5 * v * (1.0 + gelu_tanh(v))).astype(BF16)
            part = kdot(active, r.down_t[...], NT).astype(BF16)
            r.part[i // 2, :, i % 2] = part.reshape(4, rows, d)
            net.sum_start(i)

        def middle(i):
            m = i // 2
            feed = net.sum_end(i)
            r.feed[i] = feed.astype(BF16)
            full_feed = feed + row_of(r.down_b, b)
            y = r.mixed[i] + r.mod[b, m, 5:6] * full_feed
            if cross:
                way.send(i, y)
            else:
                r.y[i] = y.astype(BF16)

        stages = [(0, tile), (1, net.sum_cross), (2, middle)]
        if dy is not None:
            stages = stages + [(2, gated), (4, net.gather_forward)]
            if cross_dy:
                stages = [(0, leave)] + stages
        if cross:
            stages = stages + [(5, normed), (7, net.gather_forward)]
        pipeline(4, stages, hosts, plan)
        net.sum_drain()
        if dy is not None or cross:
            net.gather_drain()
        if cross or cross_dy:
            way.drain()

    hbm = (FULL if dy is not None or cross else ()) + (("dy",) if cross_dy else ())
    loads = tuple(up_pieces(weights[0])) + ("h2", "down_t")
    return call("feed_forward", body, ins, outs, scratch, cid, hbm, hosts, loads)


def gather_own(
    name, value_of, ins, more_outs, rows, d, cid, hosts=(), plan=(), frames=False
):
    def body(r):
        net = Narrow(r, frames)
        net.barrier(hosts)
        pipeline(
            4,
            [(0, lambda i: net.gather_start(i, value_of(r, i))), (2, net.gather_forward)],
            hosts,
            plan,
        )
        net.gather_drain()

    shape = (2, 2, 4, rows, d) if frames else (2, 4, 2, rows, d)
    outs = dict(full=sds(shape), **more_outs)
    return call(name, body, ins, outs, Narrow.gather_scratch(rows, d), cid, FULL, hosts)


def gather_normed(x_own, mod, b, cid, hosts=(), plan=()):
    def value(r, i):
        v, _ = norm_rows(r.x[i].astype(F32))
        return (v * (1.0 + r.mod[b, i // 2, 1:2]) + r.mod[b, i // 2, 0:1]).astype(BF16)

    _, rows, d = x_own.shape
    ins = dict(x=x_own, mod=mod)
    return gather_own("gather_normed", value, ins, {}, rows, d, cid, hosts, plan)


def add_rows(ref, index, v, first):
    if first:
        ref[index] = v
    else:
        ref[index] += v


def gather_gated(dy, feed, mod, down_b, b, cid, hosts=(), plan=()):
    def value(r, i):
        m = i // 2
        v = r.dy[i].astype(F32)
        gated = r.mod[b, m, 5:6] * v
        dgate = column_sum(v * (r.feed[i].astype(F32) + row_of(r.down_b, b)))
        add_rows(r.dgate, pl.ds(m, 1), dgate, i % 2 == 0)
        add_rows(r.dbias, pl.ds(0, 1), column_sum(gated), i == 0)
        return gated.astype(BF16)

    _, rows, d = dy.shape
    return gather_own(
        "gather_gated",
        value,
        dict(dy=dy, feed=feed, mod=mod, down_b=down_b),
        dict(dgate=sds((2, d), F32), dbias=sds((1, d), F32)),
        rows,
        d,
        cid,
        hosts,
        plan,
    )


def gather_plain(own, cid):
    _, rows, d = own.shape
    out = gather_own(
        "gather_plain", lambda r, i: r.x[i], dict(x=own), {}, rows, d, cid, frames=True
    )
    return out.full


def feed_back(
    dfeed, before, h2, mixed, dy, branch, mod, weights, proj_b, b, cid, hosts=(), plan=(), leaving=None,
    extra=None
):
    d, c = weights[1].shape
    _, rows, _ = mixed.shape
    tokens = 4 * rows
    ins = dict(dfeed=dfeed, before=before, h2=h2, mixed=mixed, dy=dy, branch=branch, mod=mod)
    ins.update(down_t=weights[1], proj_b=proj_b, **up_pieces(weights[0]))
    if leaving is not None:
        ins.update(leaving=leaving)
    outs = dict(
        full=sds((2, 4, 2, rows, d)),
        dmixed=sds(mixed.shape, F32),
        dup=sds((d, c)),
        dup_b=sds((1, c), F32),
        dshift=sds((2, d), F32),
        dscale=sds((2, d), F32),
        dgate=sds((2, d), F32),
        dproj_b=sds((1, d), F32),
    )
    strip = c // 3
    outs.update(ddown_b=sds((d, strip)))
    if not any(host.tag.startswith("da") for host in hosts):
        outs.update(ddown_a=sds((d, 2 * strip)))
    if leaving is not None:
        outs.update(left=sds(leaving.shape))
    if extra is not None:
        ins.update(extra=extra)
        outs.update(full2=sds((2, 2, 4, rows, d)))

    def body(r):
        net = Narrow(r)
        if extra is not None:
            second = second_gather(r)
        way = Cross(r)
        net.barrier(hosts, leaving is not None)

        def leave(i):
            way.send_back(i, r.leaving[i].astype(F32))

        def arrive(i):
            r.left[i] = way.received_back(i).astype(F32).reshape(rows, d).astype(BF16)

        def tile(i):
            need_up(r)
            r.loads.need("dfeed", i // 2)
            r.loads.need("before", i)
            da = kdot(flat(r.dfeed[i // 2, :, i % 2]), r.down_t[...], NN)
            v = r.before[i].astype(F32)
            t = gelu_tanh(v)
            r.active[i // 2, :, i % 2] = (0.5 * v * (1.0 + t)).astype(BF16).reshape(4, rows, c)
            slope = 0.5 * (1.0 + t) + 0.5 * v * (1.0 - t * t) * (
                GELU_C * (1.0 + 3.0 * GELU_A * v * v)
            )
            db = (da * slope).astype(BF16)
            r.dbefore[i // 2, :, i % 2] = db.reshape(4, rows, c)
            add_rows(r.dup_b, pl.ds(0, 1), column_sum(db.astype(F32)), i == 0)
            part = sum(
                kdot(db[:, low : low + ref.shape[1]], ref[...], NT) for low, ref in up_refs(r)
            )
            r.part[i // 2, :, i % 2] = part.astype(BF16).reshape(4, rows, d)
            net.sum_start(i)

        def middle(i):
            m = i // 2
            dh = net.sum_end(i)
            v, rs = norm_rows(r.mixed[i])
            add_rows(r.dshift, pl.ds(m, 1), column_sum(dh), i % 2 == 0)
            add_rows(r.dscale, pl.ds(m, 1), column_sum(dh * v), i % 2 == 0)
            dmixed = r.dy[i].astype(F32) + norm_back(dh, v, rs, r.mod[b, m, 4:5])
            r.dmixed[i] = dmixed
            gated = r.mod[b, m, 2:3] * dmixed
            dgate = column_sum(dmixed * (r.branch[i].astype(F32) + row_of(r.proj_b, b)))
            add_rows(r.dgate, pl.ds(m, 1), dgate, i % 2 == 0)
            add_rows(r.dproj_b, pl.ds(0, 1), column_sum(gated), i == 0)
            net.gather_start(i, gated.astype(BF16))

        def strip_of(out, at, left, right, j):
            right = right[:, :, :, :, pl.ds(j * strip, strip)].reshape(4 * tokens, strip)
            out[:, pl.ds(at * strip, strip)] = kdot(flat(left[...]), right, TN).astype(BF16)

        def weight_strip(j):
            r.loads.need("h2")
            if j == 0:
                strip_of(r.ddown_a, 0, r.dfeed, r.active, 0)
                strip_of(r.ddown_a, 1, r.dfeed, r.active, 1)
            elif j == 1:
                strip_of(r.ddown_b, 0, r.dfeed, r.active, 2)
                strip_of(r.dup, 0, r.h2, r.dbefore, 0)
            elif j < 4:
                strip_of(r.dup, j - 1, r.h2, r.dbefore, j - 1)

        stages = [(0, tile), (1, net.sum_cross), (4, weight_strip), (2, middle), (4, net.gather_forward)]
        if leaving is not None:
            stages = [(0, leave)] + stages + [(4, arrive)]
        if extra is not None:
            stages = [(0, lambda i: second.gather_start(i, r.extra[i]))] + stages
            stages += [(2, second.gather_forward)]
        pipeline(4, stages, hosts, plan)
        net.sum_drain()
        net.gather_drain()
        if leaving is not None:
            way.drain_back()
        if extra is not None:
            second.gather_drain()

    scratch = dict(Narrow.sum_scratch(rows, d), **Narrow.gather_scratch(rows, d))
    if leaving is not None:
        scratch.update(Cross.back_scratch(rows // 8, d))
    if extra is not None:
        scratch.update(second_scratch(rows, d))
    scratch.update(
        dbefore=pltpu.VMEM((2, 4, 2, rows, c), BF16), active=pltpu.VMEM((2, 4, 2, rows, c), BF16)
    )
    if "ddown_a" not in outs:
        scratch.update(ddown_a=pltpu.VMEM((d, 2 * strip), BF16))
    loads = ("down_t", "dfeed", "before") + tuple(up_pieces(weights[0])) + ("h2",)
    return call("feed_back", body, ins, outs, scratch, cid, FULL + ("full2",), hosts, loads)


class Totals:
    in_turn = False

    def __init__(self, vectors, d):
        self.vectors, self.piece = vectors, (4, d)

    def phases(self):
        return [self.start, self.sum, self.spread]

    def ins(self):
        return {
            f"vector{k}": v for k, (v, _) in enumerate(self.vectors) if not isinstance(v, str)
        }

    def scratch(self):
        return dict(
            sums=pltpu.VMEM((8,) + self.piece, F32),
            terms=pltpu.VMEM((8,) + self.piece, F32),
            parts=pltpu.VMEM((4,) + self.piece, F32),
            mine=pltpu.VMEM(self.piece, F32),
            term_sem=pltpu.SemaphoreType.DMA((2, 8)),
            part_sem=pltpu.SemaphoreType.DMA((2, 4)),
            back_sem=pltpu.SemaphoreType.DMA((2, 8)),
        )

    def bind(self, r):
        self.r, self.w, self.n = r, lax.axis_index(WIDE), lax.axis_index(NARROW)

    def wide_copy(self, src, dst, sems, k):
        return pltpu.make_async_remote_copy(
            src_ref=src,
            dst_ref=dst,
            send_sem=sems.at[0, k],
            recv_sem=sems.at[1, k],
            device_id={WIDE: lax.rem(self.w + k, 8)},
        )

    def term(self, k):
        r = self.r
        return self.wide_copy(r.sums.at[lax.rem(self.w + k, 8)], r.terms.at[k], r.term_sem, k)

    def back(self, k):
        return self.wide_copy(self.r.mine, self.r.total.at[self.w], self.r.back_sem, k)

    def part(self, k):
        r = self.r
        return pltpu.make_async_remote_copy(
            src_ref=r.parts.at[0],
            dst_ref=r.parts.at[k],
            send_sem=r.part_sem.at[0, k],
            recv_sem=r.part_sem.at[1, k],
            device_id={NARROW: lax.rem(self.n + k, 4)},
        )

    def start(self):
        r = self.r
        r.sums[7] = jnp.zeros(self.piece, F32)
        for k, (vector, places) in enumerate(self.vectors):
            value = getattr(r, vector if isinstance(vector, str) else f"vector{k}")[...]
            for j, place in enumerate(places):
                width = value.shape[1]
                r.sums[place // 4, place % 4 : place % 4 + 1, :width] = value[j : j + 1]
        for k in range(1, 8):
            self.term(k).start()

    def sum(self):
        r = self.r
        total = r.sums[self.w]
        for k in range(1, 8):
            self.term(k).wait_recv()
            total = total + r.terms[k]
        r.parts[0] = total
        for k in range(1, 4):
            self.part(k).start()

    def spread(self):
        r = self.r
        total = r.parts[0]
        everywhere = total
        for k in range(1, 4):
            self.part(k).wait_recv()
            everywhere = everywhere + r.parts[k]
        total = jnp.where(self.w == 7, total, everywhere)
        r.mine[...] = total
        for k in range(1, 8):
            self.back(k).start()
        r.total[self.w] = total

    def drain(self):
        for k in range(1, 8):
            self.term(k).wait_send()
            self.back(k).wait()
        for k in range(1, 4):
            self.part(k).wait_send()


def attention_back(
    dbranch, qkv, att, h1, x_own, dmixed, mod, pack, b, keys, cid, hosts=(), plan=(), below=None, totals=None
):
    temporal = keys is not None
    d, hc = pack.shape[0], pack.shape[1] // 4
    c = 3 * hc
    heads = hc // HEAD_DIM
    _, rows, _ = x_own.shape
    tokens = 4 * rows
    ins = dict(dbranch=dbranch, qkv=qkv, att=att, h1=h1, x_own=x_own, dmixed=dmixed, mod=mod)
    ins.update(pack=pack)
    if temporal:
        ins.update(key_rows=keys[0], key_columns=keys[1])
    outs = dict(
        **({} if below or totals else dict(dx=sds(x_own.shape))),
        **({} if totals else dict(dpack=sds(pack.shape))),
        dqkv_b=sds((1, c), F32),
        dshift=sds((2, d), F32),
        dscale=sds((2, d), F32),
    )

    if below:
        ins.update(feed=below[0], down_b=below[1])
        outs.update(dgate=sds((2, d), F32), dbias=sds((1, d), F32), dy=sds(x_own.shape))
    if below:
        outs.update(full=sds((2, 4, 2, rows, d)))
    if totals:
        ins.update(totals.ins())
        outs.update(full2=sds((2, 2, 4, rows, d)), total=sds((8, 4, d), F32))

    def body(r):
        net = Narrow(r)
        net.barrier(hosts, below is not None, totals is not None)
        if totals:
            totals.bind(r)
            second = second_gather(r)
        way = Cross(r)
        r.loads.need("pack")
        r.proj_t[...] = r.pack[:, c:]
        if temporal:
            fill_mask(r.mask, r)

        def gated(i):
            m = i // 2
            v = way.received_back(i).astype(F32).reshape(rows, d)
            r.dy[i] = v.astype(BF16)
            out = r.mod[b - 1, m, 5:6] * v
            dgate = column_sum(v * (r.feed[i].astype(F32) + row_of(r.down_b, b - 1)))
            add_rows(r.dgate, pl.ds(m, 1), dgate, i % 2 == 0)
            add_rows(r.dbias, pl.ds(0, 1), column_sum(out), i == 0)
            net.gather_start(i, out.astype(BF16))

        def weight_grads(i):
            for key in ("att", "h1"):
                r.loads.need(key)
            source = r.dbranch if temporal else r.dbr
            if i == 0:
                r.dpack[:, c:] = kdot(flat(source[...]), flat(r.att[...]), TN).astype(BF16)
            elif i == 1:
                r.dpack[:, :c] = kdot(flat(r.h1[...]), flat(r.dqkv[...]), TN).astype(BF16)

        def tile(i):
            t = tile_order(net, i, temporal)
            r.loads.need("dbranch", i // 2)
            r.loads.need("qkv", *((i // 2 * 2, i // 2 * 2 + 1) if temporal else (i,)))
            dbranch = flat(tile_at(r.dbranch, t, temporal)[...])
            if not temporal:
                r.dbr[i] = dbranch
            da = kdot(dbranch, r.proj_t[...], NN).astype(BF16)
            dqkv = attend_back(r.qkv[t], da, r.mask[i // 2] if temporal else None, heads)
            r.dqkv[t] = dqkv
            add_rows(r.dqkv_b, pl.ds(0, 1), column_sum(dqkv.astype(F32)), i == 0)
            part = kdot(dqkv, r.pack[:, :c], NT).astype(BF16)
            target = tile_at(r.part, t, temporal)
            target[...] = part.reshape(target.shape)
            send_tile(net, i, temporal)

        def middle(i):
            m = i // 2
            dh = net.sum_end(i)
            v, rs = norm_rows(r.x_own[i].astype(F32))
            add_rows(r.dshift, pl.ds(m, 1), column_sum(dh), i % 2 == 0)
            add_rows(r.dscale, pl.ds(m, 1), column_sum(dh * v), i % 2 == 0)
            dx = r.dmixed[i] + norm_back(dh, v, rs, r.mod[b, m, 1:2])
            if below:
                way.send_back(i, dx)
            elif totals:
                second.gather_start(i, dx.astype(BF16))
            else:
                r.dx[i] = dx.astype(BF16)

        before, after = cross_stages(net, temporal)
        stages = before + [(0, tile)] + after + [(2, middle)]
        if below:
            stages += [(5, weight_grads), (5, gated), (7, net.gather_forward)]
        else:
            stages += [(3, weight_grads)]
        if totals:
            stages += [(4, second.gather_forward)]
        pipeline(4, stages, tuple(hosts) + ((totals,) if totals else ()), plan)
        if totals:
            second.gather_drain()
        net.sum_drain()
        if below:
            net.gather_drain()
            way.drain_back()

    scratch = Narrow.sum_scratch(rows, d)
    scratch.update(dqkv=pltpu.VMEM((4, tokens, c), BF16), proj_t=pltpu.VMEM((d, hc), BF16))
    if temporal:
        scratch.update(mask=pltpu.VMEM((2, tokens // 2, tokens // 2), F32))
    else:
        scratch.update(dbr=pltpu.VMEM((4, tokens, d), BF16))
    if below:
        scratch.update(Narrow.gather_scratch(rows, d), **Cross.back_scratch(rows // 8, d))
    if totals:
        scratch.update(totals.scratch(), dpack=pltpu.VMEM(pack.shape, BF16))
        scratch.update(second_scratch(rows, d))
    hbm = ("full2",) if totals else FULL if below else ()
    loads = ("pack", "dbranch", "qkv", "att", "h1")
    return call("attention_back", body, ins, outs, scratch, cid, hbm, hosts, loads)


def assemble(total, silu, grads):
    rows, d = grads["u0"].shape[0], total.shape[-1]
    hc, hidden = d // 4, grads["u0"].shape[1]
    outs = dict(
        qkv=sds((2, 3, rows, hc), F32),
        proj=sds((2, rows, hc), F32),
        up=sds((2, rows, hidden), F32),
        down=sds((2, rows, hidden), F32),
        ada=sds((2, 6, rows, hc), F32),
        qkv_b=sds((2, 2, hc), F32),
        proj_b=sds((2, d), F32),
        up_b=sds((2, hidden), F32),
        down_b=sds((2, d), F32),
        ada_b=sds((2, 6, hc), F32),
    )

    def body(r):
        n = lax.axis_index(NARROW)

        def line(k):
            return r.total[k // 4, k % 4 : k % 4 + 1]

        for b in range(2):
            pack = getattr(r, f"p{b}")[...]
            for j in range(3):
                r.qkv[b, j] = pack[:, j * hc : (j + 1) * hc]
            r.proj[b] = pack[:, 3 * hc :]
            r.up[b] = getattr(r, f"u{b}")[...]
            cut = getattr(r, f"da{b}").shape[1]
            r.down[b, :, :cut] = getattr(r, f"da{b}")[...]
            r.down[b, :, cut:] = getattr(r, f"db{b}")[...]
            for k in range(6):
                mine = []
                for m in range(2):
                    every = line(b * 12 + m * 6 + k)
                    pick = every[:, :hc]
                    for j in range(1, 4):
                        pick = jnp.where(n == j, every[:, j * hc : (j + 1) * hc], pick)
                    mine.append(pick)
                r.ada[b, k] = r.silu[0] * mine[0] + r.silu[1] * mine[1]
                r.ada_b[b, k : k + 1] = mine[0] + mine[1]
            hidden_row = line(28 + 2 * b)
            r.qkv_b[b, 0:1] = hidden_row[:, :hc]
            r.qkv_b[b, 1:2] = hidden_row[:, 2 * hc : 3 * hc]
            r.up_b[b : b + 1] = line(29 + 2 * b)
            r.proj_b[b : b + 1] = line(24 + b)
            r.down_b[b : b + 1] = line(26 + b)

    ins = dict(total=total, silu=silu, **grads)
    return call("assemble", body, ins, outs, {})


def wide_scatter(grad):
    size = lax.axis_size(WIDE)
    rows = grad.shape[0] // size
    moved = lax.all_to_all(grad, WIDE, split_axis=0, concat_axis=0, tiled=True)
    return jnp.sum(moved.reshape((size, rows) + grad.shape[1:]).astype(F32), axis=0)


def exchange(rows_in, seq_group):
    mb, half, count, d = rows_in.shape
    v = rows_in.reshape(mb, half, seq_group, count // seq_group, d)
    v = group_all_to_all(jnp.moveaxis(v, 2, 0), seq_group)
    return jnp.moveaxis(v, 0, 1).reshape(mb, half, count, d)


def exchange_back(rows_in, seq_group):
    mb, half, count, d = rows_in.shape
    v = rows_in.reshape(mb, seq_group, half, count // seq_group, d)
    v = group_all_to_all(jnp.moveaxis(v, 1, 0), seq_group)
    return jnp.moveaxis(v, 0, 2).reshape(mb, half, count, d)


def group_all_to_all(v, seq_group):
    size = lax.axis_size(WIDE)
    groups = None
    if seq_group != size:
        groups = [
            list(range(first, first + seq_group)) for first in range(0, size, seq_group)
        ]
    return lax.all_to_all(
        v, WIDE, split_axis=0, concat_axis=0, tiled=True, axis_index_groups=groups
    )


def shards(
    tokens,
    conditioning,
    frame_segments,
    cotangent,
    qkv_weight,
    qkv_bias,
    proj_weight,
    proj_bias,
    up_weight,
    up_bias,
    down_weight,
    down_bias,
    ada_weight,
    ada_bias,
):
    mb, half, patches, d = tokens.shape
    parts = lax.axis_size(NARROW)
    seq_frames = frame_segments.shape[2]
    seqs = frame_segments.shape[1]
    seq_group = seq_frames // half
    n = lax.axis_index(NARROW)
    w = lax.axis_index(WIDE)
    seq_here = w // seq_group
    blocks = qkv_weight.shape[0]
    rows = patches // parts
    local = qkv_bias.shape[-1]
    shard_rows = ada_weight.shape[1]
    own_shape = (mb, half, rows, d)
    chunk_shape = (mb * half, rows, d)

    hosted = lax.axis_size(WIDE) == 8 and seqs == 1 and blocks == 2 and mb == 2
    first = [
        jnp.concatenate([qkv_weight[b].reshape(shard_rows, -1), proj_weight[b].T], axis=1)
        for b in range(blocks)
    ]
    down_rows = jnp.swapaxes(down_weight, 1, 2)
    hidden = up_weight.shape[2]
    cut = hidden // 128 * 4 // 9 * 128
    packs, grads = types.SimpleNamespace(), {}

    def gather(key, shard, b=None, low=0, cols=None, vmem=False, turn=True):
        if hosted:
            return (WideGather(key, shard, b, low, cols, vmem, turn),)
        shard = shard if b is None else shard[b]
        shard = shard[:, low : low + (cols or shard.shape[1])]
        setattr(packs, key, lax.all_gather(shard, WIDE, axis=0, tiled=True))
        return ()

    def scatter(key, grad, low=0, cols=None, depth=2):
        if hosted:
            return (WideScatter(key, grad, None, low, cols, depth),)
        grads[key] = wide_scatter(grad)
        return ()

    def take(result):
        for key, value in vars(result).items():
            if key.endswith("all"):
                setattr(packs, key[:-3], value)
            if key.endswith("sum"):
                grads[key[:-3]] = value
        return result

    def scatter_inside(key, source, cols, depth=2):
        shape = sds((shard_rows * lax.axis_size(WIDE), d))
        return (WideScatter(key, shape, source, 0, cols, depth),) if hosted else ()

    silu = jax.nn.silu(conditioning.astype(F32)).astype(BF16)
    silu_rows = lax.dynamic_slice_in_dim(silu, w * shard_rows, shard_rows, 2)
    partial = jnp.einsum(
        "msr,brck->bmsck", silu_rows, ada_weight, preferred_element_type=F32
    )
    modulation = mod = None
    first0 = gather("a0", first[0], vmem=True)
    if hosted:
        modulation = Modulation(
            partial.reshape(8, -1, local), ada_bias.astype(F32).reshape(blocks, 2, -1, local)
        )
    else:
        total = lax.psum(partial, WIDE)
        here = lax.dynamic_index_in_dim(total, seq_here, 2, keepdims=False)
        mod = lax.all_gather(
            here + ada_bias.astype(F32)[:, None], NARROW, axis=3, tiled=True
        )

    frame_ids = lax.dynamic_index_in_dim(frame_segments, seq_here, 1, keepdims=False)
    count = rows // seq_group
    keys = (frame_ids[:, :, None] * count + jnp.arange(count)).reshape(mb, -1).astype(F32)
    keys = (keys[:, None, :], keys[:, :, None])

    def own_of(full):
        return lax.dynamic_slice_in_dim(full, n * rows, rows, 2).reshape(chunk_shape)

    up0 = take(
        attention_up(
            tokens.reshape(mb * half, patches, d), None, mod, getattr(packs, "a0", None),
            (qkv_bias, proj_bias), 0, None, 0,
            gather("u0", up_weight, 0) + gather("d0", down_rows, 0), PLANS["up0"],
            first0[0] if hosted else None, modulation,
        )
    )
    mod = getattr(up0, "mod", mod)
    x0 = up0.x_own
    ff0 = take(
        feed_forward(
            up0.full, up0.mixed, mod, ((packs.u0,), packs.d0), (up_bias, down_bias),
            None, 0, 1, gather("a1", first[1], turn=False) + gather("ua1", up_weight, 1, 0, cut), PLANS["ff0"],
            cross=hosted,
        )
    )

    if hosted:
        x1, h1 = ff0.y, ff0.full
        dy1 = cotangent.reshape(mb * half, patches, d)
    else:
        x1 = exchange(ff0.y.reshape(own_shape), seq_group).reshape(chunk_shape)
        h1 = gather_normed(x1, mod, 1, 2).full
        dy1 = exchange(own_of(cotangent).reshape(own_shape), seq_group).reshape(chunk_shape)
    h1 = h1.reshape(4, patches, d)
    up1 = take(
        attention_up(
            h1, x1, mod, packs.a1, (qkv_bias, proj_bias), 1, keys, 3,
            gather("ub1", up_weight, 1, cut, hidden - cut) + gather("d1", down_rows, 1),
            PLANS["up1"],
        )
    )
    feed_weights = ((packs.ua1, packs.ub1), packs.d1)
    ff1 = feed_forward(
        up1.full, up1.mixed, mod, feed_weights, (up_bias, down_bias), dy1, 1, 4,
        cross_dy=hosted,
    )
    if hosted:
        dy1 = ff1.dy_here
    else:
        out_own = exchange_back(ff1.y.reshape(own_shape), seq_group).reshape(chunk_shape)
    fb1 = take(
        feed_back(
            ff1.full, ff1.before, up1.full, up1.mixed, dy1, up1.branch, mod,
            feed_weights, proj_bias, 1, 7, scatter_inside("da1", "ddown_a", hidden // 3 * 2), PLANS["fb1"],
            ff1.y if hosted else None,
        )
    )
    if hosted:
        out_own = fb1.left
    else:
        scatter("da1", fb1.ddown_a)
    ab1 = take(
        attention_back(
            fb1.full, up1.qkv, up1.att, h1, x1, fb1.dmixed, mod, packs.a1, 1, keys,
            8, scatter("db1", fb1.ddown_b, 0, None, 4) + scatter("u1", fb1.dup, 0, None, 1), PLANS["ab1"],
            (ff0.feed, down_bias) if hosted else None,
        )
    )
    if hosted:
        dy0, gg0 = ab1.dy, ab1
    else:
        dy0 = exchange_back(ab1.dx.reshape(own_shape), seq_group).reshape(chunk_shape)
        gg0 = gather_gated(dy0, ff0.feed, mod, down_bias, 0, 9)
    fb0 = take(
        feed_back(
            gg0.full, ff0.before, up0.full, up0.mixed, dy0, up0.branch, mod,
            ((packs.u0,), packs.d0), proj_bias, 0, 10,
            scatter("p1", ab1.dpack) + scatter_inside("da0", "ddown_a", hidden // 3 * 2), PLANS["fb0"],
            None, out_own,
        )
    )
    if not hosted:
        scatter("da0", fb0.ddown_a)
    mine = ("dshift", "dscale", "dqkv_b")
    hidden_rows = [mine[2], fb0.dup_b, ab1.dqkv_b, fb1.dup_b]
    model_rows = [fb0.dproj_b, fb1.dproj_b, gg0.dbias, ff1.dbias]
    mod_rows = [
        [shift, scale, fb.dgate, fb.dshift, fb.dscale, dgate2]
        for shift, scale, fb, dgate2 in (
            mine[:2] + (fb0, gg0.dgate),
            (ab1.dshift, ab1.dscale, fb1, ff1.dgate),
        )
    ]
    vectors = [
        (v, (b * 12 + k, b * 12 + 6 + k)) for b, group in enumerate(mod_rows) for k, v in enumerate(group)
    ]
    vectors += [(v, (24 + k,)) for k, v in enumerate(model_rows + hidden_rows)]
    ab0 = take(
        attention_back(
            fb0.full, up0.qkv, up0.att, up0.h1, x0, fb0.dmixed, mod, packs.a0, 0,
            None, 11, scatter("db0", fb0.ddown_b, 0, None, 4) + scatter("u0", fb0.dup, 0, None, 2)
            + scatter_inside("p0", "dpack", d, 4), PLANS["ab0"],
            None, Totals(vectors, d) if hosted else None,
        )
    )
    layer_out = fb0.full2.reshape(mb, half, patches, d)
    if hosted:
        input_grad = ab0.full2.astype(F32).reshape(mb, half, patches, d)
        done = assemble(
            ab0.total, silu_rows.astype(F32).reshape(mb, shard_rows, 1), grads
        )
        return (
            layer_out,
            input_grad,
            jnp.moveaxis(done.qkv, 1, 2),
            done.qkv_b,
            jnp.swapaxes(done.proj, 1, 2),
            done.proj_b,
            done.up,
            done.up_b,
            jnp.swapaxes(done.down, 1, 2),
            done.down_b,
            jnp.moveaxis(done.ada, 1, 2),
            done.ada_b,
        )
    scatter("p0", ab0.dpack)
    mod_rows[0][:2] = ab0.dshift, ab0.dscale
    hidden_rows[0] = ab0.dqkv_b
    input_grad = gather_plain(ab0.dx, 12).astype(F32).reshape(mb, half, patches, d)
    dmod = jnp.stack([jnp.stack(group, axis=1) for group in mod_rows])
    slot = (jnp.arange(seqs) == seq_here).astype(F32)
    dmod = dmod[:, :, None] * slot[None, None, :, None, None]
    model_b = jnp.concatenate(model_rows)
    dmod, model_b = lax.psum((dmod, model_b), (WIDE, NARROW))
    model_b = model_b.reshape(2, blocks, d)
    hidden_b = lax.psum(
        jnp.stack([jnp.concatenate(hidden_rows[2 * b : 2 * b + 2], axis=1)[0] for b in range(2)]),
        WIDE,
    )
    dmod = lax.dynamic_slice_in_dim(dmod, n * local, local, 4)
    silu_f = silu_rows.astype(F32)
    ada_wgrad = sum(
        silu_f[m, s][None, :, None, None] * dmod[:, m, s][:, None]
        for m in range(mb)
        for s in range(seqs)
    )
    return (
        layer_out,
        input_grad,
        jnp.stack([grads[k][:, : 3 * local] for k in ("p0", "p1")]).reshape(qkv_weight.shape),
        jnp.stack([hidden_b[:, :local], hidden_b[:, 2 * local : 3 * local]], axis=1),
        jnp.stack([grads[k][:, 3 * local :].T for k in ("p0", "p1")]),
        model_b[0],
        jnp.stack([grads[k] for k in ("u0", "u1")]),
        hidden_b[:, 3 * local :],
        jnp.stack([jnp.concatenate([grads["da" + b], grads["db" + b]], 1).T for b in "01"]),
        model_b[1],
        ada_wgrad,
        jnp.sum(dmod, axis=(1, 2)),
    )


def solution(mesh):
    return jax.shard_map(
        shards,
        mesh=mesh,
        in_specs=(
            P(None, WIDE, None, None),
            P(),
            P(),
            P(None, WIDE, None, None),
            P(None, WIDE, None, NARROW),
            P(None, None, NARROW),
            P(None, NARROW, WIDE),
            P(),
            P(None, WIDE, NARROW),
            P(None, NARROW),
            P(None, NARROW, WIDE),
            P(),
            P(None, WIDE, None, NARROW),
            P(None, None, NARROW),
        ),
        out_specs=(
            P(None, WIDE, None, None),
            P(None, WIDE, None, None),
            P(None, WIDE, None, NARROW),
            P(None, None, NARROW),
            P(None, NARROW, WIDE),
            P(),
            P(None, WIDE, NARROW),
            P(None, NARROW),
            P(None, NARROW, WIDE),
            P(),
            P(None, WIDE, None, NARROW),
            P(None, None, NARROW),
        ),
        check_vma=False,
    )
```

```python
import functools
import types

import jax
import jax.numpy as jnp
from jax import lax
from jax.experimental import pallas as pl
from jax.experimental.pallas import tpu as pltpu
from jax.sharding import PartitionSpec as P

HEAD_DIM = 72
NORM_EPS = 1e-06
WIDE, NARROW = "wide", "narrow"
MASKED = -1e30
BF16 = jnp.bfloat16
F32 = jnp.float32


NN, NT, TN = ((1,), (0,)), ((1,), (1,)), ((0,), (0,))
CHUNKS = 4
GELU_C = 0.7978845608028654
GELU_A = 0.044715
FULL = ("full",)
GROUP = 0
END = 99
PLANS = dict(
    up0=((0, 0, 0), (0, 1, 0), (2, 0, 1), (2, 1, 1), (4, 0, 2), (4, 1, 2)),
    ff0=((1, 0, 0), (2, 1, 0), (4, 0, 1), (5, 1, 1), (6, 0, 2), (7, 1, 2)),
    up1=((1, 0, 0), (2, 1, 0), (3, 0, 1), (4, 1, 1), (5, 0, 2), (5, 1, 2)),
    fb1=((4, 0, 0), (5, 0, 1), (6, 0, 2), (7, 0, 3)),
    ab1=(
        (-1, 0, 0), (-1, 1, 0), (0, 0, 1), (1, 0, 2), (2, 0, 3), (2, 1, 1), (3, 0, 4), (5, 1, 2), (8, 1, 3),
    ),
    fb0=(
        (-1, 0, 0), (1, 0, 1), (3, 0, 2), (4, 1, 0), (5, 0, 3), (6, 0, 4), (7, 1, 1),
    ),
    ab0=(
        (-1, 0, 0), (-1, 1, 0), (0, 0, 1), (1, 0, 2), (2, 0, 3), (2, 1, 1), (3, 0, 4), (3, 1, 2), (5, 1, 3),
        (6, 3, 0), (6, 2, 0), (7, 1, 4), (7, 3, 1), (END, 2, 1), (END, 3, 2), (END, 2, 2),
    ),
)


def kdot(a, b, dims):
    return lax.dot_general(a, b, (dims, ((), ())), preferred_element_type=F32)


class Loads:
    def __init__(self, refs, keys):
        self.waited = set()
        self.copies = {}
        for key in keys:
            source, target, sems = refs[key + "_hbm"], refs[key], refs[key + "_load"]
            self.copies[key] = [
                pltpu.make_async_copy(source.at[i], target.at[i], sems.at[i])
                for i in range(target.shape[0])
            ] if len(target.shape) > 2 else [
                pltpu.make_async_copy(source, target, sems.at[0])
            ]
            for copy in self.copies[key]:
                copy.start()

    def need(self, key, *chunks):
        for i in chunks or range(len(self.copies.get(key, ()))):
            if key in self.copies and (key, i) not in self.waited:
                self.waited.add((key, i))
                self.copies[key][i].wait()

    def rest(self):
        for key in self.copies:
            self.need(key)


class Stores:
    def __init__(self, refs, keys):
        self.started = set()
        self.copies = {}
        for key in keys:
            source, target, sems = refs[key], refs[key + "_hbm"], refs[key + "_store"]
            self.copies[key] = [
                pltpu.make_async_copy(source.at[i], target.at[i], sems.at[i])
                for i in range(source.shape[0])
            ] if len(source.shape) > 2 else [
                pltpu.make_async_copy(source, target, sems.at[0])
            ]

    def put(self, key, *chunks):
        for i in chunks:
            if key in self.copies and (key, i) not in self.started:
                self.started.add((key, i))
                self.copies[key][i].start()

    def rest(self):
        for key, copies in self.copies.items():
            self.put(key, *range(len(copies)))
        for copies in self.copies.values():
            for copy in copies:
                copy.wait()


def call(name, body, ins, outs, scratch, cid=None, hbm=(), hosts=(), loads=(), stores=()):
    ins, outs, scratch, hbm = dict(ins), dict(outs), dict(scratch), set(hbm)
    for host in hosts:
        ins.update(host.ins())
        outs.update(host.outs())
        scratch.update(host.scratch())
        hbm.update(host.hbm())
        loads = tuple(loads) + tuple(host.loads())
    for key in loads:
        shape = ins[key].shape
        scratch[key] = pltpu.VMEM(shape, ins[key].dtype)
        scratch[key + "_load"] = pltpu.SemaphoreType.DMA((shape[0] if len(shape) > 2 else 1,))
        hbm.add(key + "_hbm")
    for key in stores:
        shape = outs[key].shape
        scratch[key] = pltpu.VMEM(shape, outs[key].dtype)
        scratch[key + "_store"] = pltpu.SemaphoreType.DMA((shape[0] if len(shape) > 2 else 1,))
        hbm.add(key + "_hbm")
    names = [key + "_hbm" if key in loads else key for key in ins]
    names += [key + "_hbm" if key in stores else key for key in outs] + list(scratch)

    def spec(key):
        return pl.BlockSpec(memory_space=pl.ANY if key in hbm else pltpu.VMEM)

    def kernel(*refs):
        named = dict(zip(names, refs))
        r = types.SimpleNamespace(**named)
        r.loads, r.stores = Loads(named, loads), Stores(named, stores)
        for host in hosts:
            host.bind(r)
        body(r)
        r.loads.rest()
        r.stores.rest()

    results = pl.pallas_call(
        kernel,
        in_specs=[spec(key) for key in names[: len(ins)]],
        out_specs=[spec(key) for key in names[len(ins) : len(ins) + len(outs)]],
        out_shape=list(outs.values()),
        scratch_shapes=list(scratch.values()),
        compiler_params=pltpu.CompilerParams(
            vmem_limit_bytes=60 << 20,
            collective_id=cid,
            has_side_effects=cid is not None,
        ),
        name=name,
    )(*ins.values())
    return types.SimpleNamespace(**dict(zip(outs, results)))


def pipeline(count, stages, hosts=(), plan=()):
    phases = [host.phases() for host in hosts]
    for step in range(-1, count + max(lag for lag, _ in stages)):
        for lag, stage in stages:
            if step >= 0 and 0 <= step - lag < count:
                stage(step - lag)
        for at, host, phase in plan:
            if at == step and host < len(hosts):
                phases[host][phase]()
    for at, host, phase in plan:
        if at == END and host < len(hosts):
            phases[host][phase]()
    for phase in all_phases(hosts, plan):
        phase()
    for host in hosts:
        host.drain()


def all_phases(hosts, plan=()):
    done = [(host, phase) for _, host, phase in plan]
    left = [
        (k if host.in_turn else 0, h, k, phase)
        for h, host in enumerate(hosts)
        for k, phase in enumerate(host.phases())
        if (h, k) not in done
    ]
    return [item[3] for item in sorted(left, key=lambda item: item[:3])]


def wide_pair(w):
    return w + 1 - 2 * lax.rem(w, 2)


class Host:
    in_turn = True

    def loads(self):
        return ()

    def bind(self, refs):
        w = lax.axis_index(WIDE)
        self.x, self.z = lax.rem(w, 2), lax.div(w, 2)
        self.pair, self.up = wide_pair(w), lax.rem(w + 2, 8)
        self.r = refs
        size = len(self.tag)
        self.own_refs = types.SimpleNamespace(
            **{key[size:]: ref for key, ref in vars(refs).items() if key[:size] == self.tag}
        )


    def block(self, z, x):
        return pl.ds(pl.multiple_of((z * 2 + x) * self.rows, self.rows), self.rows)

    def remote(self, src, dst, sems, k, other):
        return pltpu.make_async_remote_copy(
            src_ref=src,
            dst_ref=dst,
            send_sem=sems.at[0, k],
            recv_sem=sems.at[1, k],
            device_id={WIDE: other},
        )


def column_parts(cols):
    cut = (cols // 128 + 1) // 2 * 128
    return (pl.ds(0, cut), pl.ds(cut, cols - cut))


class WideGather(Host):
    def __init__(self, tag, shard, block=None, low=0, cols=None, vmem=False, turn=True):
        self.tag, self.shard, self.index, self.low, self.vmem = tag, shard, block, low, vmem
        self.rows, self.cols = shard.shape[-2], cols or shard.shape[-1]
        turned = 128 if turn and self.cols >= 1024 else 0
        self.parts = column_parts(self.cols - turned)
        self.turned = pl.ds(self.cols - turned, turned) if turned else None

    def ins(self):
        return {self.tag + "shard": self.shard}

    def outs(self):
        return {self.tag + "all": sds((8 * self.rows, self.cols))}

    def scratch(self):
        return {
            self.tag + "zsem": pltpu.SemaphoreType.DMA((2, 12)),
            self.tag + "xsem": pltpu.SemaphoreType.DMA((2, 9)),
            self.tag + "sem": pltpu.SemaphoreType.DMA,
        }

    def hbm(self):
        return [] if self.vmem else [self.tag + "all"]

    def own(self, cols):
        cols = pl.ds(self.low + cols.start, cols.size)
        shard = self.own_refs.shard
        return shard.at[:, cols] if self.index is None else shard.at[self.index, :, cols]

    def rows_of(self, k, part):
        here = self.block(lax.rem(self.z - k + 4, 4), self.x)
        place = self.own_refs.all.at[here, self.parts[part]]
        return (self.own(self.parts[part]) if k == 0 else place), place

    def z_copy(self, k, part):
        return self.remote(*self.rows_of(k, part), self.own_refs.zsem, 2 * k + part, self.up)

    def x_copy(self, k, part):
        return self.remote(*self.rows_of(k, part), self.own_refs.xsem, 2 * k + part, self.pair)

    def turned_rows(self, k, x):
        here = self.block(lax.rem(self.z - k + 4, 4), lax.rem(self.x + x, 2))
        place = self.own_refs.all.at[here, self.turned]
        return (self.own(self.turned) if k == 0 and x == 0 else place), place

    def turned_x(self):
        return self.remote(*self.turned_rows(0, 0), self.own_refs.xsem, 8, self.pair)

    def turned_z(self, k, x):
        return self.remote(*self.turned_rows(k, x), self.own_refs.zsem, 6 + 2 * k + x, self.up)

    def local_copy(self):
        here = self.block(self.z, self.x)
        return pltpu.make_async_copy(
            self.own(pl.ds(0, self.cols)), self.own_refs.all.at[here], self.own_refs.sem
        )

    def start(self):
        if self.turned:
            self.turned_x().start()
            self.turned_z(0, 0).start()
        for part in range(2):
            self.z_copy(0, part).start()
            self.x_copy(0, part).start()
        self.local_copy().start()

    def phases(self):
        def step(k):
            for part in range(2):
                self.z_copy(k - 1, part).wait_recv()
                if k < 3:
                    self.z_copy(k, part).start()
                self.x_copy(k, part).start()
            if self.turned:
                self.turned_z(k - 1, 0).wait_recv()
                if k < 3:
                    self.turned_z(k, 0).start()
                if k == 1:
                    self.turned_x().wait_recv()
                else:
                    self.turned_z(k - 2, 1).wait_recv()
                self.turned_z(k - 1, 1).start()

        return [lambda k=k: step(k) for k in (1, 2, 3)]

    def drain(self):
        self.local_copy().wait()
        if self.turned:
            self.turned_z(2, 1).wait_recv()
            self.turned_x().wait_send()
            for k in range(3):
                for x in range(2):
                    self.turned_z(k, x).wait_send()
        for k in range(4):
            for part in range(2):
                self.x_copy(k, part).wait()
                if k < 3:
                    self.z_copy(k, part).wait_send()


class WideScatter(Host):
    in_turn = False

    def __init__(self, tag, grad, source=None, low=0, cols=None, depth=2):
        self.tag, self.grad, self.source, self.low = tag, grad, source, low
        self.late, self.depth = source is not None, depth
        self.rows, self.cols = grad.shape[0] // 8, cols or grad.shape[1]
        self.parts = column_parts(self.cols)

    def ins(self):
        return {} if self.late else {self.tag + "grad": self.grad}

    def outs(self):
        return {self.tag + "sum": sds((self.rows, self.cols), F32)}

    def scratch(self):
        size = (self.rows, self.cols)
        return {
            self.tag + "got": pltpu.VMEM((4,) + size, BF16),
            self.tag + "send": pltpu.VMEM((3,) + size, BF16),
            self.tag + "ring": pltpu.VMEM((3,) + size, BF16),
            self.tag + "xsem": pltpu.SemaphoreType.DMA((2, 8)),
            self.tag + "zsem": pltpu.SemaphoreType.DMA((2, 6)),
        }

    def hbm(self):
        return []

    def loads(self):
        return () if self.late else (self.tag + "grad",)

    def rows_of(self, s, x, part):
        grad = getattr(self.r, self.source) if self.late else self.own_refs.grad
        cols = pl.ds(self.low + self.parts[part].start, self.parts[part].size)
        return grad.at[self.block(lax.rem(self.z - s + 7, 4), x), cols]

    def x_copy(self, s, part):
        return self.remote(
            self.rows_of(s, 1 - self.x, part),
            self.own_refs.got.at[s, :, self.parts[part]],
            self.own_refs.xsem,
            2 * s + part,
            self.pair,
        )

    def z_copy(self, s, part):
        cols = self.parts[part]
        return self.remote(
            self.own_refs.send.at[s, :, cols],
            self.own_refs.ring.at[s, :, cols],
            self.own_refs.zsem,
            2 * s + part,
            self.up,
        )

    def start(self):
        pass

    def begin(self):
        if not self.late:
            self.r.loads.need(self.tag + "grad")
        for s in range(self.depth):
            for part in range(2):
                self.x_copy(s, part).start()

    def phases(self):
        def step(s):
            for part in range(2):
                cols = self.parts[part]
                self.x_copy(s, part).wait_recv()
                if s + self.depth < 4:
                    self.x_copy(s + self.depth, part).start()
                total = self.rows_of(s, self.x, part)[...].astype(F32)
                total = total + self.own_refs.got[s, :, cols].astype(F32)
                if s:
                    self.z_copy(s - 1, part).wait_recv()
                    total = total + self.own_refs.ring[s - 1, :, cols].astype(F32)
                if s < 3:
                    self.own_refs.send[s, :, cols] = total.astype(BF16)
                    self.z_copy(s, part).start()
                else:
                    self.own_refs.sum[:, cols] = total

        return [self.begin] + [lambda s=s: step(s) for s in range(4)]

    def drain(self):
        for s in range(4):
            for part in range(2):
                self.x_copy(s, part).wait_send()
                if s < 3:
                    self.z_copy(s, part).wait_send()


class Narrow:
    def __init__(self, refs, frames=False):
        n = lax.axis_index(NARROW)
        self.frames = frames
        self.n, self.core, self.across, self.far = (
            n,
            n + 1 - 2 * lax.rem(n, 2),
            lax.rem(n + 2, 4),
            3 - n,
        )
        self.r = refs

    def barrier(self, hosts=(), cross=False, everyone=False):
        sem = pltpu.get_barrier_semaphore()
        for other in (self.core, self.across) + ((self.far,) if everyone else ()):
            pl.semaphore_signal(sem, inc=1, device_id={NARROW: other})
        if cross or everyone:
            w = lax.axis_index(WIDE)
            for k in range(1, 8):
                pl.semaphore_signal(sem, inc=1, device_id={WIDE: lax.rem(w + k, 8)})
        elif hosts:
            w = lax.axis_index(WIDE)
            for other in (wide_pair(w), lax.rem(w + 6, 8)):
                pl.semaphore_signal(sem, inc=1, device_id={WIDE: other})
        count = 10 if everyone else 9 if cross else 4 if hosts else 2
        pl.semaphore_wait(sem, count)
        for host in hosts:
            host.start()

    def remote(self, src, dst, sems, index, other):
        return pltpu.make_async_remote_copy(
            src_ref=src,
            dst_ref=dst,
            send_sem=sems.at[(0,) + index],
            recv_sem=sems.at[(1,) + index],
            device_id={NARROW: other},
        )

    def sum_scratch(rows, d):
        return dict(
            part=pltpu.VMEM((CHUNKS // 2, 4, 2, rows, d), BF16),
            near=pltpu.VMEM((CHUNKS, 2, rows, d), BF16),
            pair=pltpu.VMEM((CHUNKS, rows, d), BF16),
            cross=pltpu.VMEM((CHUNKS, rows, d), BF16),
            near_sem=pltpu.SemaphoreType.DMA((2, CHUNKS, 2)),
            cross_sem=pltpu.SemaphoreType.DMA((2, CHUNKS)),
        )

    def near_copy(self, i, which):
        owner = self.core if which == 0 else self.far
        return self.remote(
            self.r.part.at[i // 2, owner, i % 2],
            self.r.near.at[i, which],
            self.r.near_sem,
            (i, which),
            self.core,
        )

    def cross_copy(self, i):
        return self.remote(
            self.r.pair.at[i], self.r.cross.at[i], self.r.cross_sem, (i,), self.across
        )

    def sum_far(self, i):
        self.near_copy(i, 1).start()

    def sum_near(self, i):
        self.near_copy(i, 0).start()

    def sum_start(self, i):
        self.sum_far(i)
        self.sum_near(i)

    def sum_cross(self, i):
        self.near_copy(i, 1).wait_recv()
        mine = self.r.part[i // 2, self.across, i % 2].astype(F32)
        self.r.pair[i] = (mine + self.r.near[i, 1].astype(F32)).astype(BF16)
        self.cross_copy(i).start()

    def sum_end(self, i):
        self.near_copy(i, 0).wait_recv()
        total = self.r.part[i // 2, self.n, i % 2].astype(F32) + self.r.near[i, 0].astype(F32)
        self.cross_copy(i).wait_recv()
        return total + self.r.cross[i].astype(F32)

    def sum_drain(self):
        for i in range(CHUNKS):
            self.near_copy(i, 0).wait_send()
            self.near_copy(i, 1).wait_send()
            self.cross_copy(i).wait_send()

    def gather_scratch(rows, d):
        return dict(
            own=pltpu.VMEM((CHUNKS, rows, d), BF16),
            own_sem=pltpu.SemaphoreType.DMA((CHUNKS,)),
            out_sem=pltpu.SemaphoreType.DMA((2, CHUNKS, 3)),
        )

    def place(self, i, n):
        if self.frames:
            return self.r.full.at[i // 2, i % 2, n]
        return self.r.full.at[i // 2, n, i % 2]

    def out_copy(self, i, which):
        if which == 2:
            rows = self.place(i, self.across)
            return self.remote(rows, rows, self.r.out_sem, (i, 2), self.core)
        other = self.across if which == 0 else self.core
        return self.remote(
            self.r.own.at[i], self.place(i, self.n), self.r.out_sem, (i, which), other
        )

    def own_copy(self, i):
        return pltpu.make_async_copy(
            self.r.own.at[i], self.place(i, self.n), self.r.own_sem.at[i]
        )

    def gather_start(self, i, value):
        self.r.own[i] = value
        self.out_copy(i, 0).start()
        self.out_copy(i, 1).start()
        self.own_copy(i).start()

    def gather_forward(self, i):
        self.out_copy(i, 0).wait_recv()
        self.out_copy(i, 2).start()

    def gather_drain(self):
        for i in range(CHUNKS):
            self.own_copy(i).wait()
            for which in range(3):
                self.out_copy(i, which).wait_send()
                if which:
                    self.out_copy(i, which).wait_recv()


def second_gather(r):
    refs = types.SimpleNamespace(full=r.full2, own=r.own2, own_sem=r.own_sem2, out_sem=r.out_sem2)
    return Narrow(refs, frames=True)


def second_scratch(rows, d):
    return {key + "2": value for key, value in Narrow.gather_scratch(rows, d).items()}


class Cross:
    def __init__(self, refs):
        self.r, self.w = refs, lax.axis_index(WIDE)

    def scratch(count, d):
        return dict(
            cross_out=pltpu.VMEM((2, 2, 8, count, d), BF16),
            cross_in=pltpu.VMEM((2, 8, 2, count, d), BF16),
            cross_sems=pltpu.SemaphoreType.DMA((2, CHUNKS, 8)),
        )

    def back_scratch(count, d):
        return dict(
            cross_out=pltpu.VMEM((2, 8, 2, count, d), BF16),
            cross_in=pltpu.VMEM((2, 2, 8, count, d), BF16),
            cross_sems=pltpu.SemaphoreType.DMA((2, CHUNKS, 8)),
        )

    def copy(self, src, dst, i, k):
        return pltpu.make_async_remote_copy(
            src_ref=src,
            dst_ref=dst,
            send_sem=self.r.cross_sems.at[0, i, k],
            recv_sem=self.r.cross_sems.at[1, i, k],
            device_id={WIDE: lax.rem(self.w + k, 8)},
        )

    def to_patches(self, i, k):
        m, f, other = i // 2, i % 2, lax.rem(self.w + k, 8)
        return self.copy(
            self.r.cross_out.at[m, f, other], self.r.cross_in.at[m, self.w, f], i, k
        )

    def send(self, i, value):
        m, f = i // 2, i % 2
        out = self.r.cross_out
        out[m, f] = value.reshape(out.shape[2:]).astype(BF16)
        for k in range(1, 8):
            self.to_patches(i, k).start()
        self.r.cross_in[m, self.w, f] = out[m, f, self.w]

    def received(self, c):
        m, h = c // 2, c % 2
        if h == 0:
            for i in (2 * m, 2 * m + 1):
                for k in range(1, 8):
                    self.to_patches(i, k).wait_recv()
        return self.r.cross_in[m, 4 * h : 4 * h + 4]

    def to_frames(self, m, k):
        other = lax.rem(self.w + k, 8)
        return self.copy(
            self.r.cross_out.at[m, other], self.r.cross_in.at[m, :, self.w], m, k
        )

    def send_back(self, c, value):
        m, h = c // 2, c % 2
        out = self.r.cross_out
        out[m, 4 * h : 4 * h + 4] = value.reshape((4,) + out.shape[2:]).astype(BF16)
        if h:
            for k in range(1, 8):
                self.to_frames(m, k).start()
            self.r.cross_in[m, :, self.w] = out[m, self.w]

    def received_back(self, i):
        m, f = i // 2, i % 2
        if f == 0:
            for k in range(1, 8):
                self.to_frames(m, k).wait_recv()
        return self.r.cross_in[m, f]

    def drain(self):
        for i in range(CHUNKS):
            for k in range(1, 8):
                self.to_patches(i, k).wait_send()

    def drain_back(self):
        for m in range(2):
            for k in range(1, 8):
                self.to_frames(m, k).wait_send()


def norm_rows(v):
    centred = v - jnp.mean(v, axis=-1, keepdims=True)
    r = lax.rsqrt(jnp.mean(centred * centred, axis=-1, keepdims=True) + NORM_EPS)
    return centred * r, r


def norm_back(grad, n, r, scale):
    dn = grad * (1.0 + scale)
    return r * (
        dn
        - jnp.mean(dn, axis=-1, keepdims=True)
        - n * jnp.mean(dn * n, axis=-1, keepdims=True)
    )


def column_sum(v):
    return jnp.sum(v, axis=0, keepdims=True)


def sds(shape, dtype=BF16):
    return jax.ShapeDtypeStruct(shape, dtype)


def softmax_of(s, mask):
    s = s * HEAD_DIM ** (-0.5)
    if mask is not None:
        s = s + mask
    p = jnp.exp(s - jnp.max(s, axis=-1, keepdims=True))
    return p * (1.0 / jnp.sum(p, axis=-1, keepdims=True))


def head_parts(v, heads, offset, size):
    return [
        v[t : t + size, offset + h * HEAD_DIM : offset + (h + 1) * HEAD_DIM]
        for t in range(0, v.shape[0], size)
        for h in range(heads)
    ]


def join_heads(pieces, heads):
    rows = [
        jnp.concatenate(pieces[t : t + heads], axis=1) for t in range(0, len(pieces), heads)
    ]
    return rows[0] if len(rows) == 1 else jnp.concatenate(rows, axis=0)


def attend(qkv, mask, heads):
    size = qkv.shape[0] if mask is None else mask.shape[0]
    width = heads * HEAD_DIM
    q, k, v = (head_parts(qkv, heads, j * width, size) for j in range(3))
    scores = [kdot(a, b, NT) for a, b in zip(q, k)]
    probs = [softmax_of(s, mask).astype(BF16) for s in scores]
    return join_heads([kdot(p, b, NN).astype(BF16) for p, b in zip(probs, v)], heads)


def attend_back(qkv, grad, mask, heads):
    size = qkv.shape[0] if mask is None else mask.shape[0]
    width = heads * HEAD_DIM
    q, k, v = (head_parts(qkv, heads, j * width, size) for j in range(3))
    g = head_parts(grad, heads, 0, size)
    group = GROUP or len(q)
    dq, dk, dv = [], [], []
    for low in range(0, len(q), group):
        part = slice(low, low + group)
        scores = [kdot(a, b, NT) for a, b in zip(q[part], k[part])]
        dps = [kdot(a, b, NT) for a, b in zip(g[part], v[part])]
        probs = [softmax_of(s, mask) for s in scores]
        dv += [kdot(p.astype(BF16), a, TN).astype(BF16) for p, a in zip(probs, g[part])]
        ds = [
            (p * (dp - jnp.sum(p * dp, axis=-1, keepdims=True)) * HEAD_DIM ** (-0.5)).astype(BF16)
            for p, dp in zip(probs, dps)
        ]
        dq += [kdot(a, b, NN).astype(BF16) for a, b in zip(ds, k[part])]
        dk += [kdot(a, b, TN).astype(BF16) for a, b in zip(ds, q[part])]
    return jnp.concatenate([join_heads(m, heads) for m in (dq, dk, dv)], axis=1)


def gelu_tanh(v):
    return jnp.tanh(GELU_C * (v + GELU_A * v * v * v))


def tile_at(ref, i, temporal):
    if temporal:
        return ref.at[lax.div(i, 2), pl.ds(lax.rem(i, 2) * 2, 2)]
    return ref.at[i // 2, :, i % 2]


def tile_order(net, i, temporal):
    if not temporal:
        return i
    across = lax.div(net.n, 2)
    return i // 2 * 2 + (across if i % 2 else 1 - across)


def send_tile(net, i, temporal):
    if not temporal:
        net.sum_start(i)
        return
    for j in (i // 2 * 2, i // 2 * 2 + 1):
        if i % 2:
            net.sum_near(j)
        else:
            net.sum_far(j)


def cross_stages(net, temporal):
    if not temporal:
        return [], [(1, net.sum_cross)]

    def both(i):
        if i % 2:
            net.sum_cross(i - 1)
            net.sum_cross(i)

    return [(0, both)], []


def flat(v):
    return v.reshape(-1, v.shape[-1])


def row_of(ref, b):
    return ref[...].astype(F32)[b : b + 1]


def fill_bias(out, qkv_b, hc):
    out[...] = jnp.zeros_like(out)
    rows = qkv_b.astype(F32)
    out[:, :hc] = rows[0:1]
    out[:, 2 * hc :] = rows[1:2]


def fill_mask(out, r):
    for m in range(2):
        out[m] = jnp.where(r.key_rows[m] == r.key_columns[m], 0.0, MASKED)


class Modulation:
    def __init__(self, partial, bias):
        self.partial, self.bias = partial, bias

    def ins(self):
        return dict(partial=self.partial, ada_b=self.bias)

    def scratch(self):
        _, rows, width = self.partial.shape
        return dict(
            terms=pltpu.VMEM((8, rows, width), F32),
            mine=pltpu.VMEM((rows, width), F32),
            every=pltpu.VMEM((8, rows, width), F32),
            parts=pltpu.VMEM((4, 8, rows, width), F32),
            term_sem=pltpu.SemaphoreType.DMA((2, 8)),
            back_sem=pltpu.SemaphoreType.DMA((2, 8)),
            part_sem=pltpu.SemaphoreType.DMA((2, 4)),
        )

    def bind(self, r):
        self.r, self.w, self.n = r, lax.axis_index(WIDE), lax.axis_index(NARROW)

    def wide_copy(self, src, dst, sems, k):
        return pltpu.make_async_remote_copy(
            src_ref=src,
            dst_ref=dst,
            send_sem=sems.at[0, k],
            recv_sem=sems.at[1, k],
            device_id={WIDE: lax.rem(self.w + k, 8)},
        )

    def term(self, k):
        r = self.r
        return self.wide_copy(
            r.partial.at[lax.rem(self.w + k, 8)], r.terms.at[k], r.term_sem, k
        )

    def back(self, k):
        return self.wide_copy(self.r.mine, self.r.every.at[self.w], self.r.back_sem, k)

    def part(self, k):
        r = self.r
        return pltpu.make_async_remote_copy(
            src_ref=r.every,
            dst_ref=r.parts.at[k],
            send_sem=r.part_sem.at[0, k],
            recv_sem=r.part_sem.at[1, k],
            device_id={NARROW: lax.rem(self.n + k, 4)},
        )

    def start(self):
        for k in range(1, 8):
            self.term(k).start()

    def sum(self):
        r, w = self.r, self.w
        total = r.partial[w] + r.ada_b[lax.div(w, 4), lax.rem(w, 2)]
        for k in range(1, 8):
            self.term(k).wait_recv()
            total = total + r.terms[k]
        r.mine[...] = total
        for k in range(1, 8):
            self.back(k).start()
        r.every[w] = total

    def spread(self):
        for k in range(1, 8):
            self.back(k).wait_recv()
        for k in range(1, 4):
            self.part(k).start()
        self.r.parts[0] = self.r.every[...]

    def store(self, out):
        for k in range(1, 4):
            self.part(k).wait_recv()
        for piece in range(8):
            low = piece % 2 * 3
            out[piece // 4, piece // 2 % 2, low : low + 3] = jnp.concatenate(
                [self.r.parts[lax.rem(self.n - owner + 4, 4), piece] for owner in range(4)], axis=1
            )

    def drain(self):
        for k in range(1, 8):
            self.term(k).wait_send()
            self.back(k).wait_send()
        for k in range(1, 4):
            self.part(k).wait_send()


def attention_up(
    x_or_h, x_own, mod, pack, biases, b, keys, cid, hosts=(), plan=(), first=None, modulation=None
):
    temporal = keys is not None
    starting = first is not None
    d = x_or_h.shape[-1]
    hc = biases[0].shape[-1]
    c = 3 * hc
    heads = hc // HEAD_DIM
    tokens = x_or_h.shape[1]
    rows = tokens // 4
    own = (4, rows, d)
    ins = dict(src=x_or_h, qkv_b=biases[0], proj_b=biases[1])
    if temporal:
        ins.update(key_rows=keys[0], key_columns=keys[1], x_own=x_own)
    if starting:
        ins.update(modulation.ins())
    else:
        ins.update(mod=mod, pack=pack)
    outs = dict(
        qkv=sds((4, tokens, c)),
        att=sds((4, tokens, hc)),
        branch=sds(own),
        mixed=sds(own, F32),
        full=sds((2, 4, 2, rows, d)),
    )
    if not temporal:
        outs.update(h1=sds((4, tokens, d)), x_own=sds(own))
    if starting:
        outs.update(mod=sds((2, 2, 6, d), F32))
    stores = ("qkv", "att") + (() if temporal else ("h1",)) + ("mixed",)

    def body(r):
        net = Narrow(r)
        fill_bias(r.qb, r.qkv_b[b], hc)
        if temporal:
            fill_mask(r.mask, r)

        def prepare(i):
            r.loads.need("src", i)
            v, _ = norm_rows(r.src[i].astype(F32))
            r.h1[i] = (v * (1.0 + r.mod[b, i // 2, 1:2]) + r.mod[b, i // 2, 0:1]).astype(BF16)
            r.x_own[i] = r.src[i, pl.ds(pl.multiple_of(net.n * rows, rows), rows)]

        if starting:
            net.barrier(everyone=True)
            modulation.bind(r)
            modulation.start()
            for host in (first,) + tuple(hosts):
                host.start()
            steps = first.phases()
            modulation.sum()
            steps[0]()
            modulation.spread()
            steps[1]()
            modulation.store(r.mod)
            for i in range(2):
                prepare(i)
            steps[2]()
            for i in range(2, 4):
                prepare(i)
            first.drain()
            weights = first.own_refs.all
        else:
            net.barrier(hosts)
            weights = r.pack
        r.loads.need("pack")
        r.proj_t[...] = weights[:, c:]

        def tile(i):
            t = tile_order(net, i, temporal)
            if temporal:
                r.loads.need("src", i // 2 * 2, i // 2 * 2 + 1)
                h = r.src[t]
            else:
                if not starting:
                    prepare(i)
                h = r.h1[i]
            qkv = (kdot(h, weights[:, :c], NN) + r.qb[...]).astype(BF16)
            r.qkv[t] = qkv
            att = attend(qkv, r.mask[i // 2] if temporal else None, heads)
            r.att[t] = att
            part = kdot(att, r.proj_t[...], NT).astype(BF16)
            target = tile_at(r.part, t, temporal)
            target[...] = part.reshape(target.shape)
            send_tile(net, i, temporal)
            for key in stores[:-1]:
                if not temporal:
                    r.stores.put(key, i)
                elif i % 2:
                    r.stores.put(key, i - 1, i)

        def middle(i):
            m = i // 2
            branch = net.sum_end(i)
            r.branch[i] = branch.astype(BF16)
            mixed = r.x_own[i].astype(F32) + r.mod[b, m, 2:3] * (branch + row_of(r.proj_b, b))
            r.mixed[i] = mixed
            r.stores.put("mixed", i)
            v, _ = norm_rows(mixed)
            net.gather_start(i, (v * (1.0 + r.mod[b, m, 4:5]) + r.mod[b, m, 3:4]).astype(BF16))

        before, after = cross_stages(net, temporal)
        pipeline(
            4,
            before + [(0, tile)] + after + [(2, middle), (3, net.gather_forward)],
            hosts,
            plan,
        )
        net.sum_drain()
        net.gather_drain()
        if starting:
            modulation.drain()

    scratch = dict(Narrow.sum_scratch(rows, d), **Narrow.gather_scratch(rows, d))
    scratch.update(proj_t=pltpu.VMEM((d, hc), BF16), qb=pltpu.VMEM((1, c), F32))
    if temporal:
        scratch.update(mask=pltpu.VMEM((2, tokens // 2, tokens // 2), F32))
    if starting:
        scratch.update(modulation.scratch())
    carried = ((first,) if starting else ()) + tuple(hosts)
    loads = ("src",) if starting else ("pack", "src")
    return call("attention_up", body, ins, outs, scratch, cid, FULL, carried, loads, stores)


def up_pieces(pieces):
    return {f"up{k}": piece for k, piece in enumerate(pieces)}


def up_refs(r):
    low = 0
    for key in ("up0", "up1"):
        if hasattr(r, key):
            ref = getattr(r, key)
            yield low, ref
            low += ref.shape[1]


def need_up(r):
    for key in ("up0", "up1", "down_t"):
        r.loads.need(key)


def times_up(r, h):
    need_up(r)
    parts = [kdot(h, ref[...], NN) for _, ref in up_refs(r)]
    return parts[0] if len(parts) == 1 else jnp.concatenate(parts, axis=1)


def feed_forward(
    h2, mixed, mod, weights, biases, dy, b, cid, hosts=(), plan=(), cross=False, cross_dy=False
):
    d, c = weights[1].shape
    _, rows, _ = mixed.shape
    ins = dict(h2=h2, mixed=mixed, mod=mod, down_t=weights[1], **up_pieces(weights[0]))
    ins.update(up_b=biases[0], down_b=biases[1])
    outs = dict(before=sds((4, 4 * rows, c)), feed=sds(mixed.shape), y=sds(mixed.shape))
    scratch = Narrow.sum_scratch(rows, d)
    if cross:
        outs.update(full=sds((2, 4, 2, rows, d)))
        scratch.update(Narrow.gather_scratch(rows, d), **Cross.scratch(rows // 8, d))
    if dy is not None:
        ins.update(dy=dy)
        outs.update(
            full=sds((2, 4, 2, rows, d)), dgate=sds((2, d), F32), dbias=sds((1, d), F32)
        )
        scratch.update(Narrow.gather_scratch(rows, d))
        if cross_dy:
            outs.update(dy_here=sds(mixed.shape))
            scratch.update(Cross.scratch(rows // 8, d))
            scratch.update(
                cot=pltpu.VMEM(mixed.shape, BF16), cot_sem=pltpu.SemaphoreType.DMA((CHUNKS,))
            )

    def body(r):
        net = Narrow(r)
        net.barrier(hosts, cross or cross_dy)
        way = Cross(r)

        def own_cot(i):
            here = pl.ds(pl.multiple_of(net.n * rows, rows), rows)
            return pltpu.make_async_copy(r.dy.at[i, here], r.cot.at[i], r.cot_sem.at[i])

        def leave(i):
            own_cot(i).wait()
            way.send(i, r.cot[i].astype(F32))

        if cross_dy:
            for i in range(CHUNKS):
                own_cot(i).start()

        def normed(i):
            x = way.received(i)
            v = x.astype(F32).reshape(rows, d)
            r.y[i] = v.astype(BF16)
            v, _ = norm_rows(v)
            m = i // 2
            h = v * (1.0 + r.mod[b + 1, m, 1:2]) + r.mod[b + 1, m, 0:1]
            net.gather_start(i, h.astype(BF16))

        def gated(i):
            m = i // 2
            if cross_dy:
                v = way.received(i).astype(F32).reshape(rows, d)
                r.dy_here[i] = v.astype(BF16)
            else:
                v = r.dy[i].astype(F32)
            dgate = column_sum(v * (r.feed[i].astype(F32) + row_of(r.down_b, b)))
            add_rows(r.dgate, pl.ds(m, 1), dgate, i % 2 == 0)
            v = r.mod[b, m, 5:6] * v
            add_rows(r.dbias, pl.ds(0, 1), column_sum(v), i == 0)
            net.gather_start(i, v.astype(BF16))

        def tile(i):
            r.loads.need("h2", i // 2)
            v = times_up(r, flat(r.h2[i // 2, :, i % 2])) + row_of(r.up_b, b)
            r.before[i] = v.astype(BF16)
            r.stores.put("before", i)
            active = (0.5 * v * (1.0 + gelu_tanh(v))).astype(BF16)
            part = kdot(active, r.down_t[...], NT).astype(BF16)
            r.part[i // 2, :, i % 2] = part.reshape(4, rows, d)
            net.sum_start(i)

        def middle(i):
            m = i // 2
            feed = net.sum_end(i)
            r.feed[i] = feed.astype(BF16)
            full_feed = feed + row_of(r.down_b, b)
            y = r.mixed[i] + r.mod[b, m, 5:6] * full_feed
            if cross:
                way.send(i, y)
            else:
                r.y[i] = y.astype(BF16)

        stages = [(0, tile), (1, net.sum_cross), (2, middle)]
        if dy is not None:
            stages = stages + [(2, gated), (4, net.gather_forward)]
            if cross_dy:
                stages = [(0, leave)] + stages
        if cross:
            stages = stages + [(5, normed), (7, net.gather_forward)]
        pipeline(4, stages, hosts, plan)
        net.sum_drain()
        if dy is not None or cross:
            net.gather_drain()
        if cross or cross_dy:
            way.drain()

    hbm = (FULL if dy is not None or cross else ()) + (("dy",) if cross_dy else ())
    loads = tuple(up_pieces(weights[0])) + ("h2", "down_t")
    return call("feed_forward", body, ins, outs, scratch, cid, hbm, hosts, loads, ("before",))


def gather_own(
    name, value_of, ins, more_outs, rows, d, cid, hosts=(), plan=(), frames=False
):
    def body(r):
        net = Narrow(r, frames)
        net.barrier(hosts)
        pipeline(
            4,
            [(0, lambda i: net.gather_start(i, value_of(r, i))), (2, net.gather_forward)],
            hosts,
            plan,
        )
        net.gather_drain()

    shape = (2, 2, 4, rows, d) if frames else (2, 4, 2, rows, d)
    outs = dict(full=sds(shape), **more_outs)
    return call(name, body, ins, outs, Narrow.gather_scratch(rows, d), cid, FULL, hosts)


def gather_normed(x_own, mod, b, cid, hosts=(), plan=()):
    def value(r, i):
        v, _ = norm_rows(r.x[i].astype(F32))
        return (v * (1.0 + r.mod[b, i // 2, 1:2]) + r.mod[b, i // 2, 0:1]).astype(BF16)

    _, rows, d = x_own.shape
    ins = dict(x=x_own, mod=mod)
    return gather_own("gather_normed", value, ins, {}, rows, d, cid, hosts, plan)


def add_rows(ref, index, v, first):
    if first:
        ref[index] = v
    else:
        ref[index] += v


def gather_gated(dy, feed, mod, down_b, b, cid, hosts=(), plan=()):
    def value(r, i):
        m = i // 2
        v = r.dy[i].astype(F32)
        gated = r.mod[b, m, 5:6] * v
        dgate = column_sum(v * (r.feed[i].astype(F32) + row_of(r.down_b, b)))
        add_rows(r.dgate, pl.ds(m, 1), dgate, i % 2 == 0)
        add_rows(r.dbias, pl.ds(0, 1), column_sum(gated), i == 0)
        return gated.astype(BF16)

    _, rows, d = dy.shape
    return gather_own(
        "gather_gated",
        value,
        dict(dy=dy, feed=feed, mod=mod, down_b=down_b),
        dict(dgate=sds((2, d), F32), dbias=sds((1, d), F32)),
        rows,
        d,
        cid,
        hosts,
        plan,
    )


def gather_plain(own, cid):
    _, rows, d = own.shape
    out = gather_own(
        "gather_plain", lambda r, i: r.x[i], dict(x=own), {}, rows, d, cid, frames=True
    )
    return out.full


def feed_back(
    dfeed, before, h2, mixed, dy, branch, mod, weights, proj_b, b, cid, hosts=(), plan=(), leaving=None,
    extra=None
):
    d, c = weights[1].shape
    _, rows, _ = mixed.shape
    tokens = 4 * rows
    ins = dict(dfeed=dfeed, before=before, h2=h2, mixed=mixed, dy=dy, branch=branch, mod=mod)
    ins.update(down_t=weights[1], proj_b=proj_b, **up_pieces(weights[0]))
    if leaving is not None:
        ins.update(leaving=leaving)
    outs = dict(
        full=sds((2, 4, 2, rows, d)),
        dmixed=sds(mixed.shape, F32),
        dup=sds((d, c)),
        dup_b=sds((1, c), F32),
        dshift=sds((2, d), F32),
        dscale=sds((2, d), F32),
        dgate=sds((2, d), F32),
        dproj_b=sds((1, d), F32),
    )
    strip = c // 3
    outs.update(ddown_b=sds((d, strip)))
    if not any(host.tag.startswith("da") for host in hosts):
        outs.update(ddown_a=sds((d, 2 * strip)))
    if leaving is not None:
        outs.update(left=sds(leaving.shape))
    if extra is not None:
        ins.update(extra=extra)
        outs.update(full2=sds((2, 2, 4, rows, d)))

    def body(r):
        net = Narrow(r)
        if extra is not None:
            second = second_gather(r)
        way = Cross(r)
        net.barrier(hosts, leaving is not None)

        def leave(i):
            way.send_back(i, r.leaving[i].astype(F32))

        def arrive(i):
            r.left[i] = way.received_back(i).astype(F32).reshape(rows, d).astype(BF16)

        def tile(i):
            need_up(r)
            r.loads.need("dfeed", i // 2)
            r.loads.need("before", i)
            da = kdot(flat(r.dfeed[i // 2, :, i % 2]), r.down_t[...], NN)
            v = r.before[i].astype(F32)
            t = gelu_tanh(v)
            r.active[i // 2, :, i % 2] = (0.5 * v * (1.0 + t)).astype(BF16).reshape(4, rows, c)
            slope = 0.5 * (1.0 + t) + 0.5 * v * (1.0 - t * t) * (
                GELU_C * (1.0 + 3.0 * GELU_A * v * v)
            )
            db = (da * slope).astype(BF16)
            r.dbefore[i // 2, :, i % 2] = db.reshape(4, rows, c)
            add_rows(r.dup_b, pl.ds(0, 1), column_sum(db.astype(F32)), i == 0)
            part = sum(
                kdot(db[:, low : low + ref.shape[1]], ref[...], NT) for low, ref in up_refs(r)
            )
            r.part[i // 2, :, i % 2] = part.astype(BF16).reshape(4, rows, d)
            net.sum_start(i)

        def middle(i):
            m = i // 2
            dh = net.sum_end(i)
            v, rs = norm_rows(r.mixed[i])
            add_rows(r.dshift, pl.ds(m, 1), column_sum(dh), i % 2 == 0)
            add_rows(r.dscale, pl.ds(m, 1), column_sum(dh * v), i % 2 == 0)
            dmixed = r.dy[i].astype(F32) + norm_back(dh, v, rs, r.mod[b, m, 4:5])
            r.dmixed[i] = dmixed
            r.stores.put("dmixed", i)
            gated = r.mod[b, m, 2:3] * dmixed
            dgate = column_sum(dmixed * (r.branch[i].astype(F32) + row_of(r.proj_b, b)))
            add_rows(r.dgate, pl.ds(m, 1), dgate, i % 2 == 0)
            add_rows(r.dproj_b, pl.ds(0, 1), column_sum(gated), i == 0)
            net.gather_start(i, gated.astype(BF16))

        def strip_of(out, at, left, right, j):
            right = right[:, :, :, :, pl.ds(j * strip, strip)].reshape(4 * tokens, strip)
            out[:, pl.ds(at * strip, strip)] = kdot(flat(left[...]), right, TN).astype(BF16)

        def weight_strip(j):
            r.loads.need("h2")
            if j == 0:
                strip_of(r.ddown_a, 0, r.dfeed, r.active, 0)
                strip_of(r.ddown_a, 1, r.dfeed, r.active, 1)
            elif j == 1:
                strip_of(r.ddown_b, 0, r.dfeed, r.active, 2)
                strip_of(r.dup, 0, r.h2, r.dbefore, 0)
            elif j < 4:
                strip_of(r.dup, j - 1, r.h2, r.dbefore, j - 1)
            if j == 1:
                r.stores.put("ddown_b", 0)
            if j == 3:
                r.stores.put("dup", 0)

        stages = [(0, tile), (1, net.sum_cross), (4, weight_strip), (2, middle), (4, net.gather_forward)]
        if leaving is not None:
            stages = [(0, leave)] + stages + [(4, arrive)]
        if extra is not None:
            stages = [(0, lambda i: second.gather_start(i, r.extra[i]))] + stages
            stages += [(2, second.gather_forward)]
        pipeline(4, stages, hosts, plan)
        net.sum_drain()
        net.gather_drain()
        if leaving is not None:
            way.drain_back()
        if extra is not None:
            second.gather_drain()

    scratch = dict(Narrow.sum_scratch(rows, d), **Narrow.gather_scratch(rows, d))
    if leaving is not None:
        scratch.update(Cross.back_scratch(rows // 8, d))
    if extra is not None:
        scratch.update(second_scratch(rows, d))
    scratch.update(
        dbefore=pltpu.VMEM((2, 4, 2, rows, c), BF16), active=pltpu.VMEM((2, 4, 2, rows, c), BF16)
    )
    if "ddown_a" not in outs:
        scratch.update(ddown_a=pltpu.VMEM((d, 2 * strip), BF16))
    loads = ("down_t", "dfeed", "before") + tuple(up_pieces(weights[0])) + ("h2",)
    stores = ("dup", "ddown_b", "dmixed")
    return call(
        "feed_back", body, ins, outs, scratch, cid, FULL + ("full2",), hosts, loads, stores
    )


class Totals:
    in_turn = False

    def __init__(self, vectors, d):
        self.vectors, self.piece = vectors, (4, d)

    def phases(self):
        return [self.start, self.sum, self.spread]

    def ins(self):
        return {
            f"vector{k}": v for k, (v, _) in enumerate(self.vectors) if not isinstance(v, str)
        }

    def scratch(self):
        return dict(
            sums=pltpu.VMEM((8,) + self.piece, F32),
            terms=pltpu.VMEM((8,) + self.piece, F32),
            parts=pltpu.VMEM((4,) + self.piece, F32),
            mine=pltpu.VMEM(self.piece, F32),
            term_sem=pltpu.SemaphoreType.DMA((2, 8)),
            part_sem=pltpu.SemaphoreType.DMA((2, 4)),
            back_sem=pltpu.SemaphoreType.DMA((2, 8)),
        )

    def bind(self, r):
        self.r, self.w, self.n = r, lax.axis_index(WIDE), lax.axis_index(NARROW)

    def wide_copy(self, src, dst, sems, k):
        return pltpu.make_async_remote_copy(
            src_ref=src,
            dst_ref=dst,
            send_sem=sems.at[0, k],
            recv_sem=sems.at[1, k],
            device_id={WIDE: lax.rem(self.w + k, 8)},
        )

    def term(self, k):
        r = self.r
        return self.wide_copy(r.sums.at[lax.rem(self.w + k, 8)], r.terms.at[k], r.term_sem, k)

    def back(self, k):
        return self.wide_copy(self.r.mine, self.r.total.at[self.w], self.r.back_sem, k)

    def part(self, k):
        r = self.r
        return pltpu.make_async_remote_copy(
            src_ref=r.parts.at[0],
            dst_ref=r.parts.at[k],
            send_sem=r.part_sem.at[0, k],
            recv_sem=r.part_sem.at[1, k],
            device_id={NARROW: lax.rem(self.n + k, 4)},
        )

    def start(self):
        r = self.r
        r.sums[7] = jnp.zeros(self.piece, F32)
        for k, (vector, places) in enumerate(self.vectors):
            value = getattr(r, vector if isinstance(vector, str) else f"vector{k}")[...]
            for j, place in enumerate(places):
                width = value.shape[1]
                r.sums[place // 4, place % 4 : place % 4 + 1, :width] = value[j : j + 1]
        for k in range(1, 8):
            self.term(k).start()

    def sum(self):
        r = self.r
        total = r.sums[self.w]
        for k in range(1, 8):
            self.term(k).wait_recv()
            total = total + r.terms[k]
        r.parts[0] = total
        for k in range(1, 4):
            self.part(k).start()

    def spread(self):
        r = self.r
        total = r.parts[0]
        everywhere = total
        for k in range(1, 4):
            self.part(k).wait_recv()
            everywhere = everywhere + r.parts[k]
        total = jnp.where(self.w == 7, total, everywhere)
        r.mine[...] = total
        for k in range(1, 8):
            self.back(k).start()
        r.total[self.w] = total

    def drain(self):
        for k in range(1, 8):
            self.term(k).wait_send()
            self.back(k).wait()
        for k in range(1, 4):
            self.part(k).wait_send()


def attention_back(
    dbranch, qkv, att, h1, x_own, dmixed, mod, pack, b, keys, cid, hosts=(), plan=(), below=None, totals=None
):
    temporal = keys is not None
    d, hc = pack.shape[0], pack.shape[1] // 4
    c = 3 * hc
    heads = hc // HEAD_DIM
    _, rows, _ = x_own.shape
    tokens = 4 * rows
    ins = dict(dbranch=dbranch, qkv=qkv, att=att, h1=h1, x_own=x_own, dmixed=dmixed, mod=mod)
    ins.update(pack=pack)
    if temporal:
        ins.update(key_rows=keys[0], key_columns=keys[1])
    outs = dict(
        **({} if below or totals else dict(dx=sds(x_own.shape))),
        **({} if totals else dict(dpack=sds(pack.shape))),
        dqkv_b=sds((1, c), F32),
        dshift=sds((2, d), F32),
        dscale=sds((2, d), F32),
    )

    if below:
        ins.update(feed=below[0], down_b=below[1])
        outs.update(dgate=sds((2, d), F32), dbias=sds((1, d), F32), dy=sds(x_own.shape))
    if below:
        outs.update(full=sds((2, 4, 2, rows, d)))
    if totals:
        ins.update(totals.ins())
        outs.update(full2=sds((2, 2, 4, rows, d)), total=sds((8, 4, d), F32))

    def body(r):
        net = Narrow(r)
        net.barrier(hosts, below is not None, totals is not None)
        if totals:
            totals.bind(r)
            second = second_gather(r)
        way = Cross(r)
        r.loads.need("pack")
        r.proj_t[...] = r.pack[:, c:]
        if temporal:
            fill_mask(r.mask, r)

        def gated(i):
            m = i // 2
            v = way.received_back(i).astype(F32).reshape(rows, d)
            r.dy[i] = v.astype(BF16)
            out = r.mod[b - 1, m, 5:6] * v
            dgate = column_sum(v * (r.feed[i].astype(F32) + row_of(r.down_b, b - 1)))
            add_rows(r.dgate, pl.ds(m, 1), dgate, i % 2 == 0)
            add_rows(r.dbias, pl.ds(0, 1), column_sum(out), i == 0)
            net.gather_start(i, out.astype(BF16))

        def weight_grads(i):
            for key in ("att", "h1"):
                r.loads.need(key)
            source = r.dbranch if temporal else r.dbr
            if i == 0:
                r.dpack[:, c:] = kdot(flat(source[...]), flat(r.att[...]), TN).astype(BF16)
            elif i == 1:
                r.dpack[:, :c] = kdot(flat(r.h1[...]), flat(r.dqkv[...]), TN).astype(BF16)
                r.stores.put("dpack", 0)

        def tile(i):
            t = tile_order(net, i, temporal)
            r.loads.need("dbranch", i // 2)
            r.loads.need("qkv", *((i // 2 * 2, i // 2 * 2 + 1) if temporal else (i,)))
            dbranch = flat(tile_at(r.dbranch, t, temporal)[...])
            if not temporal:
                r.dbr[i] = dbranch
            da = kdot(dbranch, r.proj_t[...], NN).astype(BF16)
            dqkv = attend_back(r.qkv[t], da, r.mask[i // 2] if temporal else None, heads)
            r.dqkv[t] = dqkv
            add_rows(r.dqkv_b, pl.ds(0, 1), column_sum(dqkv.astype(F32)), i == 0)
            part = kdot(dqkv, r.pack[:, :c], NT).astype(BF16)
            target = tile_at(r.part, t, temporal)
            target[...] = part.reshape(target.shape)
            send_tile(net, i, temporal)

        def middle(i):
            m = i // 2
            dh = net.sum_end(i)
            v, rs = norm_rows(r.x_own[i].astype(F32))
            add_rows(r.dshift, pl.ds(m, 1), column_sum(dh), i % 2 == 0)
            add_rows(r.dscale, pl.ds(m, 1), column_sum(dh * v), i % 2 == 0)
            dx = r.dmixed[i] + norm_back(dh, v, rs, r.mod[b, m, 1:2])
            if below:
                way.send_back(i, dx)
            elif totals:
                second.gather_start(i, dx.astype(BF16))
            else:
                r.dx[i] = dx.astype(BF16)

        before, after = cross_stages(net, temporal)
        stages = before + [(0, tile)] + after + [(2, middle)]
        if below:
            stages += [(5, weight_grads), (5, gated), (7, net.gather_forward)]
        else:
            stages += [(3, weight_grads)]
        if totals:
            stages += [(4, second.gather_forward)]
        pipeline(4, stages, tuple(hosts) + ((totals,) if totals else ()), plan)
        if totals:
            second.gather_drain()
        net.sum_drain()
        if below:
            net.gather_drain()
            way.drain_back()

    scratch = Narrow.sum_scratch(rows, d)
    scratch.update(dqkv=pltpu.VMEM((4, tokens, c), BF16), proj_t=pltpu.VMEM((d, hc), BF16))
    if temporal:
        scratch.update(mask=pltpu.VMEM((2, tokens // 2, tokens // 2), F32))
    else:
        scratch.update(dbr=pltpu.VMEM((4, tokens, d), BF16))
    if below:
        scratch.update(Narrow.gather_scratch(rows, d), **Cross.back_scratch(rows // 8, d))
    if totals:
        scratch.update(totals.scratch(), dpack=pltpu.VMEM(pack.shape, BF16))
        scratch.update(second_scratch(rows, d))
    hbm = ("full2",) if totals else FULL if below else ()
    loads = ("pack", "dbranch", "qkv", "att", "h1")
    stores = () if totals else ("dpack",)
    return call("attention_back", body, ins, outs, scratch, cid, hbm, hosts, loads, stores)


def assemble(total, silu, grads):
    rows, d = grads["u0"].shape[0], total.shape[-1]
    hc, hidden = d // 4, grads["u0"].shape[1]
    outs = dict(
        qkv=sds((2, 3, rows, hc), F32),
        proj=sds((2, rows, hc), F32),
        up=sds((2, rows, hidden), F32),
        down=sds((2, rows, hidden), F32),
        ada=sds((2, 6, rows, hc), F32),
        qkv_b=sds((2, 2, hc), F32),
        proj_b=sds((2, d), F32),
        up_b=sds((2, hidden), F32),
        down_b=sds((2, d), F32),
        ada_b=sds((2, 6, hc), F32),
    )

    def body(r):
        n = lax.axis_index(NARROW)

        def line(k):
            return r.total[k // 4, k % 4 : k % 4 + 1]

        for b in range(2):
            pack = getattr(r, f"p{b}")[...]
            for j in range(3):
                r.qkv[b, j] = pack[:, j * hc : (j + 1) * hc]
            r.proj[b] = pack[:, 3 * hc :]
            r.up[b] = getattr(r, f"u{b}")[...]
            cut = getattr(r, f"da{b}").shape[1]
            r.down[b, :, :cut] = getattr(r, f"da{b}")[...]
            r.down[b, :, cut:] = getattr(r, f"db{b}")[...]
            for k in range(6):
                mine = []
                for m in range(2):
                    every = line(b * 12 + m * 6 + k)
                    pick = every[:, :hc]
                    for j in range(1, 4):
                        pick = jnp.where(n == j, every[:, j * hc : (j + 1) * hc], pick)
                    mine.append(pick)
                r.ada[b, k] = r.silu[0] * mine[0] + r.silu[1] * mine[1]
                r.ada_b[b, k : k + 1] = mine[0] + mine[1]
            hidden_row = line(28 + 2 * b)
            r.qkv_b[b, 0:1] = hidden_row[:, :hc]
            r.qkv_b[b, 1:2] = hidden_row[:, 2 * hc : 3 * hc]
            r.up_b[b : b + 1] = line(29 + 2 * b)
            r.proj_b[b : b + 1] = line(24 + b)
            r.down_b[b : b + 1] = line(26 + b)

    ins = dict(total=total, silu=silu, **grads)
    return call("assemble", body, ins, outs, {})


def wide_scatter(grad):
    size = lax.axis_size(WIDE)
    rows = grad.shape[0] // size
    moved = lax.all_to_all(grad, WIDE, split_axis=0, concat_axis=0, tiled=True)
    return jnp.sum(moved.reshape((size, rows) + grad.shape[1:]).astype(F32), axis=0)


def exchange(rows_in, seq_group):
    mb, half, count, d = rows_in.shape
    v = rows_in.reshape(mb, half, seq_group, count // seq_group, d)
    v = group_all_to_all(jnp.moveaxis(v, 2, 0), seq_group)
    return jnp.moveaxis(v, 0, 1).reshape(mb, half, count, d)


def exchange_back(rows_in, seq_group):
    mb, half, count, d = rows_in.shape
    v = rows_in.reshape(mb, seq_group, half, count // seq_group, d)
    v = group_all_to_all(jnp.moveaxis(v, 1, 0), seq_group)
    return jnp.moveaxis(v, 0, 2).reshape(mb, half, count, d)


def group_all_to_all(v, seq_group):
    size = lax.axis_size(WIDE)
    groups = None
    if seq_group != size:
        groups = [
            list(range(first, first + seq_group)) for first in range(0, size, seq_group)
        ]
    return lax.all_to_all(
        v, WIDE, split_axis=0, concat_axis=0, tiled=True, axis_index_groups=groups
    )


def shards(
    tokens,
    conditioning,
    frame_segments,
    cotangent,
    qkv_weight,
    qkv_bias,
    proj_weight,
    proj_bias,
    up_weight,
    up_bias,
    down_weight,
    down_bias,
    ada_weight,
    ada_bias,
):
    mb, half, patches, d = tokens.shape
    parts = lax.axis_size(NARROW)
    seq_frames = frame_segments.shape[2]
    seqs = frame_segments.shape[1]
    seq_group = seq_frames // half
    n = lax.axis_index(NARROW)
    w = lax.axis_index(WIDE)
    seq_here = w // seq_group
    blocks = qkv_weight.shape[0]
    rows = patches // parts
    local = qkv_bias.shape[-1]
    shard_rows = ada_weight.shape[1]
    own_shape = (mb, half, rows, d)
    chunk_shape = (mb * half, rows, d)

    hosted = lax.axis_size(WIDE) == 8 and seqs == 1 and blocks == 2 and mb == 2
    first = [
        jnp.concatenate([qkv_weight[b].reshape(shard_rows, -1), proj_weight[b].T], axis=1)
        for b in range(blocks)
    ]
    down_rows = jnp.swapaxes(down_weight, 1, 2)
    hidden = up_weight.shape[2]
    cut = hidden // 128 * 4 // 9 * 128
    packs, grads = types.SimpleNamespace(), {}

    def gather(key, shard, b=None, low=0, cols=None, vmem=False, turn=True):
        if hosted:
            return (WideGather(key, shard, b, low, cols, vmem, turn),)
        shard = shard if b is None else shard[b]
        shard = shard[:, low : low + (cols or shard.shape[1])]
        setattr(packs, key, lax.all_gather(shard, WIDE, axis=0, tiled=True))
        return ()

    def scatter(key, grad, low=0, cols=None, depth=2):
        if hosted:
            return (WideScatter(key, grad, None, low, cols, depth),)
        grads[key] = wide_scatter(grad)
        return ()

    def take(result):
        for key, value in vars(result).items():
            if key.endswith("all"):
                setattr(packs, key[:-3], value)
            if key.endswith("sum"):
                grads[key[:-3]] = value
        return result

    def scatter_inside(key, source, cols, depth=2):
        shape = sds((shard_rows * lax.axis_size(WIDE), d))
        return (WideScatter(key, shape, source, 0, cols, depth),) if hosted else ()

    silu = jax.nn.silu(conditioning.astype(F32)).astype(BF16)
    silu_rows = lax.dynamic_slice_in_dim(silu, w * shard_rows, shard_rows, 2)
    partial = jnp.einsum(
        "msr,brck->bmsck", silu_rows, ada_weight, preferred_element_type=F32
    )
    modulation = mod = None
    first0 = gather("a0", first[0], vmem=True)
    if hosted:
        modulation = Modulation(
            partial.reshape(8, -1, local), ada_bias.astype(F32).reshape(blocks, 2, -1, local)
        )
    else:
        total = lax.psum(partial, WIDE)
        here = lax.dynamic_index_in_dim(total, seq_here, 2, keepdims=False)
        mod = lax.all_gather(
            here + ada_bias.astype(F32)[:, None], NARROW, axis=3, tiled=True
        )

    frame_ids = lax.dynamic_index_in_dim(frame_segments, seq_here, 1, keepdims=False)
    count = rows // seq_group
    keys = (frame_ids[:, :, None] * count + jnp.arange(count)).reshape(mb, -1).astype(F32)
    keys = (keys[:, None, :], keys[:, :, None])

    def own_of(full):
        return lax.dynamic_slice_in_dim(full, n * rows, rows, 2).reshape(chunk_shape)

    up0 = take(
        attention_up(
            tokens.reshape(mb * half, patches, d), None, mod, getattr(packs, "a0", None),
            (qkv_bias, proj_bias), 0, None, 0,
            gather("u0", up_weight, 0) + gather("d0", down_rows, 0), PLANS["up0"],
            first0[0] if hosted else None, modulation,
        )
    )
    mod = getattr(up0, "mod", mod)
    x0 = up0.x_own
    ff0 = take(
        feed_forward(
            up0.full, up0.mixed, mod, ((packs.u0,), packs.d0), (up_bias, down_bias),
            None, 0, 1, gather("a1", first[1], turn=False) + gather("ua1", up_weight, 1, 0, cut), PLANS["ff0"],
            cross=hosted,
        )
    )

    if hosted:
        x1, h1 = ff0.y, ff0.full
        dy1 = cotangent.reshape(mb * half, patches, d)
    else:
        x1 = exchange(ff0.y.reshape(own_shape), seq_group).reshape(chunk_shape)
        h1 = gather_normed(x1, mod, 1, 2).full
        dy1 = exchange(own_of(cotangent).reshape(own_shape), seq_group).reshape(chunk_shape)
    h1 = h1.reshape(4, patches, d)
    up1 = take(
        attention_up(
            h1, x1, mod, packs.a1, (qkv_bias, proj_bias), 1, keys, 3,
            gather("ub1", up_weight, 1, cut, hidden - cut) + gather("d1", down_rows, 1),
            PLANS["up1"],
        )
    )
    feed_weights = ((packs.ua1, packs.ub1), packs.d1)
    ff1 = feed_forward(
        up1.full, up1.mixed, mod, feed_weights, (up_bias, down_bias), dy1, 1, 4,
        cross_dy=hosted,
    )
    if hosted:
        dy1 = ff1.dy_here
    else:
        out_own = exchange_back(ff1.y.reshape(own_shape), seq_group).reshape(chunk_shape)
    fb1 = take(
        feed_back(
            ff1.full, ff1.before, up1.full, up1.mixed, dy1, up1.branch, mod,
            feed_weights, proj_bias, 1, 7, scatter_inside("da1", "ddown_a", hidden // 3 * 2), PLANS["fb1"],
            ff1.y if hosted else None,
        )
    )
    if hosted:
        out_own = fb1.left
    else:
        scatter("da1", fb1.ddown_a)
    ab1 = take(
        attention_back(
            fb1.full, up1.qkv, up1.att, h1, x1, fb1.dmixed, mod, packs.a1, 1, keys,
            8, scatter("db1", fb1.ddown_b, 0, None, 4) + scatter("u1", fb1.dup, 0, None, 1), PLANS["ab1"],
            (ff0.feed, down_bias) if hosted else None,
        )
    )
    if hosted:
        dy0, gg0 = ab1.dy, ab1
    else:
        dy0 = exchange_back(ab1.dx.reshape(own_shape), seq_group).reshape(chunk_shape)
        gg0 = gather_gated(dy0, ff0.feed, mod, down_bias, 0, 9)
    fb0 = take(
        feed_back(
            gg0.full, ff0.before, up0.full, up0.mixed, dy0, up0.branch, mod,
            ((packs.u0,), packs.d0), proj_bias, 0, 10,
            scatter("p1", ab1.dpack) + scatter_inside("da0", "ddown_a", hidden // 3 * 2), PLANS["fb0"],
            None, out_own,
        )
    )
    if not hosted:
        scatter("da0", fb0.ddown_a)
    mine = ("dshift", "dscale", "dqkv_b")
    hidden_rows = [mine[2], fb0.dup_b, ab1.dqkv_b, fb1.dup_b]
    model_rows = [fb0.dproj_b, fb1.dproj_b, gg0.dbias, ff1.dbias]
    mod_rows = [
        [shift, scale, fb.dgate, fb.dshift, fb.dscale, dgate2]
        for shift, scale, fb, dgate2 in (
            mine[:2] + (fb0, gg0.dgate),
            (ab1.dshift, ab1.dscale, fb1, ff1.dgate),
        )
    ]
    vectors = [
        (v, (b * 12 + k, b * 12 + 6 + k)) for b, group in enumerate(mod_rows) for k, v in enumerate(group)
    ]
    vectors += [(v, (24 + k,)) for k, v in enumerate(model_rows + hidden_rows)]
    ab0 = take(
        attention_back(
            fb0.full, up0.qkv, up0.att, up0.h1, x0, fb0.dmixed, mod, packs.a0, 0,
            None, 11, scatter("db0", fb0.ddown_b, 0, None, 4) + scatter("u0", fb0.dup, 0, None, 2)
            + scatter_inside("p0", "dpack", d, 4), PLANS["ab0"],
            None, Totals(vectors, d) if hosted else None,
        )
    )
    layer_out = fb0.full2.reshape(mb, half, patches, d)
    if hosted:
        input_grad = ab0.full2.astype(F32).reshape(mb, half, patches, d)
        done = assemble(
            ab0.total, silu_rows.astype(F32).reshape(mb, shard_rows, 1), grads
        )
        return (
            layer_out,
            input_grad,
            jnp.moveaxis(done.qkv, 1, 2),
            done.qkv_b,
            jnp.swapaxes(done.proj, 1, 2),
            done.proj_b,
            done.up,
            done.up_b,
            jnp.swapaxes(done.down, 1, 2),
            done.down_b,
            jnp.moveaxis(done.ada, 1, 2),
            done.ada_b,
        )
    scatter("p0", ab0.dpack)
    mod_rows[0][:2] = ab0.dshift, ab0.dscale
    hidden_rows[0] = ab0.dqkv_b
    input_grad = gather_plain(ab0.dx, 12).astype(F32).reshape(mb, half, patches, d)
    dmod = jnp.stack([jnp.stack(group, axis=1) for group in mod_rows])
    slot = (jnp.arange(seqs) == seq_here).astype(F32)
    dmod = dmod[:, :, None] * slot[None, None, :, None, None]
    model_b = jnp.concatenate(model_rows)
    dmod, model_b = lax.psum((dmod, model_b), (WIDE, NARROW))
    model_b = model_b.reshape(2, blocks, d)
    hidden_b = lax.psum(
        jnp.stack([jnp.concatenate(hidden_rows[2 * b : 2 * b + 2], axis=1)[0] for b in range(2)]),
        WIDE,
    )
    dmod = lax.dynamic_slice_in_dim(dmod, n * local, local, 4)
    silu_f = silu_rows.astype(F32)
    ada_wgrad = sum(
        silu_f[m, s][None, :, None, None] * dmod[:, m, s][:, None]
        for m in range(mb)
        for s in range(seqs)
    )
    return (
        layer_out,
        input_grad,
        jnp.stack([grads[k][:, : 3 * local] for k in ("p0", "p1")]).reshape(qkv_weight.shape),
        jnp.stack([hidden_b[:, :local], hidden_b[:, 2 * local : 3 * local]], axis=1),
        jnp.stack([grads[k][:, 3 * local :].T for k in ("p0", "p1")]),
        model_b[0],
        jnp.stack([grads[k] for k in ("u0", "u1")]),
        hidden_b[:, 3 * local :],
        jnp.stack([jnp.concatenate([grads["da" + b], grads["db" + b]], 1).T for b in "01"]),
        model_b[1],
        ada_wgrad,
        jnp.sum(dmod, axis=(1, 2)),
    )


def solution(mesh):
    return jax.shard_map(
        shards,
        mesh=mesh,
        in_specs=(
            P(None, WIDE, None, None),
            P(),
            P(),
            P(None, WIDE, None, None),
            P(None, WIDE, None, NARROW),
            P(None, None, NARROW),
            P(None, NARROW, WIDE),
            P(),
            P(None, WIDE, NARROW),
            P(None, NARROW),
            P(None, NARROW, WIDE),
            P(),
            P(None, WIDE, None, NARROW),
            P(None, None, NARROW),
        ),
        out_specs=(
            P(None, WIDE, None, None),
            P(None, WIDE, None, None),
            P(None, WIDE, None, NARROW),
            P(None, None, NARROW),
            P(None, NARROW, WIDE),
            P(),
            P(None, WIDE, NARROW),
            P(None, NARROW),
            P(None, NARROW, WIDE),
            P(),
            P(None, WIDE, None, NARROW),
            P(None, None, NARROW),
        ),
        check_vma=False,
    )
```
